128 devices in a mesh: tile: 4 (over z), lev: 32 (over y, x, core).
Axes of the slice: x: 4, y: 4, z: 4, core: 2. Of those that a mesh axis runs over, the one named last changes fastest.
Arguments:
- fields: float32 [224, 524288], P('lev', 'tile'), may hold values from -15 to 15
- chan_mean: float32 [224], replicated, may hold values from -6 to 6
- chan_scale: float32 [224], replicated, may hold values from 0.2 to 1
- w_embed_in: bfloat16 [224, 512], replicated, may hold values from -0.375 to 0.375
- b_embed: float32 [512], replicated, may hold values from -6 to 6
- w_embed_out: bfloat16 [512, 512], replicated, may hold values from -0.25 to 0.25
- halo_index: int32 [128, 2, 256], P(('tile', 'lev')), may hold values from 0 to 4095
- local_src: int32 [128, 4096], P(('tile', 'lev')), may hold values from 0 to 4607
- local_dst: int32 [128, 4096], P(('tile', 'lev')), may hold values from -1 to 319, as said below
- remote_src: int32 [128, 32, 16], P(('tile', 'lev')), may hold values from 0 to 4607
- remote_dst: int32 [128, 32, 16], P(('tile', 'lev')), may hold values from -1 to 319, as said below
- w_msg_in: bfloat16 [512, 512], replicated, may hold values from -0.25 to 0.25
- b_msg: float32 [512], replicated, may hold values from -6 to 6
- w_msg_out: bfloat16 [512, 512], replicated, may hold values from -0.25 to 0.25
- mesh_nodes: bfloat16 [40960, 512], P(('tile', 'lev')), may hold values from -6 to 6
- w_node_in: bfloat16 [1024, 512], replicated, may hold values from -0.1875 to 0.1875
- b_node: float32 [512], replicated, may hold values from -6 to 6
- w_node_out: bfloat16 [512, 512], replicated, may hold values from -0.25 to 0.25
Outputs:
- grid_latent: bfloat16 [524288, 512], P(('tile', 'lev'))
- mesh_out: bfloat16 [40960, 512], P(('tile', 'lev'))
The draws below stay inside these ranges and needn't reach their ends.
Inputs may be any that keep to these rules, and one draw needn't show every extreme that they name: `local_dst`: -1 marks a padding slot; other entries name node n of the block itself. `remote_dst`: -1 marks a padding slot; entry [b, o, s] otherwise names node n of block o of the same tile.
All inputs are finite; a program needn't handle non-finite values.
Results may differ from the reference program's by a relative error of at most 0.0075.
Values may be sent and summed in bfloat16 or wider, within the bound.
No kernel may reach another device: no remote copies, remote signals or barrier semaphores. Data moves between devices by JAX's collectives and lax.ppermute only.
A program may use at most 128 MiB of HBM per device.

```python
import math
import jax
import jax.numpy as jnp
from jax import lax

CH = 224
LAT = 512
G_DEV = 4096
HALO = 256
E_LOC = 4096
SLOT_X = 16
M_DEV = 320
GROUPS = 32
BLOCKS = 128
GRID = 524288
MESH = 40960
SRC = 4608
N_TILE = 4
N_LEV = 32


def draw_local_dst(key, part):
    first, second = jax.random.split(jax.random.fold_in(key, 7))
    node_ids = jax.random.randint(first, (BLOCKS, E_LOC), 0, M_DEV)
    keeper = jax.random.randint(second, (BLOCKS, E_LOC), 0, 4)
    return jnp.where(keeper > 0, node_ids, -1).astype(jnp.int32)


def draw_remote_dst(key, part):
    first, second = jax.random.split(jax.random.fold_in(key, 13))
    node_ids = jax.random.randint(first, (BLOCKS, GROUPS, SLOT_X), 0, M_DEV)
    keeper = jax.random.randint(second, (BLOCKS, GROUPS, SLOT_X), 0, 2)
    return jnp.where(keeper > 0, node_ids, -1).astype(jnp.int32)


def with_ends(drawn, rng, least, largest):
    extent = drawn.shape
    spot = [jax.random.randint(jax.random.fold_in(rng, axis), (), 0, extent[axis]) for axis in range(len(extent))]
    drawn = drawn.at[tuple(spot)].set(least)
    longest = extent.index(max(extent))
    spot[longest] = (spot[longest] + 1) % extent[longest]
    return drawn.at[tuple(spot)].set(largest)


def block_scale(key, dims, pieces, low, high):
    loudness = 1.0
    for axis_at, blocks in pieces:
        steps = jax.random.uniform(jax.random.fold_in(jax.random.fold_in(key, 6), axis_at), (blocks,), jnp.float32, low / len(pieces), high / len(pieces))
        loudness = loudness * jnp.repeat(jnp.exp(steps), dims[axis_at] // blocks).reshape((-1,) + (1,) * (len(dims) - 1 - axis_at))
    return loudness


def normal_values(key, dims, width, most, pieces=(), kind=jnp.bfloat16):
    entries = jax.random.normal(key, dims, jnp.float32) * width
    if len(pieces) > 0:
        entries = block_scale(key, dims, pieces, -0.22, 0.18) * entries
    return jnp.clip(entries, min=-most, max=most).astype(kind)


def setup_inputs(seed: int = 0) -> dict:
    key_of = jax.random.split(jax.random.key(seed), 19)
    fields = normal_values(key_of[0], (CH, GRID), 3.0, 15.0, ((0, 32), (1, 4)), jnp.float32)
    chan_mean = normal_values(key_of[1], (CH,), 1.0, 6.0, (), jnp.float32)
    chan_scale = jnp.clip(jnp.exp(jax.random.uniform(key_of[2], (CH,), jnp.float32, math.log(0.2), math.log(1.0))), 0.2, 1.0)
    w_embed_in = normal_values(key_of[3], (CH, LAT), CH ** -0.5, 0.375)
    b_embed = normal_values(key_of[4], (LAT,), 1.0, 6.0, (), jnp.float32)
    w_embed_out = normal_values(key_of[5], (LAT, LAT), LAT ** -0.5, 0.25)
    halo_index = with_ends(jax.random.randint(key_of[6], (BLOCKS, 2, HALO), 0, G_DEV), jax.random.fold_in(key_of[6], 1), 0, G_DEV - 1).astype(jnp.int32)
    local_src = with_ends(jax.random.randint(key_of[7], (BLOCKS, E_LOC), 0, SRC), jax.random.fold_in(key_of[7], 1), 0, SRC - 1).astype(jnp.int32)
    local_dst = draw_local_dst(jax.random.fold_in(key_of[18], 71), 0)
    remote_src = with_ends(jax.random.randint(key_of[9], (BLOCKS, N_LEV, SLOT_X), 0, SRC), jax.random.fold_in(key_of[9], 1), 0, SRC - 1).astype(jnp.int32)
    remote_dst = draw_remote_dst(jax.random.fold_in(key_of[18], 71), 0)
    w_msg_in = normal_values(key_of[11], (LAT, LAT), LAT ** -0.5, 0.25)
    b_msg = normal_values(key_of[12], (LAT,), 1.0, 6.0, (), jnp.float32)
    w_msg_out = normal_values(key_of[13], (LAT, LAT), LAT ** -0.5, 0.25)
    mesh_nodes = normal_values(key_of[14], (MESH, LAT), 1.0, 6.0, ((0, 128),))
    w_node_in = normal_values(key_of[15], (2 * LAT, LAT), (2 * LAT) ** -0.5, 0.1875)
    b_node = normal_values(key_of[16], (LAT,), 1.0, 6.0, (), jnp.float32)
    w_node_out = normal_values(key_of[17], (LAT, LAT), LAT ** -0.5, 0.25)
    return {"fields": fields, "chan_mean": chan_mean, "chan_scale": chan_scale, "w_embed_in": w_embed_in, "b_embed": b_embed, "w_embed_out": w_embed_out, "halo_index": halo_index, "local_src": local_src, "local_dst": local_dst, "remote_src": remote_src, "remote_dst": remote_dst, "w_msg_in": w_msg_in, "b_msg": b_msg, "w_msg_out": w_msg_out, "mesh_nodes": mesh_nodes, "w_node_in": w_node_in, "b_node": b_node, "w_node_out": w_node_out}


def embed(part, w_embed_in, b_embed, w_embed_out):
    pre = jnp.dot(part.T, w_embed_in, preferred_element_type=jnp.float32) + b_embed
    hidden = jax.nn.silu(pre).astype(jnp.bfloat16)
    return jnp.dot(hidden, w_embed_out, preferred_element_type=jnp.float32).astype(jnp.bfloat16)


def message(table, sources, w_msg_in, b_msg, w_msg_out):
    rows = jnp.take(table, sources, axis=0)
    pre = jnp.dot(rows, w_msg_in, preferred_element_type=jnp.float32) + b_msg
    act = jax.nn.silu(pre).astype(jnp.bfloat16)
    return jnp.dot(act, w_msg_out, preferred_element_type=jnp.float32)


def reference(fields, chan_mean, chan_scale, w_embed_in, b_embed, w_embed_out, halo_index, local_src, local_dst, remote_src, remote_dst, w_msg_in, b_msg, w_msg_out, mesh_nodes, w_node_in, b_node, w_node_out):
    tiles = N_TILE
    levels = N_LEV
    blocks = tiles * levels
    normed = ((fields - chan_mean[:, None]) * chan_scale[:, None]).astype(jnp.bfloat16)
    stacked = jnp.transpose(normed.reshape(CH, blocks, G_DEV), (1, 0, 2))
    latent = lax.map(lambda part: embed(part, w_embed_in, b_embed, w_embed_out), stacked)
    group_ids = jnp.arange(levels, dtype=jnp.int32)

    def block_step(total, number):
        tile_id = number // levels
        level_id = number % levels
        lower = ((tile_id - 1) % tiles) * levels + level_id
        upper = ((tile_id + 1) % tiles) * levels + level_id
        from_lower = jnp.take(latent[lower], halo_index[lower, 1], axis=0)
        from_upper = jnp.take(latent[upper], halo_index[upper, 0], axis=0)
        table = jnp.concatenate([latent[number], from_lower, from_upper], axis=0)
        sources = jnp.concatenate([local_src[number], remote_src[number].reshape(-1)])
        targets = jnp.concatenate([local_dst[number], remote_dst[number].reshape(-1)])
        owner_far = jnp.broadcast_to((tile_id * levels + group_ids)[:, None], (levels, SLOT_X)).reshape(-1)
        owners = jnp.concatenate([jnp.full((E_LOC,), number, jnp.int32), owner_far.astype(jnp.int32)])
        msgs = message(table, sources, w_msg_in, b_msg, w_msg_out)
        valid = targets >= 0
        msgs = jnp.where(valid[:, None], msgs, jnp.zeros_like(msgs))
        node_ids = jnp.where(valid, owners * M_DEV + targets, 0).astype(jnp.int32)
        return total.at[node_ids].add(msgs), None

    start = jnp.zeros((blocks * M_DEV, LAT), jnp.float32)
    summed, _ = lax.scan(block_step, start, jnp.arange(blocks, dtype=jnp.int32))
    summed_b = summed.astype(jnp.bfloat16)
    pre = jnp.dot(mesh_nodes, w_node_in[:LAT], preferred_element_type=jnp.float32)
    pre = pre + jnp.dot(summed_b, w_node_in[LAT:], preferred_element_type=jnp.float32) + b_node
    node_act = jax.nn.silu(pre).astype(jnp.bfloat16)
    mesh_out = (mesh_nodes.astype(jnp.float32) + jnp.dot(node_act, w_node_out, preferred_element_type=jnp.float32)).astype(jnp.bfloat16)
    grid_latent = latent.reshape(blocks * G_DEV, LAT)
    return grid_latent, mesh_out
```

```python
import functools

import jax
import jax.numpy as jnp
from jax import lax
from jax.experimental import pallas as pl
from jax.experimental.pallas import tpu as pltpu
from jax.sharding import PartitionSpec as P

BF = jnp.bfloat16
F32 = jnp.float32
NT = (((1,), (1,)), ((), ()))
TN = (((0,), (0,)), ((), ()))
LIMIT = 56 * 1024 * 1024


def params(**kw):
    return pltpu.CompilerParams(vmem_limit_bytes=LIMIT, **kw)


def whole(shape):
    return pl.BlockSpec(shape, lambda *_: (0,) * len(shape))


def cost(flops, nbytes):
    return pl.CostEstimate(flops=int(flops), bytes_accessed=int(nbytes), transcendentals=0)


def dot(a, b, dims=(((1,), (0,)), ((), ()))):
    return lax.dot_general(a, b, dims, preferred_element_type=F32)


def gate(h):
    return h + h * jnp.tanh(h)


def split(v):
    hi = v.astype(BF)
    return hi, (v - hi.astype(F32)).astype(BF)


def pack_kernel(me_ref, mean_ref, scale_ref, x_ref, code_ref, o_ref):
    chans = x_ref.shape[0]
    count, _, pts = o_ref.shape
    base = me_ref[0] * chans
    row = lax.broadcasted_iota(jnp.int32, (chans, 1), 0)
    mean = jnp.zeros((chans, 1), F32)
    scale = jnp.zeros((chans, 1), F32)
    for c in range(chans):
        mean = jnp.where(row == c, mean_ref[base + c], mean)
        scale = jnp.where(row == c, scale_ref[base + c], scale)
    for j in range(count):
        val = (x_ref[:, j * pts : (j + 1) * pts] - mean) * scale
        tail = jnp.concatenate(
            [code_ref[j], jnp.zeros((1, pts - code_ref.shape[2]), F32)], axis=1
        )
        o_ref[j] = jnp.concatenate([val, tail], axis=0).astype(BF)


def pack(me, mean, scale, fields, code, levels):
    chans, points = fields.shape
    pts = points // levels
    per = 4
    smem = pl.BlockSpec(memory_space=pltpu.SMEM)
    return pl.pallas_call(
        pack_kernel,
        grid=(levels // per,),
        in_specs=[
            smem,
            smem,
            smem,
            pl.BlockSpec((chans, per * pts), lambda i: (0, i)),
            pl.BlockSpec((per, 1, code.shape[2]), lambda i: (i, 0, 0)),
        ],
        out_specs=pl.BlockSpec((per, chans + 1, pts), lambda i: (i, 0, 0)),
        out_shape=jax.ShapeDtypeStruct((levels, chans + 1, pts), BF),
        compiler_params=params(),
        cost_estimate=cost(points * 16, points * 48),
        name="pack",
    )(me, mean, scale, fields, code)


def count_kernel(src_ref, dst_ref, o_ref, hot_ref):
    nodes, edges = hot_ref.shape
    tile = o_ref.shape[1]
    chunk = 1024

    @pl.when(pl.program_id(0) == 0)
    def _():
        ids = lax.broadcasted_iota(jnp.int32, (nodes, edges), 0)
        hot_ref[...] = jnp.where(ids == dst_ref[...], 1.0, 0.0).astype(BF)

    rows = lax.broadcasted_iota(jnp.int32, (tile, chunk), 0) + pl.program_id(0) * tile
    acc = jnp.zeros((nodes, tile), F32)
    for c in range(edges // chunk):
        at = slice(c * chunk, (c + 1) * chunk)
        hot = jnp.where(rows == src_ref[:, at], 1.0, 0.0).astype(BF)
        acc = acc + dot(hot_ref[:, at], hot, NT)
    o_ref[...] = acc.astype(BF)


def count_edges(src, dst, nodes, table):
    edges = src.shape[1]
    tile = 512
    return pl.pallas_call(
        count_kernel,
        grid=(table // tile,),
        in_specs=[whole((1, edges)), whole((1, edges))],
        out_specs=pl.BlockSpec((nodes, tile), lambda i: (0, i)),
        out_shape=jax.ShapeDtypeStruct((nodes, table), BF),
        scratch_shapes=[pltpu.VMEM((nodes, edges), BF)],
        compiler_params=params(),
        cost_estimate=cost(2 * nodes * edges * table, nodes * table * 2),
        name="count",
    )(src, dst)


def halo_kernel(x_ref, idx_ref, low_ref, high_ref):
    pts = x_ref.shape[1]
    half = low_ref.shape[1]
    chunk = 1024
    acc = jnp.zeros((x_ref.shape[0], 2 * half), F32)
    for c in range(pts // chunk):
        rows = lax.broadcasted_iota(jnp.int32, (chunk, 2 * half), 0) + c * chunk
        hot = jnp.where(rows == idx_ref[...], 1.0, 0.0).astype(BF)
        acc = acc + dot(x_ref[:, c * chunk : (c + 1) * chunk], hot)
    low_ref[...] = acc[:, :half].astype(BF)
    high_ref[...] = acc[:, half:].astype(BF)


def halo_select(x, idx):
    rows, pts = x.shape
    half = idx.shape[1] // 2
    out = jax.ShapeDtypeStruct((rows, half), BF)
    return pl.pallas_call(
        halo_kernel,
        out_shape=(out, out),
        compiler_params=params(),
        cost_estimate=cost(2 * rows * pts * 2 * half, rows * pts * 2),
        name="halo",
    )(x, idx)


def slots_kernel(x_ref, src_ref, o_ref):
    slots = o_ref.shape[0]
    pts = x_ref.shape[1]
    chunk = 1024
    acc = jnp.zeros(o_ref.shape, F32)
    for c in range(pts // chunk):
        ids = lax.broadcasted_iota(jnp.int32, (slots, chunk), 1) + c * chunk
        hot = jnp.where(ids == src_ref[...], 1.0, 0.0).astype(BF)
        acc = acc + dot(hot, x_ref[:, c * chunk : (c + 1) * chunk], NT)
    o_ref[...] = acc.astype(BF)


def slots_select(x, src):
    rows, pts = x.shape
    slots = src.shape[0]
    return pl.pallas_call(
        slots_kernel,
        out_shape=jax.ShapeDtypeStruct((slots, rows), BF),
        compiler_params=params(),
        cost_estimate=cost(2 * rows * pts * slots, rows * pts * 2),
        name="slots",
    )(x, src)


def slots_halo_kernel(own_ref, low_ref, up_ref, src_ref, o_ref, *, start):
    slots = o_ref.shape[0]
    half = low_ref.shape[1]
    ids = lax.broadcasted_iota(jnp.int32, (slots, half), 1) + start
    low = jnp.where(ids == src_ref[...], 1.0, 0.0).astype(BF)
    up = jnp.where(ids + half == src_ref[...], 1.0, 0.0).astype(BF)
    acc = own_ref[...].astype(F32) + dot(low, low_ref[...], NT) + dot(up, up_ref[...], NT)
    o_ref[...] = acc.astype(BF)


def slots_halo(own, low, up, src, start):
    slots, rows = own.shape
    return pl.pallas_call(
        functools.partial(slots_halo_kernel, start=start),
        out_shape=jax.ShapeDtypeStruct((slots, rows), BF),
        compiler_params=params(),
        cost_estimate=cost(4 * rows * low.shape[1] * slots, slots * rows * 4),
        name="slots_halo",
    )(own, low, up, src)


def latent_of(x, dims, w_in, b_in, w_out):
    hidden = gate(dot(x, w_in, dims) + b_in).astype(BF)
    return dot(hidden, w_out).astype(BF)


def act_of(latent, w_msg, b_msg):
    return gate(dot(latent, w_msg) + b_msg).astype(BF)


def embed_kernel(x_ref, s_ref, w_in, b_in, w_out, w_msg, b_msg, *rest):
    lat_ref, sum_ref = rest[-2:]

    @pl.when(pl.program_id(0) == 0)
    def _():
        if len(rest) == 4:
            sum_ref[...] = rest[1][...]
        else:
            sum_ref[...] = jnp.zeros_like(sum_ref)

    latent = latent_of(x_ref[...], TN, w_in[...], b_in[...], w_out[...])
    lat_ref[...] = latent
    act = act_of(latent, w_msg[...], b_msg[...])
    sum_ref[...] += dot(s_ref[...], act)


def embed(x, counts, weights, first, steps, tile, before=None):
    rows, pts = x.shape
    nodes = counts.shape[0]
    lat = weights[0].shape[1]
    specs = [
        pl.BlockSpec((rows, tile), lambda i: (0, i + first)),
        pl.BlockSpec((nodes, tile), lambda i: (0, i + first)),
    ] + [whole(w.shape) for w in weights]
    args = [x, counts, *weights]
    alias = {}
    if before is not None:
        alias = {len(args): 0}
        args += list(before)
        specs += [pl.BlockSpec(memory_space=pl.ANY), whole((nodes, lat))]
    return pl.pallas_call(
        embed_kernel,
        grid=(steps,),
        in_specs=specs,
        out_specs=[
            pl.BlockSpec((tile, lat), lambda i: (i + first, 0)),
            whole((nodes, lat)),
        ],
        out_shape=(
            jax.ShapeDtypeStruct((pts, lat), BF),
            jax.ShapeDtypeStruct((nodes, lat), F32),
        ),
        input_output_aliases=alias,
        compiler_params=params(),
        cost_estimate=cost(
            2 * steps * tile * lat * (rows + 2 * lat + nodes), steps * tile * (rows + lat) * 2
        ),
        name="embed",
    )(*args)


def halo_act_kernel(low_ref, up_ref, s_ref, w_in, b_in, w_out, w_msg, b_msg, sum_ref, o_ref):
    half = low_ref.shape[1]
    total = sum_ref[...]
    for k, ref in enumerate((low_ref, up_ref)):
        latent = latent_of(ref[...], TN, w_in[...], b_in[...], w_out[...])
        act = act_of(latent, w_msg[...], b_msg[...])
        total = total + dot(s_ref[:, k * half : (k + 1) * half], act)
    o_ref[...] = total


def halo_act(low, up, counts, weights, total, start):
    rows, half = low.shape
    nodes, lat = total.shape
    at = start // (2 * half)
    return pl.pallas_call(
        halo_act_kernel,
        grid=(1,),
        in_specs=[
            whole(low.shape),
            whole(up.shape),
            pl.BlockSpec((nodes, 2 * half), lambda i: (0, at)),
            *[whole(w.shape) for w in weights],
            whole(total.shape),
        ],
        out_specs=whole(total.shape),
        out_shape=jax.ShapeDtypeStruct(total.shape, F32),
        compiler_params=params(),
        cost_estimate=cost(4 * half * lat * (rows + 2 * lat + nodes), 2 * lat * lat * 2),
        name="halo_act",
    )(low, up, counts, *weights, total)


def node_kernel(
    r_ref, dst_ref, w_in, b_in, w_out, w_msg, b_msg, sum_ref, w_mo, mesh_ref, w_na, w_nb, b_n, w_no, o_ref
):
    nodes = sum_ref.shape[0]
    latent = latent_of(r_ref[...], (((1,), (0,)), ((), ())), w_in[...], b_in[...], w_out[...])
    act = act_of(latent, w_msg[...], b_msg[...])
    ids = lax.broadcasted_iota(jnp.int32, (nodes, dst_ref.shape[1]), 0)
    hot = jnp.where(ids == dst_ref[...], 1.0, 0.0).astype(BF)
    hi, lo = split(sum_ref[...] + dot(hot, act))
    summed = (dot(hi, w_mo[...]) + dot(lo, w_mo[...])).astype(BF)
    mesh = mesh_ref[...]
    pre = dot(mesh, w_na[...]) + dot(summed, w_nb[...]) + b_n[...]
    node = gate(pre).astype(BF)
    o_ref[...] = (mesh.astype(F32) + dot(node, w_no[...])).astype(BF)


def node_update(rows, dst, weights, total, w_mo, mesh, w_na, w_nb, b_n, w_no):
    slots = rows.shape[0]
    lat = total.shape[1]
    return pl.pallas_call(
        node_kernel,
        out_shape=jax.ShapeDtypeStruct(mesh.shape, BF),
        compiler_params=params(),
        cost_estimate=cost(6 * slots * lat * lat, 6 * lat * lat * 2),
        name="node",
    )(rows, dst, *weights, total, w_mo, mesh, w_na, w_nb, b_n, w_no)


def shards(
    fields,
    chan_mean,
    chan_scale,
    w_embed_in,
    b_embed,
    w_embed_out,
    halo_index,
    local_src,
    local_dst,
    remote_src,
    remote_dst,
    w_msg_in,
    b_msg,
    w_msg_out,
    mesh_nodes,
    w_node_in,
    b_node,
    w_node_out,
):
    levels = lax.axis_size("lev")
    tiles = lax.axis_size("tile")
    chans, points = fields.shape
    pts = points // levels
    nodes, lat = mesh_nodes.shape
    slot_count = remote_src.shape[2]
    halo = halo_index.shape[2]
    table = pts + 2 * halo
    wide = (chans + 1) * levels

    me = lax.axis_index("lev").astype(jnp.int32).reshape(1)
    code = remote_dst[0] + 1
    code = jnp.concatenate([code // 16, code % 16], axis=1).astype(F32)
    code = jnp.pad(code, ((0, 0), (0, 128 - code.shape[1])))[:, None, :]
    sent = pack(me, chan_mean, chan_scale, fields, code, levels)
    got = lax.all_to_all(sent, "lev", split_axis=0, concat_axis=0, tiled=True)
    x = got.reshape(wide, pts)

    counts = count_edges(local_src, local_dst, nodes, table)
    w_in = jnp.pad((w_embed_in * 0.5).reshape(levels, chans, lat), ((0, 0), (0, 1), (0, 0)))
    weights = (
        w_in.reshape(wide, lat),
        (b_embed * 0.5)[None, :],
        w_embed_out,
        w_msg_in * 0.5,
        (b_msg * 0.5)[None, :],
    )

    low, high = halo_select(x, halo_index.reshape(1, 2 * halo))
    ahead = [(i, (i + 1) % tiles) for i in range(tiles)]
    back = [(t, s) for s, t in ahead]
    from_low = lax.ppermute(high, "tile", ahead)
    from_up = lax.ppermute(low, "tile", back)
    src = remote_src.reshape(-1, 1)
    own = slots_select(x, src)
    rows = slots_halo(own, from_low, from_up, src, pts)
    rows = lax.all_to_all(
        rows.reshape(levels, slot_count, wide), "lev", split_axis=0, concat_axis=0, tiled=True
    ).reshape(levels * slot_count, wide)

    tile = 512
    steps = pts // tile
    part = embed(x, counts, weights, 0, steps // 2, tile)
    latent, total = embed(x, counts, weights, steps // 2, steps - steps // 2, tile, part)
    total = halo_act(from_low, from_up, counts, weights, total, pts)

    back_code = got[:, chans, : 2 * slot_count].astype(jnp.int32)
    dst = back_code[:, :slot_count] * 16 + back_code[:, slot_count:] - 1
    mesh_out = node_update(
        rows,
        dst.reshape(1, -1),
        weights,
        total,
        w_msg_out,
        mesh_nodes,
        w_node_in[:lat] * 0.5,
        w_node_in[lat:] * 0.5,
        (b_node * 0.5)[None, :],
        w_node_out,
    )
    return (latent, mesh_out)


def solution(mesh):
    return jax.shard_map(
        shards,
        mesh=mesh,
        in_specs=(
            P("lev", "tile"),
            P(),
            P(),
            P(),
            P(),
            P(),
            P(("tile", "lev"), None, None),
            P(("tile", "lev"), None),
            P(("tile", "lev"), None),
            P(("tile", "lev"), None, None),
            P(("tile", "lev"), None, None),
            P(),
            P(),
            P(),
            P(("tile", "lev"), None),
            P(),
            P(),
            P(),
        ),
        out_specs=(P(("tile", "lev"), None), P(("tile", "lev"), None)),
        check_vma=False,
    )
```

```python
import functools

import jax
import jax.numpy as jnp
from jax import lax
from jax.experimental import pallas as pl
from jax.experimental.pallas import tpu as pltpu
from jax.sharding import PartitionSpec as P

BF = jnp.bfloat16
F32 = jnp.float32
NT = (((1,), (1,)), ((), ()))
TN = (((0,), (0,)), ((), ()))
MIB = 1024 * 1024


def params(mib, **kw):
    return pltpu.CompilerParams(vmem_limit_bytes=mib * MIB, **kw)


def whole(shape):
    return pl.BlockSpec(shape, lambda *_: (0,) * len(shape))


def cost(flops, nbytes):
    return pl.CostEstimate(flops=int(flops), bytes_accessed=int(nbytes), transcendentals=0)


def dot(a, b, dims=(((1,), (0,)), ((), ()))):
    return lax.dot_general(a, b, dims, preferred_element_type=F32)


def silu(v):
    h = 0.5 * v
    return (h + h * jnp.tanh(h)).astype(BF)


def hot(ids, index):
    return jnp.where(ids == index, 1.0, 0.0).astype(BF)


def pack_kernel(me_ref, mean_ref, scale_ref, x_ref, o_ref, in_buf, out_buf, in_sem, out_sem, *, parts):
    chans, points = in_buf.shape
    levels, _, pts = out_buf.shape
    per = levels // parts
    width = per * pts

    def load(k):
        at = pl.ds(k * width, width)
        return pltpu.make_async_copy(x_ref.at[:, at], in_buf.at[:, at], in_sem.at[k])

    def store(k):
        at = pl.ds(k * per, per)
        return pltpu.make_async_copy(out_buf.at[at], o_ref.at[at], out_sem.at[k])

    for k in range(parts):
        load(k).start()
    base = me_ref[0] * chans
    row = lax.broadcasted_iota(jnp.int32, (chans, 1), 0)
    mean = jnp.zeros((chans, 1), F32)
    scale = jnp.zeros((chans, 1), F32)
    for c in range(chans):
        mean = jnp.where(row == c, mean_ref[base + c], mean)
        scale = jnp.where(row == c, scale_ref[base + c], scale)
    pad = jnp.zeros((1, pts), F32)
    for k in range(parts):
        load(k).wait()
        for j in range(k * per, (k + 1) * per):
            val = (in_buf[:, j * pts : (j + 1) * pts] - mean) * scale
            out_buf[j] = jnp.concatenate([val, pad], axis=0).astype(BF)
        store(k).start()
    for k in range(parts):
        store(k).wait()


def pack(me, mean, scale, fields, levels):
    chans, points = fields.shape
    pts = points // levels
    parts = 8
    smem = pl.BlockSpec(memory_space=pltpu.SMEM)
    shape = (levels, chans + 1, pts)
    return pl.pallas_call(
        functools.partial(pack_kernel, parts=parts),
        in_specs=[smem, smem, smem, pl.BlockSpec(memory_space=pl.ANY)],
        out_specs=pl.BlockSpec(memory_space=pl.ANY),
        out_shape=jax.ShapeDtypeStruct(shape, BF),
        scratch_shapes=[
            pltpu.VMEM(fields.shape, F32),
            pltpu.VMEM(shape, BF),
            pltpu.SemaphoreType.DMA((parts,)),
            pltpu.SemaphoreType.DMA((parts,)),
        ],
        compiler_params=params(60),
        cost_estimate=cost(points * 16, points * 48),
        name="pack",
    )(me, mean, scale, fields)


def count_kernel(src_ref, dst_ref, w_ref, mesh_ref, w_na, b_n, o_ref, w_in_ref, pre_ref, hot_ref, *, chans):
    nodes, edges = hot_ref.shape
    tile = o_ref.shape[1]
    chunk = 1024

    @pl.when(pl.program_id(0) == 0)
    def _():
        ids = lax.broadcasted_iota(jnp.int32, (nodes, edges), 0)
        hot_ref[...] = hot(ids, dst_ref[...])
        shape = (w_in_ref.shape[0], w_ref.shape[0])
        row = lax.broadcasted_iota(jnp.int32, shape, 0)
        col = lax.broadcasted_iota(jnp.int32, shape, 1)
        lane = row % (chans + 1)
        place = jnp.where(lane < chans, row // (chans + 1) * chans + lane, -1)
        w_in_ref[...] = dot(hot(col, place), w_ref[...]).astype(BF)
        pre_ref[...] = dot(mesh_ref[...], w_na[...]) + b_n[...]

    rows = lax.broadcasted_iota(jnp.int32, (tile, chunk), 0) + pl.program_id(0) * tile
    acc = jnp.zeros((nodes, tile), F32)
    for c in range(edges // chunk):
        at = slice(c * chunk, (c + 1) * chunk)
        acc = acc + dot(hot_ref[:, at], hot(rows, src_ref[:, at]), NT)
    o_ref[...] = acc.astype(BF)


def count_edges(src, dst, w_in, mesh, w_node, b_node, table, wide, chans):
    edges = src.shape[1]
    nodes, lat = mesh.shape
    tile = 512
    return pl.pallas_call(
        functools.partial(count_kernel, chans=chans),
        grid=(table // tile,),
        in_specs=[
            whole((1, edges)),
            whole((1, edges)),
            whole(w_in.shape),
            whole(mesh.shape),
            whole((lat, lat)),
            whole((1, lat)),
        ],
        out_specs=[
            pl.BlockSpec((nodes, tile), lambda i: (0, i)),
            whole((wide, lat)),
            whole((nodes, lat)),
        ],
        out_shape=(
            jax.ShapeDtypeStruct((nodes, table), BF),
            jax.ShapeDtypeStruct((wide, lat), BF),
            jax.ShapeDtypeStruct((nodes, lat), F32),
        ),
        scratch_shapes=[pltpu.VMEM((nodes, edges), BF)],
        compiler_params=params(28),
        cost_estimate=cost(2 * nodes * edges * table, nodes * table * 2),
        name="count",
    )(src, dst, w_in, mesh, w_node, b_node)


def select_kernel(x_ref, idx_ref, src_ref, low_ref, high_ref, own_ref):
    pts = x_ref.shape[1]
    half = low_ref.shape[1]
    chunk = 1024
    near = jnp.zeros((x_ref.shape[0], 2 * half), F32)
    far = jnp.zeros(own_ref.shape, F32)
    for c in range(pts // chunk):
        x = x_ref[:, c * chunk : (c + 1) * chunk]
        rows = lax.broadcasted_iota(jnp.int32, (chunk, 2 * half), 0) + c * chunk
        near = near + dot(x, hot(rows, idx_ref[...]))
        rows = lax.broadcasted_iota(jnp.int32, (chunk, far.shape[1]), 0) + c * chunk
        far = far + dot(x, hot(rows, src_ref[...]))
    low_ref[...] = near[:, :half].astype(BF)
    high_ref[...] = near[:, half:].astype(BF)
    own_ref[...] = far.astype(BF)


def select(x, idx, src):
    rows, pts = x.shape
    half = idx.shape[1] // 2
    slots = src.shape[1]
    out = jax.ShapeDtypeStruct((rows, half), BF)
    return pl.pallas_call(
        select_kernel,
        out_shape=(out, out, jax.ShapeDtypeStruct((rows, slots), BF)),
        compiler_params=params(24),
        cost_estimate=cost(2 * rows * pts * (2 * half + slots), rows * pts * 2),
        name="select",
    )(x, idx, src)


def slots_kernel(own_ref, low_ref, up_ref, src_ref, dst_ref, o_ref, *, start, pad):
    half = low_ref.shape[1]
    shape = (half, own_ref.shape[1])
    ids = lax.broadcasted_iota(jnp.int32, shape, 0) + start
    acc = own_ref[...].astype(F32)
    acc = acc + dot(low_ref[...], hot(ids, src_ref[...]))
    acc = acc + dot(up_ref[...], hot(ids + half, src_ref[...]))
    code = dst_ref[...] + 1
    row = lax.broadcasted_iota(jnp.int32, acc.shape, 0)
    acc = jnp.where(row == pad, (code // 16).astype(F32), acc)
    acc = jnp.where(row == 2 * pad + 1, (code % 16).astype(F32), acc)
    o_ref[...] = acc.T.astype(BF)


def slots_rows(own, low, up, src, dst, start, pad):
    rows, slots = own.shape
    return pl.pallas_call(
        functools.partial(slots_kernel, start=start, pad=pad),
        out_shape=jax.ShapeDtypeStruct((slots, rows), BF),
        compiler_params=params(16),
        cost_estimate=cost(4 * rows * low.shape[1] * slots, slots * rows * 4),
        name="slots",
    )(own, low, up, src, dst)


def act_of(x, dims, w_in, b_in, w_out, w_msg, b_msg):
    hidden = silu(dot(x, w_in[...], dims) + b_in[...])
    latent = dot(hidden, w_out[...]).astype(BF)
    return latent, silu(dot(latent, w_msg[...]) + b_msg[...])


def first_kernel(x_ref, s_ref, *rest):
    lat_ref, sum_ref = rest[-2:]
    latent, act = act_of(x_ref[...], TN, *rest[:5])
    lat_ref[...] = latent

    @pl.when(pl.program_id(0) == 0)
    def _():
        sum_ref[...] = jnp.zeros_like(sum_ref)

    sum_ref[...] += dot(s_ref[...], act)


def second_kernel(x_ref, s_ref, low_ref, up_ref, s_halo, *rest):
    lat_ref, sum_ref = rest[-2:]
    half = low_ref.shape[1]

    @pl.when(pl.program_id(0) == 0)
    def _():
        total = rest[6][...]
        for k, ref in enumerate((low_ref, up_ref)):
            _, act = act_of(ref[...], TN, *rest[:5])
            total = total + dot(s_halo[:, k * half : (k + 1) * half], act)
        sum_ref[...] = total

    latent, act = act_of(x_ref[...], TN, *rest[:5])
    lat_ref[...] = latent
    sum_ref[...] += dot(s_ref[...], act)


def embed(x, counts, weights, first, steps, tile, before=None):
    rows, pts = x.shape
    nodes = counts.shape[0]
    lat = weights[0].shape[1]
    specs = [
        pl.BlockSpec((rows, tile), lambda i: (0, i + first)),
        pl.BlockSpec((nodes, tile), lambda i: (0, i + first)),
    ]
    args = [x, counts]
    alias = {}
    if before is not None:
        latent, total, low, up = before
        both = 2 * low.shape[1]
        specs += [whole(low.shape), whole(up.shape)]
        specs += [pl.BlockSpec((nodes, both), lambda i: (0, pts // both))]
        args += [low, up, counts]
    specs += [whole(w.shape) for w in weights]
    args += weights
    if before is not None:
        alias = {len(args): 0}
        args += [latent, total]
        specs += [pl.BlockSpec(memory_space=pl.ANY), whole((nodes, lat))]
    return pl.pallas_call(
        first_kernel if before is None else second_kernel,
        grid=(steps,),
        in_specs=specs,
        out_specs=[
            pl.BlockSpec((tile, lat), lambda i: (i + first, 0)),
            whole((nodes, lat)),
        ],
        out_shape=(
            jax.ShapeDtypeStruct((pts, lat), BF),
            jax.ShapeDtypeStruct((nodes, lat), F32),
        ),
        input_output_aliases=alias,
        compiler_params=params(28),
        cost_estimate=cost(
            2 * steps * tile * lat * (rows + 2 * lat + nodes), steps * tile * (rows + lat) * 2
        ),
        name="embed",
    )(*args)


def node_kernel(r_ref, w_in, b_in, w_out, w_msg, b_msg, sum_ref, w_mo, mesh_ref, pre_ref, w_nb, w_no, o_ref, *, pad):
    nodes = sum_ref.shape[0]
    rows = r_ref[...]
    _, act = act_of(rows, (((1,), (0,)), ((), ())), w_in, b_in, w_out, w_msg, b_msg)
    lane = lax.broadcasted_iota(jnp.int32, (8, rows.shape[1]), 1)
    pick = jnp.where(lane == pad, 16.0, jnp.where(lane == 2 * pad + 1, 1.0, 0.0)).astype(BF)
    dst = dot(pick, rows, NT)[:1].astype(jnp.int32) - 1
    ids = lax.broadcasted_iota(jnp.int32, (nodes, rows.shape[0]), 0)
    total = sum_ref[...] + dot(hot(ids, dst), act)
    high = total.astype(BF)
    rest = (total - high.astype(F32)).astype(BF)
    summed = (dot(high, w_mo[...]) + dot(rest, w_mo[...])).astype(BF)
    node = silu(pre_ref[...] + dot(summed, w_nb[...]))
    o_ref[...] = (mesh_ref[...].astype(F32) + dot(node, w_no[...])).astype(BF)


def node_update(rows, weights, total, w_mo, mesh, pre, w_node, w_no, pad):
    nodes, lat = mesh.shape
    slots = rows.shape[0]
    args = [rows, *weights, total, w_mo, mesh, pre]
    return pl.pallas_call(
        functools.partial(node_kernel, pad=pad),
        grid=(1,),
        in_specs=[whole(a.shape) for a in args]
        + [pl.BlockSpec((lat, lat), lambda i: (1, 0)), whole(w_no.shape)],
        out_specs=whole(mesh.shape),
        out_shape=jax.ShapeDtypeStruct(mesh.shape, BF),
        compiler_params=params(24),
        cost_estimate=cost(6 * slots * lat * lat, 6 * lat * lat * 2),
        name="node",
    )(*args, w_node, w_no)


def shards(
    fields,
    chan_mean,
    chan_scale,
    w_embed_in,
    b_embed,
    w_embed_out,
    halo_index,
    local_src,
    local_dst,
    remote_src,
    remote_dst,
    w_msg_in,
    b_msg,
    w_msg_out,
    mesh_nodes,
    w_node_in,
    b_node,
    w_node_out,
):
    levels = lax.axis_size("lev")
    tiles = lax.axis_size("tile")
    chans, points = fields.shape
    pts = points // levels
    slot_count = remote_src.shape[2]
    halo = halo_index.shape[2]
    table = pts + 2 * halo
    wide = (chans + 1) * levels

    me = lax.axis_index("lev").astype(jnp.int32).reshape(1)
    sent = pack(me, chan_mean, chan_scale, fields, levels)
    got = lax.all_to_all(sent, "lev", split_axis=0, concat_axis=0, tiled=True)
    x = got.reshape(wide, pts)

    counts, w_in, pre = count_edges(
        local_src, local_dst, w_embed_in, mesh_nodes, w_node_in, b_node[None, :], table, wide, chans
    )
    weights = [w_in, b_embed[None, :], w_embed_out, w_msg_in, b_msg[None, :]]

    src = remote_src.reshape(1, -1)
    dst = remote_dst.reshape(1, -1)
    low, high, own = select(x, halo_index.reshape(1, 2 * halo), src)
    ahead = [(i, (i + 1) % tiles) for i in range(tiles)]
    back = [(t, s) for s, t in ahead]
    from_low = lax.ppermute(high, "tile", ahead)
    from_up = lax.ppermute(low, "tile", back)

    tile = 512
    steps = pts // tile
    latent, total = embed(x, counts, weights, 0, steps // 2, tile)

    rows = slots_rows(own, from_low, from_up, src, dst, pts, chans)
    rows = lax.all_to_all(
        rows.reshape(levels, slot_count, wide), "lev", split_axis=0, concat_axis=0, tiled=True
    ).reshape(levels * slot_count, wide)

    latent, total = embed(
        x, counts, weights, steps // 2, steps - steps // 2, tile, (latent, total, from_low, from_up)
    )
    mesh_out = node_update(
        rows, weights, total, w_msg_out, mesh_nodes, pre, w_node_in, w_node_out, chans
    )
    return (latent, mesh_out)


def solution(mesh):
    return jax.shard_map(
        shards,
        mesh=mesh,
        in_specs=(
            P("lev", "tile"),
            P(),
            P(),
            P(),
            P(),
            P(),
            P(("tile", "lev"), None, None),
            P(("tile", "lev"), None),
            P(("tile", "lev"), None),
            P(("tile", "lev"), None, None),
            P(("tile", "lev"), None, None),
            P(),
            P(),
            P(),
            P(("tile", "lev"), None),
            P(),
            P(),
            P(),
        ),
        out_specs=(P(("tile", "lev"), None), P(("tile", "lev"), None)),
        check_vma=False,
    )
```

```python
import functools

import jax
import jax.numpy as jnp
from jax import lax
from jax.experimental import pallas as pl
from jax.experimental.pallas import tpu as pltpu
from jax.sharding import PartitionSpec as P

BF = jnp.bfloat16
F32 = jnp.float32
NT = (((1,), (1,)), ((), ()))
TN = (((0,), (0,)), ((), ()))
MIB = 1024 * 1024


def params(mib, **kw):
    return pltpu.CompilerParams(vmem_limit_bytes=mib * MIB, **kw)


def whole(shape):
    return pl.BlockSpec(shape, lambda *_: (0,) * len(shape))


def cost(flops, nbytes):
    return pl.CostEstimate(flops=int(flops), bytes_accessed=int(nbytes), transcendentals=0)


def dot(a, b, dims=(((1,), (0,)), ((), ()))):
    return lax.dot_general(a, b, dims, preferred_element_type=F32)


def silu2(h):
    return (h + h * jnp.tanh(h)).astype(BF)


def hot(ids, index, value=1.0):
    return jnp.where(ids == index, jnp.asarray(value, BF), jnp.asarray(0.0, BF))


def at_vmem(*arrays):
    return [pltpu.with_memory_space_constraint(a, pltpu.VMEM) for a in arrays]


def at_hbm(array):
    return pltpu.with_memory_space_constraint(array, pltpu.HBM)


VM = pl.BlockSpec(memory_space=pltpu.VMEM)
ANY = pl.BlockSpec(memory_space=pl.ANY)


def pack_kernel(me_ref, mean_ref, scale_ref, x_ref, o_ref, in_buf, out_buf, in_sem, out_sem, *, parts):
    chans, points = in_buf.shape
    levels, _, pts = out_buf.shape
    per = levels // parts
    width = per * pts

    def load(k):
        at = pl.ds(k * width, width)
        return pltpu.make_async_copy(x_ref.at[:, at], in_buf.at[:, at], in_sem.at[k])

    def store(k):
        at = pl.ds(k * per, per)
        return pltpu.make_async_copy(out_buf.at[at], o_ref.at[at], out_sem.at[k])

    for k in range(parts):
        load(k).start()
    base = me_ref[0] * chans
    row = lax.broadcasted_iota(jnp.int32, (chans, 1), 0)
    mean = jnp.zeros((chans, 1), F32)
    scale = jnp.zeros((chans, 1), F32)
    for c in range(chans):
        mean = jnp.where(row == c, mean_ref[base + c], mean)
        scale = jnp.where(row == c, scale_ref[base + c], scale)
    pad = jnp.ones((1, pts), F32)
    for k in range(parts):
        load(k).wait()
        for j in range(k * per, (k + 1) * per):
            val = (in_buf[:, j * pts : (j + 1) * pts] - mean) * scale
            out_buf[j] = jnp.concatenate([val, pad], axis=0).astype(BF)
        store(k).start()
    for k in range(parts):
        store(k).wait()


def pack(me, mean, scale, fields, levels):
    chans, points = fields.shape
    pts = points // levels
    parts = 8
    smem = pl.BlockSpec(memory_space=pltpu.SMEM)
    shape = (levels, chans + 1, pts)
    return pl.pallas_call(
        functools.partial(pack_kernel, parts=parts),
        in_specs=[smem, smem, smem, pl.BlockSpec(memory_space=pl.ANY)],
        out_specs=pl.BlockSpec(memory_space=pl.ANY),
        out_shape=jax.ShapeDtypeStruct(shape, BF),
        scratch_shapes=[
            pltpu.VMEM(fields.shape, F32),
            pltpu.VMEM(shape, BF),
            pltpu.SemaphoreType.DMA((parts,)),
            pltpu.SemaphoreType.DMA((parts,)),
        ],
        compiler_params=params(60),
        cost_estimate=cost(points * 16, points * 48),
        name="pack",
    )(me, mean, scale, fields)


def count_kernel(
    src_ref, dst_ref, w_ref, b_ref, mesh_ref, b_n, b_m, w_node, w_out, w_msg,
    o_ref, w_in_ref, pre_ref, out_ref, msg_ref, bm_ref, nb_ref, hot_ref, na_ref, sem, *, chans,
):
    nodes, edges = hot_ref.shape
    lat = w_out.shape[0]
    tile = 512
    chunk = 1024
    pairs = (
        (w_node.at[pl.ds(0, lat)], na_ref),
        (w_node.at[pl.ds(lat, lat)], nb_ref),
        (w_out, out_ref),
        (w_msg, msg_ref),
    )
    copies = [pltpu.make_async_copy(f, t, sem.at[k]) for k, (f, t) in enumerate(pairs)]
    for c in copies:
        c.start()
    ids = lax.broadcasted_iota(jnp.int32, (nodes, edges), 0).astype(jnp.int16)
    hot_ref[...] = hot(ids, dst_ref[...].astype(jnp.int16))
    shape = (w_in_ref.shape[0], w_ref.shape[0])
    row = lax.broadcasted_iota(jnp.int32, shape, 0)
    col = lax.broadcasted_iota(jnp.int32, shape, 1)
    lane = row % (chans + 1)
    place = jnp.where(lane < chans, row // (chans + 1) * chans + lane, -1)
    w_in = dot(hot(col, place, 0.5), w_ref[...])
    rest = 0.5 * b_ref[...]
    row = lax.broadcasted_iota(jnp.int32, w_in.shape, 0)
    for k in range(3):
        part = rest.astype(BF).astype(F32)
        rest = rest - part
        w_in = jnp.where(row == (k + 3) * (chans + 1) - 1, part, w_in)
    w_in_ref[...] = w_in.astype(BF)
    bm_ref[...] = 0.5 * b_m[...]

    @pl.loop(0, o_ref.shape[1] // tile)
    def _(i):
        start = pl.multiple_of(i * tile, tile)
        rows = lax.broadcasted_iota(jnp.int32, (tile, chunk), 0).astype(jnp.int16)
        acc = jnp.zeros((nodes, tile), F32)
        for c in range(edges // chunk):
            at = slice(c * chunk, (c + 1) * chunk)
            acc = acc + dot(hot_ref[:, at], hot(rows, (src_ref[:, at] - start).astype(jnp.int16)), NT)
        o_ref[:, pl.ds(start, tile)] = acc.astype(BF)

    for c in copies:
        c.wait()
    msg_ref[...] = msg_ref[...] * 0.5
    nb_ref[...] = nb_ref[...] * 0.5
    pre_ref[...] = 0.5 * (dot(mesh_ref[...], na_ref[...]) + b_n[...])


def count_edges(src, dst, w_in, b_in, mesh, b_node, b_msg, w_node, w_out, w_msg, table, wide, chans):
    edges = src.shape[1]
    nodes, lat = mesh.shape
    square = pltpu.VMEM((lat, lat), BF)
    return pl.pallas_call(
        functools.partial(count_kernel, chans=chans),
        in_specs=[VM] * 7 + [ANY] * 3,
        out_specs=[VM] * 7,
        out_shape=(
            pltpu.HBM((nodes, table), BF),
            pltpu.VMEM((wide, lat), BF),
            pltpu.HBM((nodes, lat), F32),
            square,
            square,
            pltpu.VMEM((1, lat), F32),
            pltpu.HBM((lat, lat), BF),
        ),
        scratch_shapes=[
            pltpu.VMEM((nodes, edges), BF),
            pltpu.VMEM((lat, lat), BF),
            pltpu.SemaphoreType.DMA((4,)),
        ],
        compiler_params=params(24),
        cost_estimate=cost(2 * nodes * edges * table, nodes * table * 2),
        name="count",
    )(src, dst, w_in, b_in, mesh, b_node, b_msg, *map(at_hbm, (w_node, w_out, w_msg)))


def select_kernel(x_ref, idx_ref, src_ref, low_ref, high_ref, own_ref, keep_ref, near_hot, far_hot, sem):
    pts = x_ref.shape[1]
    half = low_ref.shape[1]
    parts = sem.shape[0]
    chunk = pts // parts

    def load(c):
        at = pl.ds(c * chunk, chunk)
        return pltpu.make_async_copy(x_ref.at[:, at], keep_ref.at[:, at], sem.at[c])

    for c in range(parts):
        load(c).start()
    rows = lax.broadcasted_iota(jnp.int32, (chunk, 2 * half), 0).astype(jnp.int16)
    for c in range(parts):
        at = pl.ds(c * chunk, chunk)
        near_hot[at] = hot(rows, (idx_ref[...] - c * chunk).astype(jnp.int16))
        far_hot[at] = hot(rows, (src_ref[...] - c * chunk).astype(jnp.int16))
    for c in range(parts):
        load(c).wait()
    near = dot(keep_ref[...], near_hot[...])
    low_ref[...] = near[:, :half].astype(BF)
    high_ref[...] = near[:, half:].astype(BF)
    own_ref[...] = dot(keep_ref[...], far_hot[...]).astype(BF)


def select(x, idx, src):
    rows, pts = x.shape
    half = idx.shape[1] // 2
    slots = src.shape[1]
    out = jax.ShapeDtypeStruct((rows, half), BF)
    return pl.pallas_call(
        select_kernel,
        in_specs=[ANY, VM, VM],
        out_specs=[VM] * 4,
        out_shape=(out, out, pltpu.VMEM((rows, slots), BF), pltpu.VMEM(x.shape, BF)),
        scratch_shapes=[
            pltpu.VMEM((pts, 2 * half), BF),
            pltpu.VMEM((pts, slots), BF),
            pltpu.SemaphoreType.DMA((4,)),
        ],
        compiler_params=params(24),
        cost_estimate=cost(2 * rows * pts * (2 * half + slots), rows * pts * 2),
        name="select",
    )(at_hbm(x), idx, src)


def slots_kernel(own_ref, low_ref, up_ref, src_ref, dst_ref, o_ref, *, start, pad):
    half = low_ref.shape[1]
    shape = (half, own_ref.shape[1])
    ids = lax.broadcasted_iota(jnp.int32, shape, 0) + start
    acc = own_ref[...].astype(F32)
    acc = acc + dot(low_ref[...], hot(ids, src_ref[...]))
    acc = acc + dot(up_ref[...], hot(ids + half, src_ref[...]))
    code = dst_ref[...] + 1
    row = lax.broadcasted_iota(jnp.int32, acc.shape, 0)
    acc = jnp.where(row == pad, (code // 16).astype(F32), acc)
    acc = jnp.where(row == 2 * pad + 1, (code % 16).astype(F32), acc)
    o_ref[...] = acc.T.astype(BF)


def slots_rows(own, low, up, src, dst, start, pad):
    rows, slots = own.shape
    return pl.pallas_call(
        functools.partial(slots_kernel, start=start, pad=pad),
        in_specs=[VM] * 5,
        out_shape=jax.ShapeDtypeStruct((slots, rows), BF),
        compiler_params=params(16),
        cost_estimate=cost(4 * rows * low.shape[1] * slots, slots * rows * 4),
        name="slots",
    )(*at_vmem(own, low, up), src, dst)


def act_of(x, dims, w_in, w_out, w_msg, b_msg):
    hidden = silu2(dot(x, w_in[...], dims))
    latent = dot(hidden, w_out[...]).astype(BF)
    return latent, silu2(dot(latent, w_msg[...]) + b_msg[...])


def embed_tiles(x_ref, s_ref, weights, lat_hbm, sum_ref, buf, sem, first, steps, ready):
    tile = buf.shape[1]

    def store(i, slot):
        at = pl.ds(pl.multiple_of((i + first) * tile, tile), tile)
        return pltpu.make_async_copy(buf.at[slot], lat_hbm.at[at], sem.at[slot])

    @pl.loop(0, steps)
    def _(i):
        slot = lax.rem(i, 2)

        @pl.when(i >= 2)
        def _():
            store(i - 2, slot).wait()

        ready(i)
        at = pl.ds(pl.multiple_of(i * tile, tile), tile)
        latent, act = act_of(x_ref[:, at], TN, *weights)
        buf[slot] = latent
        store(i, slot).start()
        sum_ref[...] += dot(s_ref[:, at], act)

    for i in range(max(steps - 2, 0), steps):
        store(i, i % 2).wait()


def columns(src, dst, sem, start):
    width = dst.shape[1]
    return pltpu.make_async_copy(src.at[:, pl.ds(start, width)], dst, sem)


def first_kernel(
    x_ref, w_in, w_out, w_msg, b_msg, s_hbm, lat_ref, sum_ref, s_buf, buf, sem, in_sem, *, first, steps
):
    load = columns(s_hbm, s_buf, in_sem.at[0], 0)
    load.start()
    sum_ref[...] = jnp.zeros_like(sum_ref)

    def ready(i):
        @pl.when(i == 0)
        def _():
            load.wait()

    embed_tiles(
        x_ref, s_buf, (w_in, w_out, w_msg, b_msg), lat_ref, sum_ref, buf, sem, first, steps, ready
    )


def second_kernel(
    low_ref, up_ref, before, w_in, w_out, w_msg, b_msg, s_hbm, x_hbm, _, lat_ref, sum_ref,
    s_buf, x_buf, h_buf, buf, sem, in_sem, *, first, steps,
):
    weights = (w_in, w_out, w_msg, b_msg)
    half = low_ref.shape[1]
    start = first * buf.shape[1]
    loads = (
        columns(s_hbm, h_buf, in_sem.at[0], x_hbm.shape[1]),
        columns(x_hbm, x_buf, in_sem.at[1], start),
        columns(s_hbm, s_buf, in_sem.at[2], start),
    )
    for c in loads:
        c.start()
    acts = [act_of(ref[...], TN, *weights)[1] for ref in (low_ref, up_ref)]
    loads[0].wait()
    total = before[...]
    for k, act in enumerate(acts):
        total = total + dot(h_buf[:, k * half : (k + 1) * half], act)
    sum_ref[...] = total
    loads[1].wait()
    loads[2].wait()
    embed_tiles(x_buf, s_buf, weights, lat_ref, sum_ref, buf, sem, first, steps, lambda i: None)


def embed(x, counts, weights, first, steps, tile, before=None):
    rows, pts = x.shape
    nodes = counts.shape[0]
    lat = weights[0].shape[1]
    span = steps * tile
    inner = [pltpu.VMEM((nodes, span), BF)]
    if before is None:
        args = [*at_vmem(x, *weights), at_hbm(counts)]
        specs = [VM] * 5 + [ANY]
        alias = {}
    else:
        latent, total, low, up = before
        args = [*at_vmem(low, up, total, *weights), at_hbm(counts), at_hbm(x), at_hbm(latent)]
        specs = [VM] * 7 + [ANY] * 3
        alias = {9: 0}
        inner += [pltpu.VMEM((rows, span), BF), pltpu.VMEM((nodes, 2 * low.shape[1]), BF)]
    return pl.pallas_call(
        functools.partial(first_kernel if before is None else second_kernel, first=first, steps=steps),
        in_specs=specs,
        out_specs=[ANY, VM],
        out_shape=(pltpu.HBM((pts, lat), BF), pltpu.VMEM((nodes, lat), F32)),
        scratch_shapes=inner
        + [
            pltpu.VMEM((2, tile, lat), BF),
            pltpu.SemaphoreType.DMA((2,)),
            pltpu.SemaphoreType.DMA((3,)),
        ],
        input_output_aliases=alias,
        compiler_params=params(24),
        cost_estimate=cost(2 * span * lat * (rows + 2 * lat + nodes), span * (rows + lat) * 2),
        name="embed",
    )(*args)


def node_kernel(r_ref, w_in, w_out, w_msg, b_msg, sum_ref, *rest, pad):
    sources, o_ref, buffers, sem = rest[:5], rest[5], rest[6:11], rest[11]
    loads = [pltpu.make_async_copy(f, t, sem.at[k]) for k, (f, t) in enumerate(zip(sources, buffers))]
    for c in loads:
        c.start()
    w_mo, w_nb, pre_ref, w_no, mesh_ref = buffers
    nodes = sum_ref.shape[0]
    rows = r_ref[...]
    _, act = act_of(rows, (((1,), (0,)), ((), ())), w_in, w_out, w_msg, b_msg)
    lane = lax.broadcasted_iota(jnp.int32, (8, rows.shape[1]), 1)
    pick = jnp.where(lane == pad, 16.0, jnp.where(lane == 2 * pad + 1, 1.0, 0.0)).astype(BF)
    dst = dot(pick, rows, NT)[:1].astype(jnp.int32) - 1
    ids = lax.broadcasted_iota(jnp.int32, (nodes, rows.shape[0]), 0)
    total = sum_ref[...] + dot(hot(ids, dst), act)
    high = total.astype(BF)
    low = (total - high.astype(F32)).astype(BF)
    for c in loads:
        c.wait()
    summed = (dot(high, w_mo[...]) + dot(low, w_mo[...])).astype(BF)
    node = silu2(pre_ref[...] + dot(summed, w_nb[...]))
    o_ref[...] = (mesh_ref[...].astype(F32) + dot(node, w_no[...])).astype(BF)


def node_update(rows, weights, total, w_mo, mesh, pre, w_nb, w_no, pad):
    args = at_vmem(rows, *weights, total)
    later = [at_hbm(a) for a in (w_mo, w_nb, pre, w_no, mesh)]
    slots = rows.shape[0]
    lat = mesh.shape[1]
    return pl.pallas_call(
        functools.partial(node_kernel, pad=pad),
        in_specs=[VM] * len(args) + [ANY] * len(later),
        out_specs=VM,
        out_shape=jax.ShapeDtypeStruct(mesh.shape, BF),
        scratch_shapes=[pltpu.VMEM(a.shape, a.dtype) for a in later]
        + [pltpu.SemaphoreType.DMA((len(later),))],
        compiler_params=params(20),
        cost_estimate=cost(6 * slots * lat * lat, 6 * lat * lat * 2),
        name="node",
    )(*args, *later)


def shards(
    fields,
    chan_mean,
    chan_scale,
    w_embed_in,
    b_embed,
    w_embed_out,
    halo_index,
    local_src,
    local_dst,
    remote_src,
    remote_dst,
    w_msg_in,
    b_msg,
    w_msg_out,
    mesh_nodes,
    w_node_in,
    b_node,
    w_node_out,
):
    levels = lax.axis_size("lev")
    tiles = lax.axis_size("tile")
    chans, points = fields.shape
    pts = points // levels
    slot_count = remote_src.shape[2]
    halo = halo_index.shape[2]
    table = pts + 2 * halo
    wide = (chans + 1) * levels

    me = lax.axis_index("lev").astype(jnp.int32).reshape(1)
    sent = pack(me, chan_mean, chan_scale, fields, levels)
    got = lax.all_to_all(sent, "lev", split_axis=0, concat_axis=0, tiled=True)
    x = got.reshape(wide, pts)

    counts, w_in, pre, w_out, w_msg, b_half, w_nb = count_edges(
        local_src,
        local_dst,
        w_embed_in,
        b_embed[None, :],
        mesh_nodes,
        b_node[None, :],
        b_msg[None, :],
        w_node_in,
        w_embed_out,
        w_msg_in,
        table,
        wide,
        chans,
    )
    weights = [w_in, w_out, w_msg, b_half]

    src = remote_src.reshape(1, -1)
    dst = remote_dst.reshape(1, -1)
    low, high, own, kept = select(x, halo_index.reshape(1, 2 * halo), src)
    ahead = [(i, (i + 1) % tiles) for i in range(tiles)]
    back = [(t, s) for s, t in ahead]
    from_low = lax.ppermute(high, "tile", ahead)
    from_up = lax.ppermute(low, "tile", back)

    tile = 512
    steps = pts // tile
    latent, total = embed(kept, counts, weights, 0, steps // 2, tile)

    rows = slots_rows(own, from_low, from_up, src, dst, pts, chans)
    rows = lax.all_to_all(
        rows.reshape(levels, slot_count, wide), "lev", split_axis=0, concat_axis=0, tiled=True
    ).reshape(levels * slot_count, wide)

    latent, total = embed(
        x, counts, weights, steps // 2, steps - steps // 2, tile, (latent, total, from_low, from_up)
    )
    mesh_out = node_update(
        rows, weights, total, w_msg_out, mesh_nodes, pre, w_nb, w_node_out, chans
    )
    return (latent, mesh_out)


def solution(mesh):
    return jax.shard_map(
        shards,
        mesh=mesh,
        in_specs=(
            P("lev", "tile"),
            P(),
            P(),
            P(),
            P(),
            P(),
            P(("tile", "lev"), None, None),
            P(("tile", "lev"), None),
            P(("tile", "lev"), None),
            P(("tile", "lev"), None, None),
            P(("tile", "lev"), None, None),
            P(),
            P(),
            P(),
            P(("tile", "lev"), None),
            P(),
            P(),
            P(),
        ),
        out_specs=(P(("tile", "lev"), None), P(("tile", "lev"), None)),
        check_vma=False,
    )
```

```python
import functools

import jax
import jax.numpy as jnp
from jax import lax
from jax.experimental import pallas as pl
from jax.experimental.pallas import tpu as pltpu
from jax.sharding import PartitionSpec as P

BF = jnp.bfloat16
F32 = jnp.float32
NT = (((1,), (1,)), ((), ()))
TN = (((0,), (0,)), ((), ()))
MIB = 1024 * 1024


def params(mib, **kw):
    return pltpu.CompilerParams(vmem_limit_bytes=mib * MIB, **kw)


def whole(shape):
    return pl.BlockSpec(shape, lambda *_: (0,) * len(shape))


def cost(flops, nbytes):
    return pl.CostEstimate(flops=int(flops), bytes_accessed=int(nbytes), transcendentals=0)


def dot(a, b, dims=(((1,), (0,)), ((), ()))):
    return lax.dot_general(a, b, dims, preferred_element_type=F32)


def silu2(h):
    return (h + h * jnp.tanh(h)).astype(BF)


def hot(ids, index, value=1.0):
    return jnp.where(ids == index, jnp.asarray(value, BF), jnp.asarray(0.0, BF))


def at_vmem(*arrays):
    return [pltpu.with_memory_space_constraint(a, pltpu.VMEM) for a in arrays]


def at_hbm(array):
    return pltpu.with_memory_space_constraint(array, pltpu.HBM)


VM = pl.BlockSpec(memory_space=pltpu.VMEM)
ANY = pl.BlockSpec(memory_space=pl.ANY)


def pack_kernel(me_ref, mean_ref, scale_ref, x_ref, o_ref, in_buf, out_buf, in_sem, out_sem, *, parts):
    chans, points = in_buf.shape
    levels, _, main = out_buf.shape
    pts = points // levels
    per = levels // parts
    width = per * pts

    def load(k):
        at = pl.ds(k * width, width)
        return pltpu.make_async_copy(x_ref.at[:, at], in_buf.at[:, at], in_sem.at[k])

    def store(k):
        at = pl.ds(k * per, per)
        return pltpu.make_async_copy(out_buf.at[at], o_ref.at[at], out_sem.at[k])

    for k in range(parts):
        load(k).start()
    base = me_ref[0] * chans
    row = lax.broadcasted_iota(jnp.int32, (chans, 1), 0)
    mean = jnp.zeros((chans, 1), F32)
    scale = jnp.zeros((chans, 1), F32)
    for c in range(chans):
        mean = jnp.where(row == c, mean_ref[base + c], mean)
        scale = jnp.where(row == c, scale_ref[base + c], scale)
    for k in range(parts):
        load(k).wait()
        for j in range(k * per, (k + 1) * per):
            val = (in_buf[:, j * pts : (j + 1) * pts] - mean) * scale
            last = jnp.concatenate([val[c : c + 1, main:] for c in range(chans)], axis=1)
            out_buf[j] = jnp.concatenate([val[:, :main], last], axis=0).astype(BF)
        store(k).start()
    for k in range(parts):
        store(k).wait()


def pack(me, mean, scale, fields, levels):
    chans, points = fields.shape
    pts = points // levels
    parts = 8
    smem = pl.BlockSpec(memory_space=pltpu.SMEM)
    shape = (levels, chans + 1, pts * chans // (chans + 1))
    return pl.pallas_call(
        functools.partial(pack_kernel, parts=parts),
        in_specs=[smem, smem, smem, pl.BlockSpec(memory_space=pl.ANY)],
        out_specs=pl.BlockSpec(memory_space=pl.ANY),
        out_shape=jax.ShapeDtypeStruct(shape, BF),
        scratch_shapes=[
            pltpu.VMEM(fields.shape, F32),
            pltpu.VMEM(shape, BF),
            pltpu.SemaphoreType.DMA((parts,)),
            pltpu.SemaphoreType.DMA((parts,)),
        ],
        compiler_params=params(60),
        cost_estimate=cost(points * 16, points * 48),
        name="pack",
    )(me, mean, scale, fields)


def count_kernel(
    src_ref, dst_ref, w_ref, b_ref, mesh_ref, b_n, b_m, w_node, w_out, w_msg,
    o_ref, w_in_ref, pre_ref, out_ref, msg_ref, bi_ref, bm_ref, nb_ref, hot_ref, na_ref, sem, *, chans,
):
    nodes, edges = hot_ref.shape
    lat = w_out.shape[0]
    tile = 512
    chunk = 1024
    pairs = (
        (w_node.at[pl.ds(0, lat)], na_ref),
        (w_node.at[pl.ds(lat, lat)], nb_ref),
        (w_out, out_ref),
        (w_msg, msg_ref),
    )
    copies = [pltpu.make_async_copy(f, t, sem.at[k]) for k, (f, t) in enumerate(pairs)]
    for c in copies:
        c.start()
    ids = lax.broadcasted_iota(jnp.int32, (nodes, edges), 0).astype(jnp.int16)
    hot_ref[...] = hot(ids, dst_ref[...].astype(jnp.int16))
    shape = (w_in_ref.shape[0], w_ref.shape[0])
    row = lax.broadcasted_iota(jnp.int32, shape, 0)
    col = lax.broadcasted_iota(jnp.int32, shape, 1)
    lane = row % (chans + 1)
    place = jnp.where(lane < chans, row // (chans + 1) * chans + lane, -1)
    w_in_ref[...] = dot(hot(col, place, 0.5), w_ref[...]).astype(BF)
    bi_ref[...] = 0.5 * b_ref[...]
    bm_ref[...] = 0.5 * b_m[...]

    @pl.loop(0, o_ref.shape[1] // tile)
    def _(i):
        start = pl.multiple_of(i * tile, tile)
        rows = lax.broadcasted_iota(jnp.int32, (tile, chunk), 0).astype(jnp.int16)
        acc = jnp.zeros((nodes, tile), F32)
        for c in range(edges // chunk):
            at = slice(c * chunk, (c + 1) * chunk)
            acc = acc + dot(hot_ref[:, at], hot(rows, (src_ref[:, at] - start).astype(jnp.int16)), NT)
        o_ref[:, pl.ds(start, tile)] = acc.astype(BF)

    for c in copies:
        c.wait()
    msg_ref[...] = msg_ref[...] * 0.5
    nb_ref[...] = nb_ref[...] * 0.5
    pre_ref[...] = 0.5 * (dot(mesh_ref[...], na_ref[...]) + b_n[...])


def count_edges(src, dst, w_in, b_in, mesh, b_node, b_msg, w_node, w_out, w_msg, table, wide, chans):
    edges = src.shape[1]
    nodes, lat = mesh.shape
    square = pltpu.VMEM((lat, lat), BF)
    return pl.pallas_call(
        functools.partial(count_kernel, chans=chans),
        in_specs=[VM] * 7 + [ANY] * 3,
        out_specs=[VM] * 8,
        out_shape=(
            pltpu.HBM((nodes, table), BF),
            pltpu.VMEM((wide, lat), BF),
            pltpu.HBM((nodes, lat), F32),
            square,
            square,
            pltpu.VMEM((1, lat), F32),
            pltpu.VMEM((1, lat), F32),
            pltpu.HBM((lat, lat), BF),
        ),
        scratch_shapes=[
            pltpu.VMEM((nodes, edges), BF),
            pltpu.VMEM((lat, lat), BF),
            pltpu.SemaphoreType.DMA((4,)),
        ],
        compiler_params=params(24),
        cost_estimate=cost(2 * nodes * edges * table, nodes * table * 2),
        name="count",
    )(src, dst, w_in, b_in, mesh, b_node, b_msg, *map(at_hbm, (w_node, w_out, w_msg)))


def hots(index, ref):
    step = 1024
    ids = lax.broadcasted_iota(jnp.int32, (step, ref.shape[1]), 0).astype(jnp.int16)
    for start in range(0, ref.shape[0], step):
        ref[pl.ds(start, step)] = hot(ids, (index - start).astype(jnp.int16))


def select_kernel(x_ref, idx_ref, src_ref, low_ref, high_ref, own_ref, keep_ref, near_hot, far_hot, sem, *, chans):
    rows, main = x_ref.shape
    half = low_ref.shape[1]
    last = main // chans
    group = chans + 1
    load = pltpu.make_async_copy(x_ref, keep_ref.at[:, pl.ds(0, main)], sem)
    load.start()
    hots(idx_ref[...], near_hot)
    hots(src_ref[...], far_hot)
    load.wait()
    row = lax.broadcasted_iota(jnp.int32, (1, group, 1), 1)
    tail = jnp.zeros((rows // group, group, last), F32)
    for c in range(chans):
        part = keep_ref[:, c * last : (c + 1) * last].astype(F32).reshape(rows // group, group, last)
        tail = jnp.where(row == c, part[:, chans:], tail)
    tail = tail.reshape(rows, last).astype(BF)
    keep_ref[:, main:] = tail
    near = dot(keep_ref[...], near_hot[...])
    low_ref[...] = near[:, :half].astype(BF)
    high_ref[...] = near[:, half:].astype(BF)
    own_ref[...] = dot(keep_ref[...], far_hot[...]).astype(BF)


def select(x, idx, src, chans):
    rows, main = x.shape
    pts = main // chans * (chans + 1)
    half = idx.shape[1] // 2
    slots = src.shape[1]
    out = jax.ShapeDtypeStruct((rows, half), BF)
    return pl.pallas_call(
        functools.partial(select_kernel, chans=chans),
        in_specs=[ANY, VM, VM],
        out_specs=[VM] * 4,
        out_shape=(out, out, pltpu.VMEM((rows, slots), BF), pltpu.VMEM((rows, pts), BF)),
        scratch_shapes=[
            pltpu.VMEM((pts, 2 * half), BF),
            pltpu.VMEM((pts, slots), BF),
            pltpu.SemaphoreType.DMA,
        ],
        compiler_params=params(24),
        cost_estimate=cost(2 * rows * pts * (2 * half + slots), rows * pts * 2),
        name="select",
    )(at_hbm(x), idx, src)


def slots_kernel(own_ref, low_ref, up_ref, src_ref, dst_ref, o_ref, *, start, pad):
    half = low_ref.shape[1]
    shape = (half, own_ref.shape[1])
    ids = lax.broadcasted_iota(jnp.int32, shape, 0) + start
    acc = own_ref[...].astype(F32)
    acc = acc + dot(low_ref[...], hot(ids, src_ref[...]))
    acc = acc + dot(up_ref[...], hot(ids + half, src_ref[...]))
    code = dst_ref[...] + 1
    row = lax.broadcasted_iota(jnp.int32, acc.shape, 0)
    acc = jnp.where(row == pad, (code // 16).astype(F32), acc)
    acc = jnp.where(row == 2 * pad + 1, (code % 16).astype(F32), acc)
    o_ref[...] = acc.T.astype(BF)


def slots_rows(own, low, up, src, dst, start, pad):
    rows, slots = own.shape
    return pl.pallas_call(
        functools.partial(slots_kernel, start=start, pad=pad),
        in_specs=[VM] * 5,
        out_shape=jax.ShapeDtypeStruct((slots, rows), BF),
        compiler_params=params(16),
        cost_estimate=cost(4 * rows * low.shape[1] * slots, slots * rows * 4),
        name="slots",
    )(*at_vmem(own, low, up), src, dst)


def act_of(x, dims, w_in, b_in, w_out, w_msg, b_msg):
    hidden = silu2(dot(x, w_in[...], dims) + b_in[...])
    latent = dot(hidden, w_out[...]).astype(BF)
    return latent, silu2(dot(latent, w_msg[...]) + b_msg[...])


def columns(src, dst, sem, spans):
    copies = []
    at = 0
    for k, (start, width) in enumerate(spans):
        copies.append(
            pltpu.make_async_copy(
                src.at[:, pl.ds(start, width)], dst.at[:, pl.ds(at, width)], sem.at[k]
            )
        )
        copies[-1].start()
        at += width
    return copies


def embed_tiles(x_ref, weights, lat_hbm, act_ref, buf, sem, starts, tile):
    stores = []
    for i, (col, point) in enumerate(starts):
        rows = pl.ds(i * tile, tile)
        latent, act = act_of(x_ref[:, col : col + tile], TN, *weights)
        buf[rows] = latent
        stores.append(
            pltpu.make_async_copy(buf.at[rows], lat_hbm.at[pl.ds(point, tile)], sem.at[i])
        )
        stores[-1].start()
        act_ref[rows] = act
    return stores


def first_kernel(x_ref, w_in, b_in, w_out, w_msg, b_msg, s_hbm, lat_ref, sum_ref, s_buf, act_buf, buf, sem, in_sem, *, spans, tile):
    loads = columns(s_hbm, s_buf, in_sem, spans)
    weights = (w_in, b_in, w_out, w_msg, b_msg)
    starts = [(p, p) for start, width in spans for p in range(start, start + width, tile)]
    stores = embed_tiles(x_ref, weights, lat_ref, act_buf, buf, sem, starts, tile)
    for c in loads:
        c.wait()
    sum_ref[...] = dot(s_buf[...], act_buf[...])
    for c in stores:
        c.wait()


def second_kernel(
    low_ref, up_ref, before, w_in, b_in, w_out, w_msg, b_msg, s_hbm, x_hbm, _, lat_ref, sum_ref,
    s_buf, act_buf, buf, x_buf, sem, in_sem, x_sem, *, spans, tile,
):
    weights = (w_in, b_in, w_out, w_msg, b_msg)
    half = low_ref.shape[1]
    x_load = columns(x_hbm, x_buf, x_sem, spans[:1])
    loads = columns(s_hbm, s_buf, in_sem, spans)
    start, width = spans[0]
    for k, ref in enumerate((low_ref, up_ref)):
        act_buf[pl.ds(width + k * half, half)] = act_of(ref[...], TN, *weights)[1]
    x_load[0].wait()
    starts = [(p, start + p) for p in range(0, width, tile)]
    stores = embed_tiles(x_buf, weights, lat_ref, act_buf, buf, sem, starts, tile)
    for c in loads:
        c.wait()
    sum_ref[...] = before[...] + dot(s_buf[...], act_buf[...])
    for c in stores:
        c.wait()


def embed(x, counts, weights, pts, spans, tile, before=None):
    rows = x.shape[0]
    nodes = counts.shape[0]
    lat = weights[0].shape[1]
    wide = sum(width for _, width in spans)
    if before is None:
        kernel = first_kernel
        span = wide
        args = [*at_vmem(x, *weights), at_hbm(counts)]
        specs = [VM] * 6 + [ANY]
        alias = {}
        inner = []
        tail = []
    else:
        kernel = second_kernel
        span = spans[0][1]
        latent, total, low, up = before
        args = [*at_vmem(low, up, total, *weights), at_hbm(counts), at_hbm(x), at_hbm(latent)]
        specs = [VM] * 8 + [ANY] * 3
        alias = {10: 0}
        inner = [pltpu.VMEM((rows, span), BF)]
        tail = [pltpu.SemaphoreType.DMA((1,))]
    return pl.pallas_call(
        functools.partial(kernel, spans=spans, tile=tile),
        in_specs=specs,
        out_specs=[ANY, VM],
        out_shape=(pltpu.HBM((pts, lat), BF), pltpu.VMEM((nodes, lat), F32)),
        scratch_shapes=[
            pltpu.VMEM((nodes, wide), BF),
            pltpu.VMEM((wide, lat), BF),
            pltpu.VMEM((span, lat), BF),
            *inner,
            pltpu.SemaphoreType.DMA((span // tile,)),
            pltpu.SemaphoreType.DMA((len(spans),)),
            *tail,
        ],
        input_output_aliases=alias,
        compiler_params=params(24),
        cost_estimate=cost(2 * span * lat * (rows + 2 * lat + nodes), span * (rows + lat) * 2),
        name="embed",
    )(*args)


def node_kernel(r_ref, w_in, b_in, w_out, w_msg, b_msg, sum_ref, *rest, pad):
    sources, o_ref, buffers, sem = rest[:5], rest[5], rest[6:11], rest[11]
    loads = [pltpu.make_async_copy(f, t, sem.at[k]) for k, (f, t) in enumerate(zip(sources, buffers))]
    for c in loads:
        c.start()
    w_mo, w_nb, pre_ref, w_no, mesh_ref = buffers
    nodes = sum_ref.shape[0]
    rows = r_ref[...]
    _, act = act_of(rows, (((1,), (0,)), ((), ())), w_in, b_in, w_out, w_msg, b_msg)
    lane = lax.broadcasted_iota(jnp.int32, (8, rows.shape[1]), 1)
    pick = jnp.where(lane == pad, 16.0, jnp.where(lane == 2 * pad + 1, 1.0, 0.0)).astype(BF)
    dst = dot(pick, rows, NT)[:1].astype(jnp.int32) - 1
    ids = lax.broadcasted_iota(jnp.int32, (nodes, rows.shape[0]), 0)
    total = sum_ref[...] + dot(hot(ids, dst), act)
    high = total.astype(BF)
    low = (total - high.astype(F32)).astype(BF)
    for c in loads:
        c.wait()
    summed = (dot(high, w_mo[...]) + dot(low, w_mo[...])).astype(BF)
    node = silu2(pre_ref[...] + dot(summed, w_nb[...]))
    o_ref[...] = (mesh_ref[...].astype(F32) + dot(node, w_no[...])).astype(BF)


def node_update(rows, weights, total, w_mo, mesh, pre, w_nb, w_no, pad):
    args = at_vmem(rows, *weights, total)
    later = [at_hbm(a) for a in (w_mo, w_nb, pre, w_no, mesh)]
    slots = rows.shape[0]
    lat = mesh.shape[1]
    return pl.pallas_call(
        functools.partial(node_kernel, pad=pad),
        in_specs=[VM] * len(args) + [ANY] * len(later),
        out_specs=VM,
        out_shape=jax.ShapeDtypeStruct(mesh.shape, BF),
        scratch_shapes=[pltpu.VMEM(a.shape, a.dtype) for a in later]
        + [pltpu.SemaphoreType.DMA((len(later),))],
        compiler_params=params(20),
        cost_estimate=cost(6 * slots * lat * lat, 6 * lat * lat * 2),
        name="node",
    )(*args, *later)


def shards(
    fields,
    chan_mean,
    chan_scale,
    w_embed_in,
    b_embed,
    w_embed_out,
    halo_index,
    local_src,
    local_dst,
    remote_src,
    remote_dst,
    w_msg_in,
    b_msg,
    w_msg_out,
    mesh_nodes,
    w_node_in,
    b_node,
    w_node_out,
):
    levels = lax.axis_size("lev")
    tiles = lax.axis_size("tile")
    chans, points = fields.shape
    pts = points // levels
    slot_count = remote_src.shape[2]
    halo = halo_index.shape[2]
    table = pts + 2 * halo
    wide = (chans + 1) * levels

    me = lax.axis_index("lev").astype(jnp.int32).reshape(1)
    sent = pack(me, chan_mean, chan_scale, fields, levels)
    got = lax.all_to_all(sent, "lev", split_axis=0, concat_axis=0, tiled=True)
    main = pts // (chans + 1) * chans
    x = got.reshape(wide, main)

    counts, w_in, pre, w_out, w_msg, b_in, b_out, w_nb = count_edges(
        local_src,
        local_dst,
        w_embed_in,
        b_embed[None, :],
        mesh_nodes,
        b_node[None, :],
        b_msg[None, :],
        w_node_in,
        w_embed_out,
        w_msg_in,
        table,
        wide,
        chans,
    )
    weights = [w_in, b_in, w_out, w_msg, b_out]

    src = remote_src.reshape(1, -1)
    dst = remote_dst.reshape(1, -1)
    low, high, own, kept = select(x, halo_index.reshape(1, 2 * halo), src, chans)
    ahead = [(i, (i + 1) % tiles) for i in range(tiles)]
    back = [(t, s) for s, t in ahead]
    from_low = lax.ppermute(high, "tile", ahead)
    from_up = lax.ppermute(low, "tile", back)

    tile = 512
    cut = pts // 2 - (pts - main)
    latent, total = embed(kept, counts, weights, pts, ((0, cut), (main, pts - main)), tile)

    rows = slots_rows(own, from_low, from_up, src, dst, pts, chans)
    rows = lax.all_to_all(
        rows.reshape(levels, slot_count, wide), "lev", split_axis=0, concat_axis=0, tiled=True
    ).reshape(levels * slot_count, wide)

    latent, total = embed(
        x,
        counts,
        weights,
        pts,
        ((cut, main - cut), (pts, 2 * halo)),
        tile,
        (latent, total, from_low, from_up),
    )
    mesh_out = node_update(
        rows, weights, total, w_msg_out, mesh_nodes, pre, w_nb, w_node_out, chans
    )
    return (latent, mesh_out)


def solution(mesh):
    return jax.shard_map(
        shards,
        mesh=mesh,
        in_specs=(
            P("lev", "tile"),
            P(),
            P(),
            P(),
            P(),
            P(),
            P(("tile", "lev"), None, None),
            P(("tile", "lev"), None),
            P(("tile", "lev"), None),
            P(("tile", "lev"), None, None),
            P(("tile", "lev"), None, None),
            P(),
            P(),
            P(),
            P(("tile", "lev"), None),
            P(),
            P(),
            P(),
        ),
        out_specs=(P(("tile", "lev"), None), P(("tile", "lev"), None)),
        check_vma=False,
    )
```

```python
import functools

import jax
import jax.numpy as jnp
from jax import lax
from jax.experimental import pallas as pl
from jax.experimental.pallas import tpu as pltpu
from jax.sharding import PartitionSpec as P

BF = jnp.bfloat16
F32 = jnp.float32
NT = (((1,), (1,)), ((), ()))
TN = (((0,), (0,)), ((), ()))
CUT = 1
MIB = 1024 * 1024


def params(mib, **kw):
    return pltpu.CompilerParams(vmem_limit_bytes=mib * MIB, **kw)


def whole(shape):
    return pl.BlockSpec(shape, lambda *_: (0,) * len(shape))


def cost(flops, nbytes):
    return pl.CostEstimate(flops=int(flops), bytes_accessed=int(nbytes), transcendentals=0)


def dot(a, b, dims=(((1,), (0,)), ((), ()))):
    return lax.dot_general(a, b, dims, preferred_element_type=F32)


def silu2(h):
    return (h + h * jnp.tanh(h)).astype(BF)


def hot(ids, index, value=1.0):
    return jnp.where(ids == index, jnp.asarray(value, BF), jnp.asarray(0.0, BF))


def at_vmem(*arrays):
    return [pltpu.with_memory_space_constraint(a, pltpu.VMEM) for a in arrays]


def at_hbm(array):
    return pltpu.with_memory_space_constraint(array, pltpu.HBM)


VM = pl.BlockSpec(memory_space=pltpu.VMEM)
ANY = pl.BlockSpec(memory_space=pl.ANY)


def pack_kernel(me_ref, mean_ref, scale_ref, x_ref, o_ref, in_buf, out_buf, in_sem, out_sem, *, parts):
    chans, points = in_buf.shape
    levels, _, main = out_buf.shape
    pts = points // levels
    per = levels // parts
    width = per * pts

    def load(k):
        at = pl.ds(k * width, width)
        return pltpu.make_async_copy(x_ref.at[:, at], in_buf.at[:, at], in_sem.at[k])

    def store(k):
        at = pl.ds(k * per, per)
        return pltpu.make_async_copy(out_buf.at[at], o_ref.at[at], out_sem.at[k])

    for k in range(parts):
        load(k).start()
    base = me_ref[0] * chans
    row = lax.broadcasted_iota(jnp.int32, (chans, 1), 0)
    mean = jnp.zeros((chans, 1), F32)
    scale = jnp.zeros((chans, 1), F32)
    for c in range(chans):
        mean = jnp.where(row == c, mean_ref[base + c], mean)
        scale = jnp.where(row == c, scale_ref[base + c], scale)
    for k in range(parts):
        load(k).wait()
        for j in range(k * per, (k + 1) * per):
            val = (in_buf[:, j * pts : (j + 1) * pts] - mean) * scale
            last = jnp.concatenate([val[c : c + 1, main:] for c in range(chans)], axis=1)
            out_buf[j] = jnp.concatenate([val[:, :main], last], axis=0).astype(BF)
        store(k).start()
    for k in range(parts):
        store(k).wait()


def pack(me, mean, scale, fields, levels):
    chans, points = fields.shape
    pts = points // levels
    parts = 8
    smem = pl.BlockSpec(memory_space=pltpu.SMEM)
    shape = (levels, chans + 1, pts * chans // (chans + 1))
    return pl.pallas_call(
        functools.partial(pack_kernel, parts=parts),
        in_specs=[smem, smem, smem, pl.BlockSpec(memory_space=pl.ANY)],
        out_specs=pl.BlockSpec(memory_space=pl.ANY),
        out_shape=jax.ShapeDtypeStruct(shape, BF),
        scratch_shapes=[
            pltpu.VMEM(fields.shape, F32),
            pltpu.VMEM(shape, BF),
            pltpu.SemaphoreType.DMA((parts,)),
            pltpu.SemaphoreType.DMA((parts,)),
        ],
        compiler_params=params(60),
        cost_estimate=cost(points * 16, points * 48),
        name="pack",
    )(me, mean, scale, fields)


def count_kernel(
    src_ref, dst_ref, w_ref, b_ref, mesh_ref, b_n, b_m, w_node, w_out, w_msg,
    o_ref, w_in_ref, pre_ref, out_ref, msg_ref, bi_ref, bm_ref, nb_ref, hot_ref, na_ref, sem, *, chans,
):
    nodes, edges = hot_ref.shape
    lat = w_out.shape[0]
    tile = 512
    chunk = 1024
    pairs = (
        (w_node.at[pl.ds(0, lat)], na_ref),
        (w_node.at[pl.ds(lat, lat)], nb_ref),
        (w_out, out_ref),
        (w_msg, msg_ref),
    )
    copies = [pltpu.make_async_copy(f, t, sem.at[k]) for k, (f, t) in enumerate(pairs)]
    for c in copies:
        c.start()
    ids = lax.broadcasted_iota(jnp.int32, (nodes, edges), 0).astype(jnp.int16)
    hot_ref[...] = hot(ids, dst_ref[...].astype(jnp.int16))
    shape = (w_in_ref.shape[0], w_ref.shape[0])
    row = lax.broadcasted_iota(jnp.int32, shape, 0)
    col = lax.broadcasted_iota(jnp.int32, shape, 1)
    lane = row % (chans + 1)
    place = jnp.where(lane < chans, row // (chans + 1) * chans + lane, -1)
    w_in_ref[...] = dot(hot(col, place, 0.5), w_ref[...]).astype(BF)
    bi_ref[...] = 0.5 * b_ref[...]
    bm_ref[...] = 0.5 * b_m[...]

    @pl.loop(0, o_ref.shape[1] // tile)
    def _(i):
        start = pl.multiple_of(i * tile, tile)
        rows = lax.broadcasted_iota(jnp.int32, (tile, chunk), 0).astype(jnp.int16)
        acc = jnp.zeros((nodes, tile), F32)
        for c in range(edges // chunk):
            at = slice(c * chunk, (c + 1) * chunk)
            acc = acc + dot(hot_ref[:, at], hot(rows, (src_ref[:, at] - start).astype(jnp.int16)), NT)
        o_ref[:, pl.ds(start, tile)] = acc.astype(BF)

    for c in copies:
        c.wait()
    msg_ref[...] = msg_ref[...] * 0.5
    nb_ref[...] = nb_ref[...] * 0.5
    pre_ref[...] = 0.5 * (dot(mesh_ref[...], na_ref[...]) + b_n[...])


def count_edges(src, dst, w_in, b_in, mesh, b_node, b_msg, w_node, w_out, w_msg, table, wide, chans):
    edges = src.shape[1]
    nodes, lat = mesh.shape
    square = pltpu.VMEM((lat, lat), BF)
    return pl.pallas_call(
        functools.partial(count_kernel, chans=chans),
        in_specs=[VM] * 7 + [ANY] * 3,
        out_specs=[VM] * 8,
        out_shape=(
            pltpu.HBM((nodes, table), BF),
            pltpu.VMEM((wide, lat), BF),
            pltpu.HBM((nodes, lat), F32),
            square,
            square,
            pltpu.VMEM((1, lat), F32),
            pltpu.VMEM((1, lat), F32),
            pltpu.HBM((lat, lat), BF),
        ),
        scratch_shapes=[
            pltpu.VMEM((nodes, edges), BF),
            pltpu.VMEM((lat, lat), BF),
            pltpu.SemaphoreType.DMA((4,)),
        ],
        compiler_params=params(24),
        cost_estimate=cost(2 * nodes * edges * table, nodes * table * 2),
        name="count",
    )(src, dst, w_in, b_in, mesh, b_node, b_msg, *map(at_hbm, (w_node, w_out, w_msg)))


def hots(index, ref):
    step = 1024
    ids = lax.broadcasted_iota(jnp.int32, (step, ref.shape[1]), 0).astype(jnp.int16)
    for start in range(0, ref.shape[0], step):
        ref[pl.ds(start, step)] = hot(ids, (index - start).astype(jnp.int16))


def select_kernel(x_ref, idx_ref, low_ref, high_ref, keep_ref, near_hot, sem, *, chans):
    rows, main = x_ref.shape
    half = low_ref.shape[1]
    last = main // chans
    group = chans + 1
    load = pltpu.make_async_copy(x_ref, keep_ref.at[:, pl.ds(0, main)], sem)
    load.start()
    hots(idx_ref[...], near_hot)
    load.wait()
    near = dot(keep_ref[:, :main], near_hot[:main])
    row = lax.broadcasted_iota(jnp.int32, (1, group, 1), 1)
    tail = jnp.zeros((rows // group, group, last), F32)
    for c in range(chans):
        part = keep_ref[:, c * last : (c + 1) * last].astype(F32).reshape(rows // group, group, last)
        tail = jnp.where(row == c, part[:, chans:], tail)
    tail = tail.reshape(rows, last).astype(BF)
    keep_ref[:, main:] = tail
    near = near + dot(tail, near_hot[main:])
    low_ref[...] = near[:, :half].astype(BF)
    high_ref[...] = near[:, half:].astype(BF)


def select(x, idx, chans):
    rows, main = x.shape
    pts = main // chans * (chans + 1)
    half = idx.shape[1] // 2
    out = jax.ShapeDtypeStruct((rows, half), BF)
    return pl.pallas_call(
        functools.partial(select_kernel, chans=chans),
        in_specs=[ANY, VM],
        out_specs=[VM] * 3,
        out_shape=(out, out, pltpu.VMEM((rows, pts), BF)),
        scratch_shapes=[pltpu.VMEM((pts, 2 * half), BF), pltpu.SemaphoreType.DMA],
        compiler_params=params(24),
        cost_estimate=cost(4 * rows * pts * half, rows * pts * 2),
        name="select",
    )(at_hbm(x), idx)


def slots_kernel(own_ref, low_ref, up_ref, src_ref, dst_ref, o_ref, *, start, pad):
    half = low_ref.shape[1]
    shape = (half, own_ref.shape[1])
    ids = lax.broadcasted_iota(jnp.int32, shape, 0) + start
    acc = own_ref[...].astype(F32)
    acc = acc + dot(low_ref[...], hot(ids, src_ref[...]))
    acc = acc + dot(up_ref[...], hot(ids + half, src_ref[...]))
    code = dst_ref[...] + 1
    row = lax.broadcasted_iota(jnp.int32, acc.shape, 0)
    acc = jnp.where(row == pad, (code // 16).astype(F32), acc)
    acc = jnp.where(row == 2 * pad + 1, (code % 16).astype(F32), acc)
    o_ref[...] = acc.T.astype(BF)


def slots_rows(own, low, up, src, dst, start, pad):
    rows, slots = own.shape
    return pl.pallas_call(
        functools.partial(slots_kernel, start=start, pad=pad),
        in_specs=[VM] * 5,
        out_shape=jax.ShapeDtypeStruct((slots, rows), BF),
        compiler_params=params(16),
        cost_estimate=cost(4 * rows * low.shape[1] * slots, slots * rows * 4),
        name="slots",
    )(*at_vmem(own, low, up), src, dst)


def act_of(x, dims, w_in, b_in, w_out, w_msg, b_msg):
    hidden = silu2(dot(x, w_in[...], dims) + b_in[...])
    latent = dot(hidden, w_out[...]).astype(BF)
    return latent, silu2(dot(latent, w_msg[...]) + b_msg[...])


def columns(src, dst, sem, spans):
    copies = []
    at = 0
    for k, (start, width) in enumerate(spans):
        copies.append(
            pltpu.make_async_copy(
                src.at[:, pl.ds(start, width)], dst.at[:, pl.ds(at, width)], sem.at[k]
            )
        )
        copies[-1].start()
        at += width
    return copies


def embed_tiles(x_ref, weights, lat_hbm, act_ref, buf, sem, starts, tile):
    stores = []
    for i, (col, point) in enumerate(starts):
        rows = pl.ds(i * tile, tile)
        latent, act = act_of(x_ref[:, col : col + tile], TN, *weights)
        buf[rows] = latent
        stores.append(
            pltpu.make_async_copy(buf.at[rows], lat_hbm.at[pl.ds(point, tile)], sem.at[i])
        )
        stores[-1].start()
        act_ref[rows] = act
    return stores


def first_kernel(
    x_ref, src_ref, w_in, b_in, w_out, w_msg, b_msg, s_hbm, lat_ref, sum_ref, own_ref,
    s_buf, act_buf, buf, far_hot, sem, in_sem, *, spans, tile,
):
    loads = columns(s_hbm, s_buf, in_sem, spans)
    weights = (w_in, b_in, w_out, w_msg, b_msg)
    starts = [(p, p) for start, width in spans for p in range(start, start + width, tile)]
    hots(src_ref[...], far_hot)
    stores = embed_tiles(x_ref, weights, lat_ref, act_buf, buf, sem, starts, tile)
    own_ref[...] = dot(x_ref[...], far_hot[...]).astype(BF)
    for c in loads:
        c.wait()
    sum_ref[...] = dot(s_buf[...], act_buf[...])
    for c in stores:
        c.wait()


def second_kernel(
    low_ref, up_ref, before, w_in, b_in, w_out, w_msg, b_msg, s_hbm, x_hbm, _, lat_ref, sum_ref,
    s_buf, act_buf, buf, x_buf, sem, in_sem, x_sem, *, spans, tile,
):
    weights = (w_in, b_in, w_out, w_msg, b_msg)
    half = low_ref.shape[1]
    x_load = columns(x_hbm, x_buf, x_sem, spans[:1])
    loads = columns(s_hbm, s_buf, in_sem, spans)
    start, width = spans[0]
    for k, ref in enumerate((low_ref, up_ref)):
        act_buf[pl.ds(width + k * half, half)] = act_of(ref[...], TN, *weights)[1]
    x_load[0].wait()
    starts = [(p, start + p) for p in range(0, width, tile)]
    stores = embed_tiles(x_buf, weights, lat_ref, act_buf, buf, sem, starts, tile)
    for c in loads:
        c.wait()
    sum_ref[...] = before[...] + dot(s_buf[...], act_buf[...])
    for c in stores:
        c.wait()


def embed(x, counts, weights, pts, spans, tile, src=None, before=None):
    rows = x.shape[0]
    nodes = counts.shape[0]
    lat = weights[0].shape[1]
    wide = sum(width for _, width in spans)
    if before is None:
        kernel = first_kernel
        span = wide
        args = [*at_vmem(x), src, *at_vmem(*weights), at_hbm(counts)]
        specs = [VM] * 7 + [ANY]
        alias = {}
        inner = [pltpu.VMEM((pts, src.shape[1]), BF)]
        tail = []
        more = [pltpu.VMEM((rows, src.shape[1]), BF)]
    else:
        kernel = second_kernel
        span = spans[0][1]
        latent, total, low, up = before
        args = [*at_vmem(low, up, total, *weights), at_hbm(counts), at_hbm(x), at_hbm(latent)]
        specs = [VM] * 8 + [ANY] * 3
        alias = {10: 0}
        inner = [pltpu.VMEM((rows, span), BF)]
        tail = [pltpu.SemaphoreType.DMA((1,))]
        more = []
    return pl.pallas_call(
        functools.partial(kernel, spans=spans, tile=tile),
        in_specs=specs,
        out_specs=[ANY, VM] + [VM] * len(more),
        out_shape=(pltpu.HBM((pts, lat), BF), pltpu.VMEM((nodes, lat), F32), *more),
        scratch_shapes=[
            pltpu.VMEM((nodes, wide), BF),
            pltpu.VMEM((wide, lat), BF),
            pltpu.VMEM((span, lat), BF),
            *inner,
            pltpu.SemaphoreType.DMA((span // tile,)),
            pltpu.SemaphoreType.DMA((len(spans),)),
            *tail,
        ],
        input_output_aliases=alias,
        compiler_params=params(24),
        cost_estimate=cost(2 * span * lat * (rows + 2 * lat + nodes), span * (rows + lat) * 2),
        name="embed",
    )(*args)


def node_kernel(r_ref, w_in, b_in, w_out, w_msg, b_msg, sum_ref, *rest, pad):
    sources, o_ref, buffers, sem = rest[:5], rest[5], rest[6:11], rest[11]
    loads = [pltpu.make_async_copy(f, t, sem.at[k]) for k, (f, t) in enumerate(zip(sources, buffers))]
    for c in loads:
        c.start()
    w_mo, w_nb, pre_ref, w_no, mesh_ref = buffers
    nodes = sum_ref.shape[0]
    rows = r_ref[...]
    _, act = act_of(rows, (((1,), (0,)), ((), ())), w_in, b_in, w_out, w_msg, b_msg)
    lane = lax.broadcasted_iota(jnp.int32, (8, rows.shape[1]), 1)
    pick = jnp.where(lane == pad, 16.0, jnp.where(lane == 2 * pad + 1, 1.0, 0.0)).astype(BF)
    dst = dot(pick, rows, NT)[:1].astype(jnp.int32) - 1
    ids = lax.broadcasted_iota(jnp.int32, (nodes, rows.shape[0]), 0)
    total = sum_ref[...] + dot(hot(ids, dst), act)
    high = total.astype(BF)
    low = (total - high.astype(F32)).astype(BF)
    for c in loads:
        c.wait()
    summed = (dot(high, w_mo[...]) + dot(low, w_mo[...])).astype(BF)
    node = silu2(pre_ref[...] + dot(summed, w_nb[...]))
    o_ref[...] = (mesh_ref[...].astype(F32) + dot(node, w_no[...])).astype(BF)


def node_update(rows, weights, total, w_mo, mesh, pre, w_nb, w_no, pad):
    args = at_vmem(rows, *weights, total)
    later = [at_hbm(a) for a in (w_mo, w_nb, pre, w_no, mesh)]
    slots = rows.shape[0]
    lat = mesh.shape[1]
    return pl.pallas_call(
        functools.partial(node_kernel, pad=pad),
        in_specs=[VM] * len(args) + [ANY] * len(later),
        out_specs=VM,
        out_shape=jax.ShapeDtypeStruct(mesh.shape, BF),
        scratch_shapes=[pltpu.VMEM(a.shape, a.dtype) for a in later]
        + [pltpu.SemaphoreType.DMA((len(later),))],
        compiler_params=params(20),
        cost_estimate=cost(6 * slots * lat * lat, 6 * lat * lat * 2),
        name="node",
    )(*args, *later)


def shards(
    fields,
    chan_mean,
    chan_scale,
    w_embed_in,
    b_embed,
    w_embed_out,
    halo_index,
    local_src,
    local_dst,
    remote_src,
    remote_dst,
    w_msg_in,
    b_msg,
    w_msg_out,
    mesh_nodes,
    w_node_in,
    b_node,
    w_node_out,
):
    levels = lax.axis_size("lev")
    tiles = lax.axis_size("tile")
    chans, points = fields.shape
    pts = points // levels
    slot_count = remote_src.shape[2]
    halo = halo_index.shape[2]
    table = pts + 2 * halo
    wide = (chans + 1) * levels

    me = lax.axis_index("lev").astype(jnp.int32).reshape(1)
    sent = pack(me, chan_mean, chan_scale, fields, levels)
    got = lax.all_to_all(sent, "lev", split_axis=0, concat_axis=0, tiled=True)
    main = pts // (chans + 1) * chans
    x = got.reshape(wide, main)

    counts, w_in, pre, w_out, w_msg, b_in, b_out, w_nb = count_edges(
        local_src,
        local_dst,
        w_embed_in,
        b_embed[None, :],
        mesh_nodes,
        b_node[None, :],
        b_msg[None, :],
        w_node_in,
        w_embed_out,
        w_msg_in,
        table,
        wide,
        chans,
    )
    weights = [w_in, b_in, w_out, w_msg, b_out]

    src = remote_src.reshape(1, -1)
    dst = remote_dst.reshape(1, -1)
    low, high, kept = select(x, halo_index.reshape(1, 2 * halo), chans)
    ahead = [(i, (i + 1) % tiles) for i in range(tiles)]
    back = [(t, s) for s, t in ahead]
    from_low = lax.ppermute(high, "tile", ahead)
    from_up = lax.ppermute(low, "tile", back)

    tile = 512
    cut = CUT * tile
    latent, total, own = embed(
        kept, counts, weights, pts, ((0, cut), (main, pts - main)), tile, src
    )

    rows = slots_rows(own, from_low, from_up, src, dst, pts, chans)
    rows = lax.all_to_all(
        rows.reshape(levels, slot_count, wide), "lev", split_axis=0, concat_axis=0, tiled=True
    ).reshape(levels * slot_count, wide)

    latent, total = embed(
        x,
        counts,
        weights,
        pts,
        ((cut, main - cut), (pts, 2 * halo)),
        tile,
        before=(latent, total, from_low, from_up),
    )
    mesh_out = node_update(
        rows, weights, total, w_msg_out, mesh_nodes, pre, w_nb, w_node_out, chans
    )
    return (latent, mesh_out)


def solution(mesh):
    return jax.shard_map(
        shards,
        mesh=mesh,
        in_specs=(
            P("lev", "tile"),
            P(),
            P(),
            P(),
            P(),
            P(),
            P(("tile", "lev"), None, None),
            P(("tile", "lev"), None),
            P(("tile", "lev"), None),
            P(("tile", "lev"), None, None),
            P(("tile", "lev"), None, None),
            P(),
            P(),
            P(),
            P(("tile", "lev"), None),
            P(),
            P(),
            P(),
        ),
        out_specs=(P(("tile", "lev"), None), P(("tile", "lev"), None)),
        check_vma=False,
    )
```

```python
import functools

import jax
import jax.numpy as jnp
from jax import lax
from jax.experimental import pallas as pl
from jax.experimental.pallas import tpu as pltpu
from jax.sharding import PartitionSpec as P

BF = jnp.bfloat16
F32 = jnp.float32
NT = (((1,), (1,)), ((), ()))
TN = (((0,), (0,)), ((), ()))
PIECE = 512
MIB = 1024 * 1024


def params(mib, **kw):
    return pltpu.CompilerParams(vmem_limit_bytes=mib * MIB, **kw)


def whole(shape):
    return pl.BlockSpec(shape, lambda *_: (0,) * len(shape))


def cost(flops, nbytes):
    return pl.CostEstimate(flops=int(flops), bytes_accessed=int(nbytes), transcendentals=0)


def dot(a, b, dims=(((1,), (0,)), ((), ()))):
    return lax.dot_general(a, b, dims, preferred_element_type=F32)


def silu2(h):
    return (h + h * jnp.tanh(h)).astype(BF)


def hot(ids, index, value=1.0):
    return jnp.where(ids == index, jnp.asarray(value, BF), jnp.asarray(0.0, BF))


def at_vmem(*arrays):
    return [pltpu.with_memory_space_constraint(a, pltpu.VMEM) for a in arrays]


def at_hbm(array):
    return pltpu.with_memory_space_constraint(array, pltpu.HBM)


VM = pl.BlockSpec(memory_space=pltpu.VMEM)
ANY = pl.BlockSpec(memory_space=pl.ANY)


def pack_kernel(me_ref, mean_ref, scale_ref, x_ref, o_ref, in_buf, out_buf, in_sem, out_sem, *, parts):
    chans, points = in_buf.shape
    levels, _, main = out_buf.shape
    pts = points // levels
    per = levels // parts
    width = per * pts

    def load(k):
        at = pl.ds(k * width, width)
        return pltpu.make_async_copy(x_ref.at[:, at], in_buf.at[:, at], in_sem.at[k])

    def store(k):
        at = pl.ds(k * per, per)
        return pltpu.make_async_copy(out_buf.at[at], o_ref.at[at], out_sem.at[k])

    for k in range(parts):
        load(k).start()
    base = me_ref[0] * chans
    row = lax.broadcasted_iota(jnp.int32, (chans, 1), 0)
    mean = jnp.zeros((chans, 1), F32)
    scale = jnp.zeros((chans, 1), F32)
    for c in range(chans):
        mean = jnp.where(row == c, mean_ref[base + c], mean)
        scale = jnp.where(row == c, scale_ref[base + c], scale)
    for k in range(parts):
        load(k).wait()
        for j in range(k * per, (k + 1) * per):
            val = (in_buf[:, j * pts : (j + 1) * pts] - mean) * scale
            last = jnp.concatenate([val[c : c + 1, main:] for c in range(chans)], axis=1)
            out_buf[j] = jnp.concatenate([val[:, :main], last], axis=0).astype(BF)
        store(k).start()
    for k in range(parts):
        store(k).wait()


def pack(me, mean, scale, fields, levels):
    chans, points = fields.shape
    pts = points // levels
    parts = 8
    smem = pl.BlockSpec(memory_space=pltpu.SMEM)
    shape = (levels, chans + 1, pts * chans // (chans + 1))
    return pl.pallas_call(
        functools.partial(pack_kernel, parts=parts),
        in_specs=[smem, smem, smem, pl.BlockSpec(memory_space=pl.ANY)],
        out_specs=pl.BlockSpec(memory_space=pl.ANY),
        out_shape=jax.ShapeDtypeStruct(shape, BF),
        scratch_shapes=[
            pltpu.VMEM(fields.shape, F32),
            pltpu.VMEM(shape, BF),
            pltpu.SemaphoreType.DMA((parts,)),
            pltpu.SemaphoreType.DMA((parts,)),
        ],
        compiler_params=params(60),
        cost_estimate=cost(points * 16, points * 48),
        name="pack",
    )(me, mean, scale, fields)


def count_kernel(
    src_ref, dst_ref, w_ref, b_ref, mesh_ref, b_n, b_m, w_node, w_out, w_msg,
    o_ref, w_in_ref, pre_ref, msg_ref, both_ref, bi_ref, bm_ref, nb_ref, hot_ref, na_ref, out_ref, sem, *, chans,
):
    nodes, edges = hot_ref.shape
    lat = w_out.shape[0]
    tile = 512
    chunk = 1024
    pairs = (
        (w_node.at[pl.ds(0, lat)], na_ref),
        (w_node.at[pl.ds(lat, lat)], nb_ref),
        (w_out, out_ref),
        (w_msg, msg_ref),
    )
    copies = [pltpu.make_async_copy(f, t, sem.at[k]) for k, (f, t) in enumerate(pairs)]
    for c in copies:
        c.start()
    ids = lax.broadcasted_iota(jnp.int32, (nodes, edges), 0).astype(jnp.int16)
    hot_ref[...] = hot(ids, dst_ref[...].astype(jnp.int16))
    shape = (w_in_ref.shape[0], w_ref.shape[0])
    row = lax.broadcasted_iota(jnp.int32, shape, 0)
    col = lax.broadcasted_iota(jnp.int32, shape, 1)
    lane = row % (chans + 1)
    place = jnp.where(lane < chans, row // (chans + 1) * chans + lane, -1)
    w_in_ref[...] = dot(hot(col, place, 0.5), w_ref[...]).astype(BF)
    bi_ref[...] = 0.5 * b_ref[...]
    bm_ref[...] = 0.5 * b_m[...]

    @pl.loop(0, o_ref.shape[1] // tile)
    def _(i):
        start = pl.multiple_of(i * tile, tile)
        rows = lax.broadcasted_iota(jnp.int32, (tile, chunk), 0).astype(jnp.int16)
        acc = jnp.zeros((nodes, tile), F32)
        for c in range(edges // chunk):
            at = slice(c * chunk, (c + 1) * chunk)
            acc = acc + dot(hot_ref[:, at], hot(rows, (src_ref[:, at] - start).astype(jnp.int16)), NT)
        o_ref[:, pl.ds(start, tile)] = acc.astype(BF)

    for c in copies:
        c.wait()
    msg_ref[...] = msg_ref[...] * 0.5
    both_ref[...] = dot(out_ref[...], msg_ref[...]).astype(BF)
    nb_ref[...] = nb_ref[...] * 0.5
    pre_ref[...] = 0.5 * (dot(mesh_ref[...], na_ref[...]) + b_n[...])


def count_edges(src, dst, w_in, b_in, mesh, b_node, b_msg, w_node, w_out, w_msg, table, wide, chans):
    edges = src.shape[1]
    nodes, lat = mesh.shape
    square = pltpu.VMEM((lat, lat), BF)
    return pl.pallas_call(
        functools.partial(count_kernel, chans=chans),
        in_specs=[VM] * 7 + [ANY] * 3,
        out_specs=[VM] * 8,
        out_shape=(
            pltpu.HBM((nodes, table), BF),
            pltpu.VMEM((wide, lat), BF),
            pltpu.HBM((nodes, lat), F32),
            pltpu.HBM((lat, lat), BF),
            square,
            pltpu.VMEM((1, lat), F32),
            pltpu.VMEM((1, lat), F32),
            pltpu.HBM((lat, lat), BF),
        ),
        scratch_shapes=[
            pltpu.VMEM((nodes, edges), BF),
            pltpu.VMEM((lat, lat), BF),
            pltpu.VMEM((lat, lat), BF),
            pltpu.SemaphoreType.DMA((4,)),
        ],
        compiler_params=params(24),
        cost_estimate=cost(2 * nodes * edges * table, nodes * table * 2),
        name="count",
    )(src, dst, w_in, b_in, mesh, b_node, b_msg, *map(at_hbm, (w_node, w_out, w_msg)))


def hots(index, ref):
    step = 1024
    ids = lax.broadcasted_iota(jnp.int32, (step, ref.shape[1]), 0).astype(jnp.int16)
    for start in range(0, ref.shape[0], step):
        ref[pl.ds(start, step)] = hot(ids, (index - start).astype(jnp.int16))


def select_kernel(x_ref, idx_ref, low_ref, high_ref, tail_ref, near_hot, *, chans):
    rows, main = x_ref.shape
    half = low_ref.shape[1]
    last = main // chans
    group = chans + 1
    hots(idx_ref[...], near_hot)
    near = dot(x_ref[...], near_hot[:main])
    row = lax.broadcasted_iota(jnp.int32, (1, group, 1), 1)
    tail = jnp.zeros((rows // group, group, last), F32)
    for c in range(chans):
        part = x_ref[:, c * last : (c + 1) * last].astype(F32).reshape(rows // group, group, last)
        tail = jnp.where(row == c, part[:, chans:], tail)
    tail = tail.reshape(rows, last).astype(BF)
    tail_ref[...] = tail
    near = near + dot(tail, near_hot[main:])
    low_ref[...] = near[:, :half].astype(BF)
    high_ref[...] = near[:, half:].astype(BF)


def select(x, idx, chans):
    rows, main = x.shape
    last = main // chans
    pts = main + last
    half = idx.shape[1] // 2
    out = jax.ShapeDtypeStruct((rows, half), BF)
    return pl.pallas_call(
        functools.partial(select_kernel, chans=chans),
        in_specs=[VM, VM],
        out_specs=[VM] * 3,
        out_shape=(out, out, pltpu.VMEM((rows, last), BF)),
        scratch_shapes=[pltpu.VMEM((pts, 2 * half), BF)],
        compiler_params=params(24),
        cost_estimate=cost(4 * rows * pts * half, rows * pts * 2),
        name="select",
    )(*at_vmem(x), idx)


def slots_kernel(own_ref, low_ref, up_ref, src_ref, dst_ref, o_ref, *, start, pad):
    half = low_ref.shape[1]
    shape = (half, own_ref.shape[1])
    ids = lax.broadcasted_iota(jnp.int32, shape, 0) + start
    acc = own_ref[...].astype(F32)
    acc = acc + dot(low_ref[...], hot(ids, src_ref[...]))
    acc = acc + dot(up_ref[...], hot(ids + half, src_ref[...]))
    code = dst_ref[...] + 1
    row = lax.broadcasted_iota(jnp.int32, acc.shape, 0)
    acc = jnp.where(row == pad, (code // 16).astype(F32), acc)
    acc = jnp.where(row == 2 * pad + 1, (code % 16).astype(F32), acc)
    o_ref[...] = acc.T.astype(BF)


def slots_rows(own, low, up, src, dst, start, pad):
    rows, slots = own.shape
    return pl.pallas_call(
        functools.partial(slots_kernel, start=start, pad=pad),
        in_specs=[VM] * 5,
        out_shape=jax.ShapeDtypeStruct((slots, rows), BF),
        compiler_params=params(16),
        cost_estimate=cost(4 * rows * low.shape[1] * slots, slots * rows * 4),
        name="slots",
    )(*at_vmem(own, low, up), src, dst)


def act_of(x, dims, w_in, b_in, w_out, w_msg, b_msg):
    hidden = silu2(dot(x, w_in[...], dims) + b_in[...])
    latent = dot(hidden, w_out[...]).astype(BF)
    return latent, silu2(dot(latent, w_msg[...]) + b_msg[...])


def act_only(x, dims, w_in, b_in, w_both, b_msg):
    hidden = silu2(dot(x, w_in[...], dims) + b_in[...])
    return silu2(dot(hidden, w_both[...]) + b_msg[...])


def columns(src, dst, sem, spans):
    copies = []
    at = 0
    for k, (start, width) in enumerate(spans):
        copies.append(
            pltpu.make_async_copy(
                src.at[:, pl.ds(start, width)], dst.at[:, pl.ds(at, width)], sem.at[k]
            )
        )
        copies[-1].start()
        at += width
    return copies


def embed_tile(x, weights, lat_hbm, act_ref, buf, sem, row, pieces):
    latent, act = act_of(x, TN, *weights)
    rows = pl.ds(row, x.shape[1])
    buf[rows] = latent
    act_ref[rows] = act
    stores = []
    for point, width in pieces:
        stores.append(
            pltpu.make_async_copy(
                buf.at[pl.ds(row, width)], lat_hbm.at[pl.ds(point, width)], sem.at[row // PIECE]
            )
        )
        stores[-1].start()
        row += width
    return stores


def whole_copies(pairs, sem):
    copies = [pltpu.make_async_copy(f, t, sem.at[k]) for k, (f, t) in enumerate(pairs)]
    for c in copies:
        c.start()
    return copies


def first_kernel(
    x_ref, tail_ref, src_ref, w_in, b_in, b_msg, w_out_hbm, w_msg_hbm, s_hbm, lat_ref, sum_ref, own_ref,
    s_buf, act_buf, buf, w_out, w_msg, far_hot, sem, in_sem, w_sem, *, spans,
):
    w_loads = whole_copies(((w_out_hbm, w_out), (w_msg_hbm, w_msg)), w_sem)
    loads = columns(s_hbm, s_buf, in_sem, spans)
    hots(src_ref[...], far_hot)
    main = x_ref.shape[1]
    far = dot(x_ref[...], far_hot[:main]) + dot(tail_ref[...], far_hot[main:])
    own_ref[...] = far.astype(BF)
    x = jnp.concatenate([x_ref[:, : spans[0][1]], tail_ref[...]], axis=1)
    for c in w_loads:
        c.wait()
    stores = embed_tile(x, (w_in, b_in, w_out, w_msg, b_msg), lat_ref, act_buf, buf, sem, 0, spans)
    for c in loads:
        c.wait()
    sum_ref[...] = dot(s_buf[...], act_buf[...])
    for c in stores:
        c.wait()


def second_kernel(
    low_ref, up_ref, w_both, w_in, b_in, b_msg, w_out_hbm, w_msg_hbm, s_hbm, before, x_hbm, _, lat_ref, sum_ref,
    s_buf, act_buf, buf, w_out, w_msg, x_buf, sem, in_sem, w_sem, x_sem, *, spans, tile,
):
    half = low_ref.shape[1]
    x_load = columns(x_hbm, x_buf, x_sem, spans[:1])
    w_loads = whole_copies(((w_out_hbm, w_out), (w_msg_hbm, w_msg), (before, sum_ref)), w_sem)
    loads = columns(s_hbm, s_buf, in_sem, spans)
    start, width = spans[0]
    halo = jnp.concatenate([low_ref[...], up_ref[...]], axis=1)
    act_buf[pl.ds(width, 2 * half)] = act_only(halo, TN, w_in, b_in, w_both, b_msg)
    x_load[0].wait()
    for c in w_loads:
        c.wait()
    weights = (w_in, b_in, w_out, w_msg, b_msg)
    stores = []
    for p in range(0, width, tile):
        stores += embed_tile(
            x_buf[:, p : p + tile], weights, lat_ref, act_buf, buf, sem, p, [(start + p, tile)]
        )
    for c in loads:
        c.wait()
    sum_ref[...] += dot(s_buf[...], act_buf[...])
    for c in stores:
        c.wait()


def embed(x, counts, weights, later, pts, spans, tile, tail=None, src=None, before=None):
    rows = x.shape[0]
    nodes = counts.shape[0]
    w_in, b_in, w_both, b_msg = weights
    lat = w_in.shape[1]
    wide = sum(width for _, width in spans)
    held = at_vmem(w_in, b_in, b_msg)
    remote = [at_hbm(a) for a in (*later, counts)]
    if before is None:
        kernel = functools.partial(first_kernel, spans=spans)
        span = wide
        args = [*at_vmem(x, tail), src, *held, *remote]
        specs = [VM] * 6 + [ANY] * 3
        alias = {}
        inner = [pltpu.VMEM((pts, src.shape[1]), BF)]
        sems = []
        more = [pltpu.VMEM((rows, src.shape[1]), BF)]
    else:
        kernel = functools.partial(second_kernel, spans=spans, tile=tile)
        span = spans[0][1]
        latent, total, low, up = before
        args = [*at_vmem(low, up, w_both), *held, *remote, at_hbm(total), at_hbm(x), at_hbm(latent)]
        specs = [VM] * 6 + [ANY] * 6
        alias = {11: 0}
        inner = [pltpu.VMEM((rows, span), BF)]
        sems = [pltpu.SemaphoreType.DMA((1,))]
        more = []
    return pl.pallas_call(
        kernel,
        in_specs=specs,
        out_specs=[ANY, VM] + [VM] * len(more),
        out_shape=(pltpu.HBM((pts, lat), BF), pltpu.VMEM((nodes, lat), F32), *more),
        scratch_shapes=[
            pltpu.VMEM((nodes, wide), BF),
            pltpu.VMEM((wide, lat), BF),
            pltpu.VMEM((span, lat), BF),
            pltpu.VMEM((lat, lat), BF),
            pltpu.VMEM((lat, lat), BF),
            *inner,
            pltpu.SemaphoreType.DMA((span // PIECE,)),
            pltpu.SemaphoreType.DMA((len(spans),)),
            pltpu.SemaphoreType.DMA((3,)),
            *sems,
        ],
        input_output_aliases=alias,
        compiler_params=params(28),
        cost_estimate=cost(2 * span * lat * (rows + 2 * lat + nodes), span * (rows + lat) * 2),
        name="embed",
    )(*args)


def node_kernel(r_ref, w_in, b_in, w_both, b_msg, sum_ref, *rest, pad):
    sources, o_ref, buffers, sem = rest[:5], rest[5], rest[6:11], rest[11]
    loads = [pltpu.make_async_copy(f, t, sem.at[k]) for k, (f, t) in enumerate(zip(sources, buffers))]
    for c in loads:
        c.start()
    w_mo, w_nb, pre_ref, w_no, mesh_ref = buffers
    nodes = sum_ref.shape[0]
    rows = r_ref[...]
    act = act_only(rows, (((1,), (0,)), ((), ())), w_in, b_in, w_both, b_msg)
    lane = lax.broadcasted_iota(jnp.int32, (8, rows.shape[1]), 1)
    pick = jnp.where(lane == pad, 16.0, jnp.where(lane == 2 * pad + 1, 1.0, 0.0)).astype(BF)
    dst = dot(pick, rows, NT)[:1].astype(jnp.int32) - 1
    ids = lax.broadcasted_iota(jnp.int32, (nodes, rows.shape[0]), 0)
    total = sum_ref[...] + dot(hot(ids, dst), act)
    for c in loads:
        c.wait()
    summed = dot(total.astype(BF), w_mo[...]).astype(BF)
    node = silu2(pre_ref[...] + dot(summed, w_nb[...]))
    o_ref[...] = (mesh_ref[...].astype(F32) + dot(node, w_no[...])).astype(BF)


def node_update(rows, weights, total, w_mo, mesh, pre, w_nb, w_no, pad):
    args = at_vmem(rows, *weights, total)
    later = [at_hbm(a) for a in (w_mo, w_nb, pre, w_no, mesh)]
    slots = rows.shape[0]
    lat = mesh.shape[1]
    return pl.pallas_call(
        functools.partial(node_kernel, pad=pad),
        in_specs=[VM] * len(args) + [ANY] * len(later),
        out_specs=VM,
        out_shape=jax.ShapeDtypeStruct(mesh.shape, BF),
        scratch_shapes=[pltpu.VMEM(a.shape, a.dtype) for a in later]
        + [pltpu.SemaphoreType.DMA((len(later),))],
        compiler_params=params(20),
        cost_estimate=cost(6 * slots * lat * lat, 6 * lat * lat * 2),
        name="node",
    )(*args, *later)


def shards(
    fields,
    chan_mean,
    chan_scale,
    w_embed_in,
    b_embed,
    w_embed_out,
    halo_index,
    local_src,
    local_dst,
    remote_src,
    remote_dst,
    w_msg_in,
    b_msg,
    w_msg_out,
    mesh_nodes,
    w_node_in,
    b_node,
    w_node_out,
):
    levels = lax.axis_size("lev")
    tiles = lax.axis_size("tile")
    chans, points = fields.shape
    pts = points // levels
    slot_count = remote_src.shape[2]
    halo = halo_index.shape[2]
    table = pts + 2 * halo
    wide = (chans + 1) * levels

    me = lax.axis_index("lev").astype(jnp.int32).reshape(1)
    sent = pack(me, chan_mean, chan_scale, fields, levels)
    got = lax.all_to_all(sent, "lev", split_axis=0, concat_axis=0, tiled=True)
    main = pts // (chans + 1) * chans
    x = got.reshape(wide, main)

    counts, w_in, pre, w_msg, w_both, b_in, b_out, w_nb = count_edges(
        local_src,
        local_dst,
        w_embed_in,
        b_embed[None, :],
        mesh_nodes,
        b_node[None, :],
        b_msg[None, :],
        w_node_in,
        w_embed_out,
        w_msg_in,
        table,
        wide,
        chans,
    )
    weights = [w_in, b_in, w_both, b_out]
    later = [w_embed_out, w_msg]

    src = remote_src.reshape(1, -1)
    dst = remote_dst.reshape(1, -1)
    low, high, tail = select(x, halo_index.reshape(1, 2 * halo), chans)
    ahead = [(i, (i + 1) % tiles) for i in range(tiles)]
    back = [(t, s) for s, t in ahead]
    from_low = lax.ppermute(high, "tile", ahead)
    from_up = lax.ppermute(low, "tile", back)

    tile = 2 * PIECE
    cut = PIECE
    latent, total, own = embed(
        x, counts, weights, later, pts, ((0, cut), (main, pts - main)), tile, tail, src
    )

    rows = slots_rows(own, from_low, from_up, src, dst, pts, chans)
    rows = lax.all_to_all(
        rows.reshape(levels, slot_count, wide), "lev", split_axis=0, concat_axis=0, tiled=True
    ).reshape(levels * slot_count, wide)

    latent, total = embed(
        x,
        counts,
        weights,
        later,
        pts,
        ((cut, main - cut), (pts, 2 * halo)),
        tile,
        before=(latent, total, from_low, from_up),
    )
    mesh_out = node_update(
        rows, weights, total, w_msg_out, mesh_nodes, pre, w_nb, w_node_out, chans
    )
    return (latent, mesh_out)


def solution(mesh):
    return jax.shard_map(
        shards,
        mesh=mesh,
        in_specs=(
            P("lev", "tile"),
            P(),
            P(),
            P(),
            P(),
            P(),
            P(("tile", "lev"), None, None),
            P(("tile", "lev"), None),
            P(("tile", "lev"), None),
            P(("tile", "lev"), None, None),
            P(("tile", "lev"), None, None),
            P(),
            P(),
            P(),
            P(("tile", "lev"), None),
            P(),
            P(),
            P(),
        ),
        out_specs=(P(("tile", "lev"), None), P(("tile", "lev"), None)),
        check_vma=False,
    )
```

```python
import functools

import jax
import jax.numpy as jnp
from jax import lax
from jax.experimental import pallas as pl
from jax.experimental.pallas import tpu as pltpu
from jax.sharding import PartitionSpec as P

BF = jnp.bfloat16
F32 = jnp.float32
NT = (((1,), (1,)), ((), ()))
TN = (((0,), (0,)), ((), ()))
PIECE = 512
MIB = 1024 * 1024


def params(mib, **kw):
    return pltpu.CompilerParams(vmem_limit_bytes=mib * MIB, **kw)


def whole(shape):
    return pl.BlockSpec(shape, lambda *_: (0,) * len(shape))


def cost(flops, nbytes):
    return pl.CostEstimate(flops=int(flops), bytes_accessed=int(nbytes), transcendentals=0)


def dot(a, b, dims=(((1,), (0,)), ((), ()))):
    return lax.dot_general(a, b, dims, preferred_element_type=F32)


def silu2(h):
    return (h + h * jnp.tanh(h)).astype(BF)


def hot(ids, index, value=1.0):
    return jnp.where(ids == index, jnp.asarray(value, BF), jnp.asarray(0.0, BF))


def at_vmem(*arrays):
    return [pltpu.with_memory_space_constraint(a, pltpu.VMEM) for a in arrays]


def at_hbm(array):
    return pltpu.with_memory_space_constraint(array, pltpu.HBM)


VM = pl.BlockSpec(memory_space=pltpu.VMEM)
ANY = pl.BlockSpec(memory_space=pl.ANY)


def pack_kernel(me_ref, mean_ref, scale_ref, x_ref, o_ref, in_buf, out_buf, in_sem, out_sem, *, parts):
    chans, points = in_buf.shape
    levels, _, main = out_buf.shape
    pts = points // levels
    per = levels // parts
    width = per * pts

    def load(k):
        at = pl.ds(k * width, width)
        return pltpu.make_async_copy(x_ref.at[:, at], in_buf.at[:, at], in_sem.at[k])

    def store(k):
        at = pl.ds(k * per, per)
        return pltpu.make_async_copy(out_buf.at[at], o_ref.at[at], out_sem.at[k])

    for k in range(parts):
        load(k).start()
    base = me_ref[0] * chans
    row = lax.broadcasted_iota(jnp.int32, (chans, 1), 0)
    mean = jnp.zeros((chans, 1), F32)
    scale = jnp.zeros((chans, 1), F32)
    for c in range(chans):
        mean = jnp.where(row == c, mean_ref[base + c], mean)
        scale = jnp.where(row == c, scale_ref[base + c], scale)
    for k in range(parts):
        load(k).wait()
        for j in range(k * per, (k + 1) * per):
            val = (in_buf[:, j * pts : (j + 1) * pts] - mean) * scale
            last = jnp.concatenate([val[c : c + 1, main:] for c in range(chans)], axis=1)
            out_buf[j] = jnp.concatenate([val[:, :main], last], axis=0).astype(BF)
        store(k).start()
    for k in range(parts):
        store(k).wait()


def pack(me, mean, scale, fields, levels):
    chans, points = fields.shape
    pts = points // levels
    parts = 16
    smem = pl.BlockSpec(memory_space=pltpu.SMEM)
    shape = (levels, chans + 1, pts * chans // (chans + 1))
    return pl.pallas_call(
        functools.partial(pack_kernel, parts=parts),
        in_specs=[smem, smem, smem, pl.BlockSpec(memory_space=pl.ANY)],
        out_specs=pl.BlockSpec(memory_space=pl.ANY),
        out_shape=jax.ShapeDtypeStruct(shape, BF),
        scratch_shapes=[
            pltpu.VMEM(fields.shape, F32),
            pltpu.VMEM(shape, BF),
            pltpu.SemaphoreType.DMA((parts,)),
            pltpu.SemaphoreType.DMA((parts,)),
        ],
        compiler_params=params(60),
        cost_estimate=cost(points * 16, points * 48),
        name="pack",
    )(me, mean, scale, fields)


def count_kernel(
    src_ref, dst_ref, w_ref, b_ref, mesh_ref, b_n, b_m, w_node, w_out, w_msg,
    o_ref, w_in_ref, pre_ref, msg_ref, both_ref, bi_ref, bm_ref, nb_ref, hot_ref, na_ref, out_ref, sem, *, chans,
):
    nodes, edges = hot_ref.shape
    lat = w_out.shape[0]
    tile = 512
    chunk = 1024
    pairs = (
        (w_node.at[pl.ds(0, lat)], na_ref),
        (w_node.at[pl.ds(lat, lat)], nb_ref),
        (w_out, out_ref),
        (w_msg, msg_ref),
    )
    copies = [pltpu.make_async_copy(f, t, sem.at[k]) for k, (f, t) in enumerate(pairs)]
    for c in copies:
        c.start()
    ids = lax.broadcasted_iota(jnp.int32, (nodes, edges), 0).astype(jnp.int16)
    hot_ref[...] = hot(ids, dst_ref[...].astype(jnp.int16))
    shape = (w_in_ref.shape[0], w_ref.shape[0])
    row = lax.broadcasted_iota(jnp.int32, shape, 0)
    col = lax.broadcasted_iota(jnp.int32, shape, 1)
    lane = row % (chans + 1)
    place = jnp.where(lane < chans, row // (chans + 1) * chans + lane, -1)
    w_in_ref[...] = dot(hot(col, place, 0.5), w_ref[...]).astype(BF)
    bi_ref[...] = 0.5 * b_ref[...]
    bm_ref[...] = 0.5 * b_m[...]

    @pl.loop(0, o_ref.shape[1] // tile)
    def _(i):
        start = pl.multiple_of(i * tile, tile)
        rows = lax.broadcasted_iota(jnp.int32, (tile, chunk), 0).astype(jnp.int16)
        acc = jnp.zeros((nodes, tile), F32)
        for c in range(edges // chunk):
            at = slice(c * chunk, (c + 1) * chunk)
            acc = acc + dot(hot_ref[:, at], hot(rows, (src_ref[:, at] - start).astype(jnp.int16)), NT)
        o_ref[:, pl.ds(start, tile)] = acc.astype(BF)

    for c in copies:
        c.wait()
    msg_ref[...] = msg_ref[...] * 0.5
    both_ref[...] = dot(out_ref[...], msg_ref[...]).astype(BF)
    nb_ref[...] = nb_ref[...] * 0.5
    pre_ref[...] = 0.5 * (dot(mesh_ref[...], na_ref[...]) + b_n[...])


def count_edges(src, dst, w_in, b_in, mesh, b_node, b_msg, w_node, w_out, w_msg, table, wide, chans):
    edges = src.shape[1]
    nodes, lat = mesh.shape
    square = pltpu.VMEM((lat, lat), BF)
    return pl.pallas_call(
        functools.partial(count_kernel, chans=chans),
        in_specs=[VM] * 7 + [ANY] * 3,
        out_specs=[VM] * 8,
        out_shape=(
            pltpu.HBM((nodes, table), BF),
            pltpu.VMEM((wide, lat), BF),
            pltpu.HBM((nodes, lat), F32),
            pltpu.HBM((lat, lat), BF),
            square,
            pltpu.VMEM((1, lat), F32),
            pltpu.VMEM((1, lat), F32),
            pltpu.HBM((lat, lat), BF),
        ),
        scratch_shapes=[
            pltpu.VMEM((nodes, edges), BF),
            pltpu.VMEM((lat, lat), BF),
            pltpu.VMEM((lat, lat), BF),
            pltpu.SemaphoreType.DMA((4,)),
        ],
        compiler_params=params(24),
        cost_estimate=cost(2 * nodes * edges * table, nodes * table * 2),
        name="count",
    )(src, dst, w_in, b_in, mesh, b_node, b_msg, *map(at_hbm, (w_node, w_out, w_msg)))


def hots(index, ref):
    step = 1024
    ids = lax.broadcasted_iota(jnp.int32, (step, ref.shape[1]), 0).astype(jnp.int16)
    for start in range(0, ref.shape[0], step):
        ref[pl.ds(start, step)] = hot(ids, (index - start).astype(jnp.int16))


def select_kernel(x_ref, idx_ref, low_ref, high_ref, tail_ref, near_hot, *, chans):
    rows, main = x_ref.shape
    half = low_ref.shape[1]
    last = main // chans
    group = chans + 1
    hots(idx_ref[...], near_hot)
    near = dot(x_ref[...], near_hot[:main])
    row = lax.broadcasted_iota(jnp.int32, (1, group, 1), 1)
    tail = jnp.zeros((rows // group, group, last), F32)
    for c in range(chans):
        part = x_ref[:, c * last : (c + 1) * last].astype(F32).reshape(rows // group, group, last)
        tail = jnp.where(row == c, part[:, chans:], tail)
    tail = tail.reshape(rows, last).astype(BF)
    tail_ref[...] = tail
    near = near + dot(tail, near_hot[main:])
    low_ref[...] = near[:, :half].astype(BF)
    high_ref[...] = near[:, half:].astype(BF)


def select(x, idx, chans):
    rows, main = x.shape
    last = main // chans
    pts = main + last
    half = idx.shape[1] // 2
    out = jax.ShapeDtypeStruct((rows, half), BF)
    return pl.pallas_call(
        functools.partial(select_kernel, chans=chans),
        in_specs=[VM, VM],
        out_specs=[VM] * 3,
        out_shape=(out, out, pltpu.VMEM((rows, last), BF)),
        scratch_shapes=[pltpu.VMEM((pts, 2 * half), BF)],
        compiler_params=params(24),
        cost_estimate=cost(4 * rows * pts * half, rows * pts * 2),
        name="select",
    )(*at_vmem(x), idx)


def slots_kernel(own_ref, low_ref, up_ref, src_ref, dst_ref, o_ref, *, start, pad):
    half = low_ref.shape[1]
    shape = (half, own_ref.shape[1])
    ids = lax.broadcasted_iota(jnp.int32, shape, 0) + start
    acc = own_ref[...].astype(F32)
    acc = acc + dot(low_ref[...], hot(ids, src_ref[...]))
    acc = acc + dot(up_ref[...], hot(ids + half, src_ref[...]))
    code = dst_ref[...] + 1
    row = lax.broadcasted_iota(jnp.int32, acc.shape, 0)
    acc = jnp.where(row == pad, (code // 16).astype(F32), acc)
    acc = jnp.where(row == 2 * pad + 1, (code % 16).astype(F32), acc)
    o_ref[...] = acc.T.astype(BF)


def slots_rows(own, low, up, src, dst, start, pad):
    rows, slots = own.shape
    return pl.pallas_call(
        functools.partial(slots_kernel, start=start, pad=pad),
        in_specs=[VM] * 5,
        out_shape=jax.ShapeDtypeStruct((slots, rows), BF),
        compiler_params=params(16),
        cost_estimate=cost(4 * rows * low.shape[1] * slots, slots * rows * 4),
        name="slots",
    )(*at_vmem(own, low, up), src, dst)


def act_of(x, dims, w_in, b_in, w_out, w_msg, b_msg):
    hidden = silu2(dot(x, w_in[...], dims) + b_in[...])
    latent = dot(hidden, w_out[...]).astype(BF)
    return latent, silu2(dot(latent, w_msg[...]) + b_msg[...])


def act_only(x, dims, w_in, b_in, w_both, b_msg):
    hidden = silu2(dot(x, w_in[...], dims) + b_in[...])
    return silu2(dot(hidden, w_both[...]) + b_msg[...])


def columns(src, dst, sem, spans):
    copies = []
    at = 0
    for k, (start, width) in enumerate(spans):
        copies.append(
            pltpu.make_async_copy(
                src.at[:, pl.ds(start, width)], dst.at[:, pl.ds(at, width)], sem.at[k]
            )
        )
        copies[-1].start()
        at += width
    return copies


def embed_tile(x, weights, lat_hbm, act_ref, buf, sem, row, point):
    latent, act = act_of(x, TN, *weights)
    rows = pl.ds(row, x.shape[1])
    buf[rows] = latent
    act_ref[rows] = act
    store = pltpu.make_async_copy(
        buf.at[rows], lat_hbm.at[pl.ds(point, x.shape[1])], sem.at[row // PIECE]
    )
    store.start()
    return [store]


def whole_copies(pairs, sem):
    copies = [pltpu.make_async_copy(f, t, sem.at[k]) for k, (f, t) in enumerate(pairs)]
    for c in copies:
        c.start()
    return copies


def first_kernel(
    x_ref, tail_ref, src_ref, w_in, b_in, b_msg, w_out_hbm, w_msg_hbm, s_hbm, lat_ref, sum_ref, own_ref,
    s_buf, act_buf, buf, w_out, w_msg, far_hot, sem, in_sem, w_sem, *, spans,
):
    w_loads = whole_copies(((w_out_hbm, w_out), (w_msg_hbm, w_msg)), w_sem)
    loads = columns(s_hbm, s_buf, in_sem, spans)
    hots(src_ref[...], far_hot)
    main = x_ref.shape[1]
    far = dot(x_ref[...], far_hot[:main]) + dot(tail_ref[...], far_hot[main:])
    own_ref[...] = far.astype(BF)
    for c in w_loads:
        c.wait()
    weights = (w_in, b_in, w_out, w_msg, b_msg)
    cut = spans[0][1]
    stores = embed_tile(x_ref[:, :cut], weights, lat_ref, act_buf, buf, sem, 0, spans[0][0])
    stores += embed_tile(tail_ref[...], weights, lat_ref, act_buf, buf, sem, cut, spans[1][0])
    for c in loads:
        c.wait()
    sum_ref[...] = dot(s_buf[...], act_buf[...])
    for c in stores:
        c.wait()


def second_kernel(
    low_ref, up_ref, w_both, w_in, b_in, b_msg, w_out_hbm, w_msg_hbm, s_hbm, before, x_hbm, _, lat_ref, sum_ref,
    s_buf, act_buf, buf, w_out, w_msg, x_buf, sem, in_sem, w_sem, x_sem, *, spans, tile,
):
    half = low_ref.shape[1]
    x_load = columns(x_hbm, x_buf, x_sem, spans[:1])
    w_loads = whole_copies(((w_out_hbm, w_out), (w_msg_hbm, w_msg), (before, sum_ref)), w_sem)
    loads = columns(s_hbm, s_buf, in_sem, spans)
    start, width = spans[0]
    halo = jnp.concatenate([low_ref[...], up_ref[...]], axis=1)
    act_buf[pl.ds(width, 2 * half)] = act_only(halo, TN, w_in, b_in, w_both, b_msg)
    x_load[0].wait()
    for c in w_loads:
        c.wait()
    weights = (w_in, b_in, w_out, w_msg, b_msg)
    stores = []
    for p in range(0, width, tile):
        x = x_buf[:, p : min(p + tile, width)]
        stores += embed_tile(x, weights, lat_ref, act_buf, buf, sem, p, start + p)
    for c in loads:
        c.wait()
    sum_ref[...] += dot(s_buf[...], act_buf[...])
    for c in stores:
        c.wait()


def embed(x, counts, weights, later, pts, spans, tile, tail=None, src=None, before=None):
    rows = x.shape[0]
    nodes = counts.shape[0]
    w_in, b_in, w_both, b_msg = weights
    lat = w_in.shape[1]
    wide = sum(width for _, width in spans)
    held = at_vmem(w_in, b_in, b_msg)
    remote = [at_hbm(a) for a in (*later, counts)]
    if before is None:
        kernel = functools.partial(first_kernel, spans=spans)
        span = wide
        args = [*at_vmem(x, tail), src, *held, *remote]
        specs = [VM] * 6 + [ANY] * 3
        alias = {}
        inner = [pltpu.VMEM((pts, src.shape[1]), BF)]
        sems = []
        more = [pltpu.VMEM((rows, src.shape[1]), BF)]
    else:
        kernel = functools.partial(second_kernel, spans=spans, tile=tile)
        span = spans[0][1]
        latent, total, low, up = before
        args = [*at_vmem(low, up, w_both), *held, *remote, at_hbm(total), at_hbm(x), at_hbm(latent)]
        specs = [VM] * 6 + [ANY] * 6
        alias = {11: 0}
        inner = [pltpu.VMEM((rows, span), BF)]
        sems = [pltpu.SemaphoreType.DMA((1,))]
        more = []
    return pl.pallas_call(
        kernel,
        in_specs=specs,
        out_specs=[ANY, VM] + [VM] * len(more),
        out_shape=(pltpu.HBM((pts, lat), BF), pltpu.VMEM((nodes, lat), F32), *more),
        scratch_shapes=[
            pltpu.VMEM((nodes, wide), BF),
            pltpu.VMEM((wide, lat), BF),
            pltpu.VMEM((span, lat), BF),
            pltpu.VMEM((lat, lat), BF),
            pltpu.VMEM((lat, lat), BF),
            *inner,
            pltpu.SemaphoreType.DMA((span // PIECE,)),
            pltpu.SemaphoreType.DMA((len(spans),)),
            pltpu.SemaphoreType.DMA((3,)),
            *sems,
        ],
        input_output_aliases=alias,
        compiler_params=params(28),
        cost_estimate=cost(2 * span * lat * (rows + 2 * lat + nodes), span * (rows + lat) * 2),
        name="embed",
    )(*args)


def node_kernel(r_ref, w_in, b_in, w_both, b_msg, sum_ref, *rest, pad):
    sources, o_ref, buffers, sem = rest[:5], rest[5], rest[6:11], rest[11]
    loads = [pltpu.make_async_copy(f, t, sem.at[k]) for k, (f, t) in enumerate(zip(sources, buffers))]
    for c in loads:
        c.start()
    w_mo, w_nb, pre_ref, w_no, mesh_ref = buffers
    nodes = sum_ref.shape[0]
    rows = r_ref[...]
    act = act_only(rows, (((1,), (0,)), ((), ())), w_in, b_in, w_both, b_msg)
    lane = lax.broadcasted_iota(jnp.int32, (8, rows.shape[1]), 1)
    pick = jnp.where(lane == pad, 16.0, jnp.where(lane == 2 * pad + 1, 1.0, 0.0)).astype(BF)
    dst = dot(pick, rows, NT)[:1].astype(jnp.int32) - 1
    ids = lax.broadcasted_iota(jnp.int32, (nodes, rows.shape[0]), 0)
    total = sum_ref[...] + dot(hot(ids, dst), act)
    high = total.astype(BF)
    low = (total - high.astype(F32)).astype(BF)
    loads[0].wait()
    summed = (dot(high, w_mo[...]) + dot(low, w_mo[...])).astype(BF)
    loads[1].wait()
    loads[2].wait()
    node = silu2(pre_ref[...] + dot(summed, w_nb[...]))
    loads[3].wait()
    loads[4].wait()
    o_ref[...] = (mesh_ref[...].astype(F32) + dot(node, w_no[...])).astype(BF)


def node_update(rows, weights, total, w_mo, mesh, pre, w_nb, w_no, pad):
    args = at_vmem(rows, *weights, total)
    later = [at_hbm(a) for a in (w_mo, w_nb, pre, w_no, mesh)]
    slots = rows.shape[0]
    lat = mesh.shape[1]
    return pl.pallas_call(
        functools.partial(node_kernel, pad=pad),
        in_specs=[VM] * len(args) + [ANY] * len(later),
        out_specs=VM,
        out_shape=jax.ShapeDtypeStruct(mesh.shape, BF),
        scratch_shapes=[pltpu.VMEM(a.shape, a.dtype) for a in later]
        + [pltpu.SemaphoreType.DMA((len(later),))],
        compiler_params=params(20),
        cost_estimate=cost(6 * slots * lat * lat, 6 * lat * lat * 2),
        name="node",
    )(*args, *later)


def shards(
    fields,
    chan_mean,
    chan_scale,
    w_embed_in,
    b_embed,
    w_embed_out,
    halo_index,
    local_src,
    local_dst,
    remote_src,
    remote_dst,
    w_msg_in,
    b_msg,
    w_msg_out,
    mesh_nodes,
    w_node_in,
    b_node,
    w_node_out,
):
    levels = lax.axis_size("lev")
    tiles = lax.axis_size("tile")
    chans, points = fields.shape
    pts = points // levels
    slot_count = remote_src.shape[2]
    halo = halo_index.shape[2]
    table = pts + 2 * halo
    wide = (chans + 1) * levels

    me = lax.axis_index("lev").astype(jnp.int32).reshape(1)
    sent = pack(me, chan_mean, chan_scale, fields, levels)
    got = lax.all_to_all(sent, "lev", split_axis=0, concat_axis=0, tiled=True)
    main = pts // (chans + 1) * chans
    x = got.reshape(wide, main)

    counts, w_in, pre, w_msg, w_both, b_in, b_out, w_nb = count_edges(
        local_src,
        local_dst,
        w_embed_in,
        b_embed[None, :],
        mesh_nodes,
        b_node[None, :],
        b_msg[None, :],
        w_node_in,
        w_embed_out,
        w_msg_in,
        table,
        wide,
        chans,
    )
    weights = [w_in, b_in, w_both, b_out]
    later = [w_embed_out, w_msg]

    src = remote_src.reshape(1, -1)
    dst = remote_dst.reshape(1, -1)
    low, high, tail = select(x, halo_index.reshape(1, 2 * halo), chans)
    ahead = [(i, (i + 1) % tiles) for i in range(tiles)]
    back = [(t, s) for s, t in ahead]
    from_low = lax.ppermute(high, "tile", ahead)
    from_up = lax.ppermute(low, "tile", back)

    tile = 2 * PIECE
    cut = tile
    latent, total, own = embed(
        x, counts, weights, later, pts, ((0, cut), (main, pts - main)), tile, tail, src
    )

    rows = slots_rows(own, from_low, from_up, src, dst, pts, chans)
    rows = lax.all_to_all(
        rows.reshape(levels, slot_count, wide), "lev", split_axis=0, concat_axis=0, tiled=True
    ).reshape(levels * slot_count, wide)

    latent, total = embed(
        x,
        counts,
        weights,
        later,
        pts,
        ((cut, main - cut), (pts, 2 * halo)),
        tile,
        before=(latent, total, from_low, from_up),
    )
    mesh_out = node_update(
        rows, weights, total, w_msg_out, mesh_nodes, pre, w_nb, w_node_out, chans
    )
    return (latent, mesh_out)


def solution(mesh):
    return jax.shard_map(
        shards,
        mesh=mesh,
        in_specs=(
            P("lev", "tile"),
            P(),
            P(),
            P(),
            P(),
            P(),
            P(("tile", "lev"), None, None),
            P(("tile", "lev"), None),
            P(("tile", "lev"), None),
            P(("tile", "lev"), None, None),
            P(("tile", "lev"), None, None),
            P(),
            P(),
            P(),
            P(("tile", "lev"), None),
            P(),
            P(),
            P(),
        ),
        out_specs=(P(("tile", "lev"), None), P(("tile", "lev"), None)),
        check_vma=False,
    )
```

```python
import functools

import jax
import jax.numpy as jnp
from jax import lax
from jax.experimental import pallas as pl
from jax.experimental.pallas import tpu as pltpu
from jax.sharding import PartitionSpec as P

BF = jnp.bfloat16
F32 = jnp.float32
NT = (((1,), (1,)), ((), ()))
TN = (((0,), (0,)), ((), ()))
PIECE = 512
MIB = 1024 * 1024


def params(mib, **kw):
    return pltpu.CompilerParams(vmem_limit_bytes=mib * MIB, **kw)


def whole(shape):
    return pl.BlockSpec(shape, lambda *_: (0,) * len(shape))


def cost(flops, nbytes):
    return pl.CostEstimate(flops=int(flops), bytes_accessed=int(nbytes), transcendentals=0)


def dot(a, b, dims=(((1,), (0,)), ((), ()))):
    return lax.dot_general(a, b, dims, preferred_element_type=F32)


def silu2(h):
    return (h + h * jnp.tanh(h)).astype(BF)


def hot(ids, index, value=1.0):
    return jnp.where(ids == index, jnp.asarray(value, BF), jnp.asarray(0.0, BF))


def at_vmem(*arrays):
    return [pltpu.with_memory_space_constraint(a, pltpu.VMEM) for a in arrays]


def at_hbm(array):
    return pltpu.with_memory_space_constraint(array, pltpu.HBM)


VM = pl.BlockSpec(memory_space=pltpu.VMEM)
ANY = pl.BlockSpec(memory_space=pl.ANY)


def pack_kernel(me_ref, mean_ref, scale_ref, x_ref, o_ref, in_buf, out_buf, in_sem, out_sem, *, parts):
    chans, points = in_buf.shape
    levels, _, main = out_buf.shape
    pts = points // levels
    per = levels // parts
    width = per * pts

    def load(k):
        at = pl.ds(k * width, width)
        return pltpu.make_async_copy(x_ref.at[:, at], in_buf.at[:, at], in_sem.at[k])

    def store(k):
        at = pl.ds(k * per, per)
        return pltpu.make_async_copy(out_buf.at[at], o_ref.at[at], out_sem.at[k])

    for k in range(parts):
        load(k).start()
    base = me_ref[0] * chans
    row = lax.broadcasted_iota(jnp.int32, (chans, 1), 0)
    mean = jnp.zeros((chans, 1), F32)
    scale = jnp.zeros((chans, 1), F32)
    for c in range(chans):
        mean = jnp.where(row == c, mean_ref[base + c], mean)
        scale = jnp.where(row == c, scale_ref[base + c], scale)
    for k in range(parts):
        load(k).wait()
        for j in range(k * per, (k + 1) * per):
            val = (in_buf[:, j * pts : (j + 1) * pts] - mean) * scale
            last = jnp.concatenate([val[c : c + 1, main:] for c in range(chans)], axis=1)
            out_buf[j] = jnp.concatenate([val[:, :main], last], axis=0).astype(BF)
        store(k).start()
    for k in range(parts):
        store(k).wait()


def pack(me, mean, scale, fields, levels):
    chans, points = fields.shape
    pts = points // levels
    parts = 8
    smem = pl.BlockSpec(memory_space=pltpu.SMEM)
    shape = (levels, chans + 1, pts * chans // (chans + 1))
    return pl.pallas_call(
        functools.partial(pack_kernel, parts=parts),
        in_specs=[smem, smem, smem, pl.BlockSpec(memory_space=pl.ANY)],
        out_specs=pl.BlockSpec(memory_space=pl.ANY),
        out_shape=jax.ShapeDtypeStruct(shape, BF),
        scratch_shapes=[
            pltpu.VMEM(fields.shape, F32),
            pltpu.VMEM(shape, BF),
            pltpu.SemaphoreType.DMA((parts,)),
            pltpu.SemaphoreType.DMA((parts,)),
        ],
        compiler_params=params(60),
        cost_estimate=cost(points * 16, points * 48),
        name="pack",
    )(me, mean, scale, fields)


def count_kernel(
    src_ref, dst_ref, w_ref, b_ref, mesh_ref, b_n, b_m, w_node, w_out, w_msg,
    o_ref, w_in_ref, pre_ref, msg_ref, both_ref, bi_ref, bm_ref, nb_ref, hot_ref, na_ref, out_ref, sem, *, chans,
):
    nodes, edges = hot_ref.shape
    lat = w_out.shape[0]
    tile = 512
    chunk = 1024
    pairs = (
        (w_node.at[pl.ds(0, lat)], na_ref),
        (w_node.at[pl.ds(lat, lat)], nb_ref),
        (w_out, out_ref),
        (w_msg, msg_ref),
    )
    copies = [pltpu.make_async_copy(f, t, sem.at[k]) for k, (f, t) in enumerate(pairs)]
    for c in copies:
        c.start()
    ids = lax.broadcasted_iota(jnp.int32, (nodes, edges), 0).astype(jnp.int16)
    hot_ref[...] = hot(ids, dst_ref[...].astype(jnp.int16))
    shape = (w_in_ref.shape[0], w_ref.shape[0])
    row = lax.broadcasted_iota(jnp.int32, shape, 0)
    col = lax.broadcasted_iota(jnp.int32, shape, 1)
    lane = row % (chans + 1)
    place = jnp.where(lane < chans, row // (chans + 1) * chans + lane, -1)
    w_in_ref[...] = dot(hot(col, place, 0.5), w_ref[...]).astype(BF)
    bi_ref[...] = 0.5 * b_ref[...]
    bm_ref[...] = 0.5 * b_m[...]

    @pl.loop(0, o_ref.shape[1] // tile)
    def _(i):
        start = pl.multiple_of(i * tile, tile)
        rows = lax.broadcasted_iota(jnp.int32, (tile, chunk), 0).astype(jnp.int16)
        acc = jnp.zeros((nodes, tile), F32)
        for c in range(edges // chunk):
            at = slice(c * chunk, (c + 1) * chunk)
            acc = acc + dot(hot_ref[:, at], hot(rows, (src_ref[:, at] - start).astype(jnp.int16)), NT)
        o_ref[:, pl.ds(start, tile)] = acc.astype(BF)

    for c in copies:
        c.wait()
    msg_ref[...] = msg_ref[...] * 0.5
    both_ref[...] = dot(out_ref[...], msg_ref[...]).astype(BF)
    nb_ref[...] = nb_ref[...] * 0.5
    pre_ref[...] = 0.5 * (dot(mesh_ref[...], na_ref[...]) + b_n[...])


def count_edges(src, dst, w_in, b_in, mesh, b_node, b_msg, w_node, w_out, w_msg, table, wide, chans):
    edges = src.shape[1]
    nodes, lat = mesh.shape
    square = pltpu.VMEM((lat, lat), BF)
    return pl.pallas_call(
        functools.partial(count_kernel, chans=chans),
        in_specs=[VM] * 7 + [ANY] * 3,
        out_specs=[VM] * 8,
        out_shape=(
            pltpu.HBM((nodes, table), BF),
            pltpu.VMEM((wide, lat), BF),
            pltpu.HBM((nodes, lat), F32),
            pltpu.HBM((lat, lat), BF),
            square,
            pltpu.VMEM((1, lat), F32),
            pltpu.VMEM((1, lat), F32),
            pltpu.HBM((lat, lat), BF),
        ),
        scratch_shapes=[
            pltpu.VMEM((nodes, edges), BF),
            pltpu.VMEM((lat, lat), BF),
            pltpu.VMEM((lat, lat), BF),
            pltpu.SemaphoreType.DMA((4,)),
        ],
        compiler_params=params(24),
        cost_estimate=cost(2 * nodes * edges * table, nodes * table * 2),
        name="count",
    )(src, dst, w_in, b_in, mesh, b_node, b_msg, *map(at_hbm, (w_node, w_out, w_msg)))


def hots(index, ref):
    step = 1024
    ids = lax.broadcasted_iota(jnp.int32, (step, ref.shape[1]), 0).astype(jnp.int16)
    for start in range(0, ref.shape[0], step):
        ref[pl.ds(start, step)] = hot(ids, (index - start).astype(jnp.int16))


def select_kernel(x_ref, idx_ref, low_ref, high_ref, tail_ref, near_hot, *, chans):
    rows, main = x_ref.shape
    half = low_ref.shape[1]
    last = main // chans
    group = chans + 1
    hots(idx_ref[...], near_hot)
    near = dot(x_ref[...], near_hot[:main])
    row = lax.broadcasted_iota(jnp.int32, (1, group, 1), 1)
    tail = jnp.zeros((rows // group, group, last), F32)
    for c in range(chans):
        part = x_ref[:, c * last : (c + 1) * last].astype(F32).reshape(rows // group, group, last)
        tail = jnp.where(row == c, part[:, chans:], tail)
    tail = tail.reshape(rows, last).astype(BF)
    tail_ref[...] = tail
    near = near + dot(tail, near_hot[main:])
    low_ref[...] = near[:, :half].astype(BF)
    high_ref[...] = near[:, half:].astype(BF)


def select(x, idx, chans):
    rows, main = x.shape
    last = main // chans
    pts = main + last
    half = idx.shape[1] // 2
    out = jax.ShapeDtypeStruct((rows, half), BF)
    return pl.pallas_call(
        functools.partial(select_kernel, chans=chans),
        in_specs=[VM, VM],
        out_specs=[VM] * 3,
        out_shape=(out, out, pltpu.VMEM((rows, last), BF)),
        scratch_shapes=[pltpu.VMEM((pts, 2 * half), BF)],
        compiler_params=params(24),
        cost_estimate=cost(4 * rows * pts * half, rows * pts * 2),
        name="select",
    )(*at_vmem(x), idx)


def slots_kernel(own_ref, low_ref, up_ref, src_ref, dst_ref, o_ref, *, start, pad):
    half = low_ref.shape[1]
    shape = (half, own_ref.shape[1])
    ids = lax.broadcasted_iota(jnp.int32, shape, 0) + start
    acc = own_ref[...].astype(F32)
    acc = acc + dot(low_ref[...], hot(ids, src_ref[...]))
    acc = acc + dot(up_ref[...], hot(ids + half, src_ref[...]))
    code = dst_ref[...] + 1
    row = lax.broadcasted_iota(jnp.int32, acc.shape, 0)
    acc = jnp.where(row == pad, (code // 16).astype(F32), acc)
    acc = jnp.where(row == 2 * pad + 1, (code % 16).astype(F32), acc)
    o_ref[...] = acc.T.astype(BF)


def slots_rows(own, low, up, src, dst, start, pad):
    rows, slots = own.shape
    return pl.pallas_call(
        functools.partial(slots_kernel, start=start, pad=pad),
        in_specs=[VM] * 5,
        out_shape=jax.ShapeDtypeStruct((slots, rows), BF),
        compiler_params=params(16),
        cost_estimate=cost(4 * rows * low.shape[1] * slots, slots * rows * 4),
        name="slots",
    )(*at_vmem(own, low, up), src, dst)


def act_of(x, dims, w_in, b_in, w_out, w_msg, b_msg):
    hidden = silu2(dot(x, w_in[...], dims) + b_in[...])
    latent = dot(hidden, w_out[...]).astype(BF)
    return latent, silu2(dot(latent, w_msg[...]) + b_msg[...])


def act_only(x, dims, w_in, b_in, w_both, b_msg):
    hidden = silu2(dot(x, w_in[...], dims) + b_in[...])
    return silu2(dot(hidden, w_both[...]) + b_msg[...])


def columns(src, dst, sem, spans):
    copies = []
    at = 0
    for k, (start, width) in enumerate(spans):
        copies.append(
            pltpu.make_async_copy(
                src.at[:, pl.ds(start, width)], dst.at[:, pl.ds(at, width)], sem.at[k]
            )
        )
        copies[-1].start()
        at += width
    return copies


def embed_tile(x, weights, lat_hbm, act_ref, buf, sem, row, point):
    latent, act = act_of(x, TN, *weights)
    rows = pl.ds(row, x.shape[1])
    buf[rows] = latent
    act_ref[rows] = act
    store = pltpu.make_async_copy(
        buf.at[rows], lat_hbm.at[pl.ds(point, x.shape[1])], sem.at[row // PIECE]
    )
    store.start()
    return [store]


def whole_copies(pairs, sem):
    copies = [pltpu.make_async_copy(f, t, sem.at[k]) for k, (f, t) in enumerate(pairs)]
    for c in copies:
        c.start()
    return copies


def first_kernel(
    x_ref, tail_ref, src_ref, w_in, b_in, b_msg, w_out_hbm, w_msg_hbm, s_hbm, lat_ref, sum_ref, own_ref,
    s_buf, act_buf, buf, w_out, w_msg, far_hot, sem, in_sem, w_sem, *, spans,
):
    w_loads = whole_copies(((w_out_hbm, w_out), (w_msg_hbm, w_msg)), w_sem)
    loads = columns(s_hbm, s_buf, in_sem, spans)
    hots(src_ref[...], far_hot)
    main = x_ref.shape[1]
    far = dot(x_ref[...], far_hot[:main]) + dot(tail_ref[...], far_hot[main:])
    own_ref[...] = far.astype(BF)
    for c in w_loads:
        c.wait()
    weights = (w_in, b_in, w_out, w_msg, b_msg)
    stores = embed_tile(tail_ref[...], weights, lat_ref, act_buf, buf, sem, 0, spans[0][0])
    for c in loads:
        c.wait()
    sum_ref[...] = dot(s_buf[...], act_buf[...])
    for c in stores:
        c.wait()


def second_kernel(
    low_ref, up_ref, w_both, w_in, b_in, b_msg, w_out_hbm, w_msg_hbm, s_hbm, before, x_hbm, _, lat_ref, sum_ref,
    s_buf, act_buf, buf, w_out, w_msg, x_buf, sem, in_sem, w_sem, x_sem, *, spans, tile,
):
    half = low_ref.shape[1]
    x_load = columns(x_hbm, x_buf, x_sem, spans[:1])
    w_loads = whole_copies(((w_out_hbm, w_out), (w_msg_hbm, w_msg), (before, sum_ref)), w_sem)
    loads = columns(s_hbm, s_buf, in_sem, spans)
    start, width = spans[0]
    halo = jnp.concatenate([low_ref[...], up_ref[...]], axis=1)
    act_buf[pl.ds(width, 2 * half)] = act_only(halo, TN, w_in, b_in, w_both, b_msg)
    x_load[0].wait()
    for c in w_loads:
        c.wait()
    weights = (w_in, b_in, w_out, w_msg, b_msg)
    stores = []
    for p in range(0, width, tile):
        x = x_buf[:, p : min(p + tile, width)]
        stores += embed_tile(x, weights, lat_ref, act_buf, buf, sem, p, start + p)
    for c in loads:
        c.wait()
    sum_ref[...] += dot(s_buf[...], act_buf[...])
    for c in stores:
        c.wait()


def embed(x, counts, weights, later, pts, spans, tile, tail=None, src=None, before=None):
    rows = x.shape[0]
    nodes = counts.shape[0]
    w_in, b_in, w_both, b_msg = weights
    lat = w_in.shape[1]
    wide = sum(width for _, width in spans)
    held = at_vmem(w_in, b_in, b_msg)
    remote = [at_hbm(a) for a in (*later, counts)]
    if before is None:
        kernel = functools.partial(first_kernel, spans=spans)
        span = wide
        args = [*at_vmem(x, tail), src, *held, *remote]
        specs = [VM] * 6 + [ANY] * 3
        alias = {}
        inner = [pltpu.VMEM((pts, src.shape[1]), BF)]
        sems = []
        more = [pltpu.VMEM((rows, src.shape[1]), BF)]
    else:
        kernel = functools.partial(second_kernel, spans=spans, tile=tile)
        span = spans[0][1]
        latent, total, low, up = before
        args = [*at_vmem(low, up, w_both), *held, *remote, at_hbm(total), at_hbm(x), at_hbm(latent)]
        specs = [VM] * 6 + [ANY] * 6
        alias = {11: 0}
        inner = [pltpu.VMEM((rows, span), BF)]
        sems = [pltpu.SemaphoreType.DMA((1,))]
        more = []
    return pl.pallas_call(
        kernel,
        in_specs=specs,
        out_specs=[ANY, VM] + [VM] * len(more),
        out_shape=(pltpu.HBM((pts, lat), BF), pltpu.VMEM((nodes, lat), F32), *more),
        scratch_shapes=[
            pltpu.VMEM((nodes, wide), BF),
            pltpu.VMEM((wide, lat), BF),
            pltpu.VMEM((span, lat), BF),
            pltpu.VMEM((lat, lat), BF),
            pltpu.VMEM((lat, lat), BF),
            *inner,
            pltpu.SemaphoreType.DMA((span // PIECE,)),
            pltpu.SemaphoreType.DMA((len(spans),)),
            pltpu.SemaphoreType.DMA((3,)),
            *sems,
        ],
        input_output_aliases=alias,
        compiler_params=params(28),
        cost_estimate=cost(2 * span * lat * (rows + 2 * lat + nodes), span * (rows + lat) * 2),
        name="embed",
    )(*args)


def node_kernel(r_ref, w_in, b_in, w_both, b_msg, sum_ref, *rest, pad):
    sources, o_ref, buffers, sem = rest[:5], rest[5], rest[6:11], rest[11]
    loads = [pltpu.make_async_copy(f, t, sem.at[k]) for k, (f, t) in enumerate(zip(sources, buffers))]
    for c in loads:
        c.start()
    w_mo, w_nb, pre_ref, w_no, mesh_ref = buffers
    nodes = sum_ref.shape[0]
    rows = r_ref[...]
    act = act_only(rows, (((1,), (0,)), ((), ())), w_in, b_in, w_both, b_msg)
    lane = lax.broadcasted_iota(jnp.int32, (8, rows.shape[1]), 1)
    pick = jnp.where(lane == pad, 16.0, jnp.where(lane == 2 * pad + 1, 1.0, 0.0)).astype(BF)
    dst = dot(pick, rows, NT)[:1].astype(jnp.int32) - 1
    ids = lax.broadcasted_iota(jnp.int32, (nodes, rows.shape[0]), 0)
    total = sum_ref[...] + dot(hot(ids, dst), act)
    high = total.astype(BF)
    low = (total - high.astype(F32)).astype(BF)
    loads[0].wait()
    summed = (dot(high, w_mo[...]) + dot(low, w_mo[...])).astype(BF)
    loads[1].wait()
    loads[2].wait()
    node = silu2(pre_ref[...] + dot(summed, w_nb[...]))
    loads[3].wait()
    loads[4].wait()
    o_ref[...] = (mesh_ref[...].astype(F32) + dot(node, w_no[...])).astype(BF)


def node_update(rows, weights, total, w_mo, mesh, pre, w_nb, w_no, pad):
    args = at_vmem(rows, *weights, total)
    later = [at_hbm(a) for a in (w_mo, w_nb, pre, w_no, mesh)]
    slots = rows.shape[0]
    lat = mesh.shape[1]
    return pl.pallas_call(
        functools.partial(node_kernel, pad=pad),
        in_specs=[VM] * len(args) + [ANY] * len(later),
        out_specs=VM,
        out_shape=jax.ShapeDtypeStruct(mesh.shape, BF),
        scratch_shapes=[pltpu.VMEM(a.shape, a.dtype) for a in later]
        + [pltpu.SemaphoreType.DMA((len(later),))],
        compiler_params=params(20),
        cost_estimate=cost(6 * slots * lat * lat, 6 * lat * lat * 2),
        name="node",
    )(*args, *later)


def shards(
    fields,
    chan_mean,
    chan_scale,
    w_embed_in,
    b_embed,
    w_embed_out,
    halo_index,
    local_src,
    local_dst,
    remote_src,
    remote_dst,
    w_msg_in,
    b_msg,
    w_msg_out,
    mesh_nodes,
    w_node_in,
    b_node,
    w_node_out,
):
    levels = lax.axis_size("lev")
    tiles = lax.axis_size("tile")
    chans, points = fields.shape
    pts = points // levels
    slot_count = remote_src.shape[2]
    halo = halo_index.shape[2]
    table = pts + 2 * halo
    wide = (chans + 1) * levels

    me = lax.axis_index("lev").astype(jnp.int32).reshape(1)
    sent = pack(me, chan_mean, chan_scale, fields, levels)
    got = lax.all_to_all(sent, "lev", split_axis=0, concat_axis=0, tiled=True)
    main = pts // (chans + 1) * chans
    x = got.reshape(wide, main)

    counts, w_in, pre, w_msg, w_both, b_in, b_out, w_nb = count_edges(
        local_src,
        local_dst,
        w_embed_in,
        b_embed[None, :],
        mesh_nodes,
        b_node[None, :],
        b_msg[None, :],
        w_node_in,
        w_embed_out,
        w_msg_in,
        table,
        wide,
        chans,
    )
    weights = [w_in, b_in, w_both, b_out]
    later = [w_embed_out, w_msg]

    src = remote_src.reshape(1, -1)
    dst = remote_dst.reshape(1, -1)
    low, high, tail = select(x, halo_index.reshape(1, 2 * halo), chans)
    ahead = [(i, (i + 1) % tiles) for i in range(tiles)]
    back = [(t, s) for s, t in ahead]
    from_low = lax.ppermute(high, "tile", ahead)
    from_up = lax.ppermute(low, "tile", back)

    tile = 2 * PIECE
    latent, total, own = embed(
        x, counts, weights, later, pts, ((main, pts - main),), tile, tail, src
    )

    rows = slots_rows(own, from_low, from_up, src, dst, pts, chans)
    rows = lax.all_to_all(
        rows.reshape(levels, slot_count, wide), "lev", split_axis=0, concat_axis=0, tiled=True
    ).reshape(levels * slot_count, wide)

    latent, total = embed(
        x,
        counts,
        weights,
        later,
        pts,
        ((0, main), (pts, 2 * halo)),
        tile,
        before=(latent, total, from_low, from_up),
    )
    mesh_out = node_update(
        rows, weights, total, w_msg_out, mesh_nodes, pre, w_nb, w_node_out, chans
    )
    return (latent, mesh_out)


def solution(mesh):
    return jax.shard_map(
        shards,
        mesh=mesh,
        in_specs=(
            P("lev", "tile"),
            P(),
            P(),
            P(),
            P(),
            P(),
            P(("tile", "lev"), None, None),
            P(("tile", "lev"), None),
            P(("tile", "lev"), None),
            P(("tile", "lev"), None, None),
            P(("tile", "lev"), None, None),
            P(),
            P(),
            P(),
            P(("tile", "lev"), None),
            P(),
            P(),
            P(),
        ),
        out_specs=(P(("tile", "lev"), None), P(("tile", "lev"), None)),
        check_vma=False,
    )
```

```python
import functools

import jax
import jax.numpy as jnp
from jax import lax
from jax.experimental import pallas as pl
from jax.experimental.pallas import tpu as pltpu
from jax.sharding import PartitionSpec as P


BF = jnp.bfloat16
F32 = jnp.float32
NT = (((1,), (1,)), ((), ()))
TN = (((0,), (0,)), ((), ()))
PIECE = 512
MIB = 1024 * 1024


def params(mib, **kw):
    return pltpu.CompilerParams(vmem_limit_bytes=mib * MIB, **kw)


def cost(flops, nbytes):
    return pl.CostEstimate(flops=int(flops), bytes_accessed=int(nbytes), transcendentals=0)


def dot(a, b, dims=(((1,), (0,)), ((), ()))):
    return lax.dot_general(a, b, dims, preferred_element_type=F32)


def silu2(h):
    return (h + h * jnp.tanh(h)).astype(BF)


def hot(ids, index, value=1.0):
    return jnp.where(ids == index, jnp.asarray(value, BF), jnp.asarray(0.0, BF))


def at_vmem(*arrays):
    return [pltpu.with_memory_space_constraint(a, pltpu.VMEM) for a in arrays]


def at_hbm(array):
    return pltpu.with_memory_space_constraint(array, pltpu.HBM)


VM = pl.BlockSpec(memory_space=pltpu.VMEM)
ANY = pl.BlockSpec(memory_space=pl.ANY)


def pack_kernel(me_ref, mean_ref, scale_ref, x_ref, o_ref, in_buf, out_buf, in_sem, out_sem, *, parts):
    chans, points = in_buf.shape
    levels, _, main = out_buf.shape
    pts = points // levels
    per = levels // parts
    width = per * pts

    def load(k):
        at = pl.ds(k * width, width)
        return pltpu.make_async_copy(x_ref.at[:, at], in_buf.at[:, at], in_sem.at[k])

    def store(k):
        at = pl.ds(k * per, per)
        return pltpu.make_async_copy(out_buf.at[at], o_ref.at[at], out_sem.at[k])

    for k in range(parts):
        load(k).start()
    base = me_ref[0] * chans
    row = lax.broadcasted_iota(jnp.int32, (chans, 1), 0)
    mean = jnp.zeros((chans, 1), F32)
    scale = jnp.zeros((chans, 1), F32)
    for c in range(chans):
        mean = jnp.where(row == c, mean_ref[base + c], mean)
        scale = jnp.where(row == c, scale_ref[base + c], scale)
    for k in range(parts):
        load(k).wait()
        for j in range(k * per, (k + 1) * per):
            val = (in_buf[:, j * pts : (j + 1) * pts] - mean) * scale
            last = jnp.concatenate([val[c : c + 1, main:] for c in range(chans)], axis=1)
            out_buf[j] = jnp.concatenate([val[:, :main], last], axis=0).astype(BF)
        store(k).start()
    for k in range(parts):
        store(k).wait()


def pack(me, mean, scale, fields, levels):
    chans, points = fields.shape
    pts = points // levels
    parts = 8
    smem = pl.BlockSpec(memory_space=pltpu.SMEM)
    shape = (levels, chans + 1, pts * chans // (chans + 1))
    return pl.pallas_call(
        functools.partial(pack_kernel, parts=parts),
        in_specs=[smem, smem, smem, pl.BlockSpec(memory_space=pl.ANY)],
        out_specs=pl.BlockSpec(memory_space=pl.ANY),
        out_shape=jax.ShapeDtypeStruct(shape, BF),
        scratch_shapes=[
            pltpu.VMEM(fields.shape, F32),
            pltpu.VMEM(shape, BF),
            pltpu.SemaphoreType.DMA((parts,)),
            pltpu.SemaphoreType.DMA((parts,)),
        ],
        compiler_params=params(60),
        cost_estimate=cost(points * 16, points * 48),
        name="pack",
    )(me, mean, scale, fields)


def count_kernel(
    src_ref, dst_ref, w_ref, b_ref, mesh_ref, b_n, b_m, w_node, w_out, w_msg,
    o_ref, w_in_ref, pre_ref, msg_ref, both_ref, bi_ref, bm_ref, nb_ref, hot_ref, na_ref, out_ref, sem, *, chans,
):
    nodes, edges = hot_ref.shape
    lat = w_out.shape[0]
    tile = 512
    chunk = 1024
    pairs = (
        (w_node.at[pl.ds(0, lat)], na_ref),
        (w_node.at[pl.ds(lat, lat)], nb_ref),
        (w_out, out_ref),
        (w_msg, msg_ref),
    )
    copies = [pltpu.make_async_copy(f, t, sem.at[k]) for k, (f, t) in enumerate(pairs)]
    for c in copies:
        c.start()
    ids = lax.broadcasted_iota(jnp.int32, (nodes, edges), 0).astype(jnp.int16)
    hot_ref[...] = hot(ids, dst_ref[...].astype(jnp.int16))
    shape = (w_in_ref.shape[0], w_ref.shape[0])
    row = lax.broadcasted_iota(jnp.int32, shape, 0)
    col = lax.broadcasted_iota(jnp.int32, shape, 1)
    lane = row % (chans + 1)
    place = jnp.where(lane < chans, row // (chans + 1) * chans + lane, -1)
    w_in_ref[...] = dot(hot(col, place, 0.5), w_ref[...]).astype(BF)
    bi_ref[...] = 0.5 * b_ref[...]
    bm_ref[...] = 0.5 * b_m[...]

    @pl.loop(0, o_ref.shape[1] // tile)
    def _(i):
        start = pl.multiple_of(i * tile, tile)
        rows = lax.broadcasted_iota(jnp.int32, (tile, chunk), 0).astype(jnp.int16)
        acc = jnp.zeros((nodes, tile), F32)
        for c in range(edges // chunk):
            at = slice(c * chunk, (c + 1) * chunk)
            acc = acc + dot(hot_ref[:, at], hot(rows, (src_ref[:, at] - start).astype(jnp.int16)), NT)
        o_ref[:, pl.ds(start, tile)] = acc.astype(BF)

    for c in copies:
        c.wait()
    msg_ref[...] = msg_ref[...] * 0.5
    both_ref[...] = dot(out_ref[...], msg_ref[...]).astype(BF)
    nb_ref[...] = nb_ref[...] * 0.5
    pre_ref[...] = 0.5 * (dot(mesh_ref[...], na_ref[...]) + b_n[...])


def count_edges(src, dst, w_in, b_in, mesh, b_node, b_msg, w_node, w_out, w_msg, table, wide, chans):
    edges = src.shape[1]
    nodes, lat = mesh.shape
    square = pltpu.VMEM((lat, lat), BF)
    return pl.pallas_call(
        functools.partial(count_kernel, chans=chans),
        in_specs=[VM] * 7 + [ANY] * 3,
        out_specs=[VM] * 8,
        out_shape=(
            pltpu.HBM((nodes, table), BF),
            pltpu.VMEM((wide, lat), BF),
            pltpu.HBM((nodes, lat), F32),
            pltpu.HBM((lat, lat), BF),
            square,
            pltpu.VMEM((1, lat), F32),
            pltpu.VMEM((1, lat), F32),
            pltpu.HBM((lat, lat), BF),
        ),
        scratch_shapes=[
            pltpu.VMEM((nodes, edges), BF),
            pltpu.VMEM((lat, lat), BF),
            pltpu.VMEM((lat, lat), BF),
            pltpu.SemaphoreType.DMA((4,)),
        ],
        compiler_params=params(24),
        cost_estimate=cost(2 * nodes * edges * table, nodes * table * 2),
        name="count",
    )(src, dst, w_in, b_in, mesh, b_node, b_msg, *map(at_hbm, (w_node, w_out, w_msg)))


def hots(index, ref):
    step = 1024
    ids = lax.broadcasted_iota(jnp.int32, (step, ref.shape[1]), 0).astype(jnp.int16)
    for start in range(0, ref.shape[0], step):
        ref[pl.ds(start, step)] = hot(ids, (index - start).astype(jnp.int16))


def select_kernel(x_ref, idx_ref, low_ref, high_ref, tail_ref, near_hot, *, chans):
    rows, main = x_ref.shape
    half = low_ref.shape[1]
    last = main // chans
    group = chans + 1
    hots(idx_ref[...], near_hot)
    near = dot(x_ref[...], near_hot[:main])
    row = lax.broadcasted_iota(jnp.int32, (1, group, 1), 1)
    tail = jnp.zeros((rows // group, group, last), F32)
    for c in range(chans):
        part = x_ref[:, c * last : (c + 1) * last].astype(F32).reshape(rows // group, group, last)
        tail = jnp.where(row == c, part[:, chans:], tail)
    tail = tail.reshape(rows, last).astype(BF)
    tail_ref[...] = tail
    near = near + dot(tail, near_hot[main:])
    low_ref[...] = near[:, :half].astype(BF)
    high_ref[...] = near[:, half:].astype(BF)


def select(x, idx, chans):
    rows, main = x.shape
    last = main // chans
    pts = main + last
    half = idx.shape[1] // 2
    out = jax.ShapeDtypeStruct((rows, half), BF)
    return pl.pallas_call(
        functools.partial(select_kernel, chans=chans),
        in_specs=[VM, VM],
        out_specs=[VM] * 3,
        out_shape=(out, out, pltpu.VMEM((rows, last), BF)),
        scratch_shapes=[pltpu.VMEM((pts, 2 * half), BF)],
        compiler_params=params(24),
        cost_estimate=cost(4 * rows * pts * half, rows * pts * 2),
        name="select",
    )(*at_vmem(x), idx)


def slots_kernel(own_ref, low_ref, up_ref, src_ref, dst_ref, o_ref, *, start, pad):
    half = low_ref.shape[1]
    shape = (half, own_ref.shape[1])
    ids = lax.broadcasted_iota(jnp.int32, shape, 0) + start
    acc = own_ref[...].astype(F32)
    acc = acc + dot(low_ref[...], hot(ids, src_ref[...]))
    acc = acc + dot(up_ref[...], hot(ids + half, src_ref[...]))
    code = dst_ref[...] + 1
    row = lax.broadcasted_iota(jnp.int32, acc.shape, 0)
    acc = jnp.where(row == pad, (code // 16).astype(F32), acc)
    acc = jnp.where(row == 2 * pad + 1, (code % 16).astype(F32), acc)
    o_ref[...] = acc.T.astype(BF)


def slots_rows(own, low, up, src, dst, start, pad):
    rows, slots = own.shape
    return pl.pallas_call(
        functools.partial(slots_kernel, start=start, pad=pad),
        in_specs=[VM] * 5,
        out_shape=jax.ShapeDtypeStruct((slots, rows), BF),
        compiler_params=params(16),
        cost_estimate=cost(4 * rows * low.shape[1] * slots, slots * rows * 4),
        name="slots",
    )(*at_vmem(own, low, up), src, dst)


def act_of(x, dims, w_in, b_in, w_out, w_msg, b_msg):
    hidden = silu2(dot(x, w_in[...], dims) + b_in[...])
    latent = dot(hidden, w_out[...]).astype(BF)
    return latent, silu2(dot(latent, w_msg[...]) + b_msg[...])


def act_only(x, dims, w_in, b_in, w_both, b_msg):
    hidden = silu2(dot(x, w_in[...], dims) + b_in[...])
    return silu2(dot(hidden, w_both[...]) + b_msg[...])


def columns(src, dst, sem, spans):
    copies = []
    at = 0
    for k, (start, width) in enumerate(spans):
        copies.append(
            pltpu.make_async_copy(
                src.at[:, pl.ds(start, width)], dst.at[:, pl.ds(at, width)], sem.at[k]
            )
        )
        copies[-1].start()
        at += width
    return copies


def embed_tile(x, weights, lat_hbm, act_ref, buf, sem, row, point):
    latent, act = act_of(x, TN, *weights)
    rows = pl.ds(row, x.shape[1])
    buf[rows] = latent
    act_ref[rows] = act
    store = pltpu.make_async_copy(
        buf.at[rows], lat_hbm.at[pl.ds(point, x.shape[1])], sem.at[row // PIECE]
    )
    store.start()
    return [store]


def whole_copies(pairs, sem):
    copies = [pltpu.make_async_copy(f, t, sem.at[k]) for k, (f, t) in enumerate(pairs)]
    for c in copies:
        c.start()
    return copies


def first_kernel(
    x_ref, tail_ref, src_ref, w_in, b_in, b_msg, w_out_hbm, w_msg_hbm, s_hbm, lat_ref, sum_ref, own_ref,
    s_buf, act_buf, buf, w_out, w_msg, far_hot, sem, in_sem, w_sem, *, spans,
):
    w_loads = whole_copies(((w_out_hbm, w_out), (w_msg_hbm, w_msg)), w_sem)
    loads = columns(s_hbm, s_buf, in_sem, spans)
    hots(src_ref[...], far_hot)
    main = x_ref.shape[1]
    far = dot(x_ref[...], far_hot[:main]) + dot(tail_ref[...], far_hot[main:])
    own_ref[...] = far.astype(BF)
    for c in w_loads:
        c.wait()
    weights = (w_in, b_in, w_out, w_msg, b_msg)
    stores = embed_tile(tail_ref[...], weights, lat_ref, act_buf, buf, sem, 0, spans[0][0])
    for c in loads:
        c.wait()
    sum_ref[...] = dot(s_buf[...], act_buf[...])
    for c in stores:
        c.wait()


def second_kernel(
    low_ref, up_ref, w_both, w_in, b_in, b_msg, w_out_hbm, w_msg_hbm, s_hbm, before, x_hbm, _, lat_ref, sum_ref,
    s_buf, act_buf, buf, w_out, w_msg, x_buf, sem, in_sem, w_sem, x_sem, *, spans, tile,
):
    half = low_ref.shape[1]
    x_load = columns(x_hbm, x_buf, x_sem, spans[:1])
    w_loads = whole_copies(((w_out_hbm, w_out), (w_msg_hbm, w_msg), (before, sum_ref)), w_sem)
    loads = columns(s_hbm, s_buf, in_sem, spans)
    start, width = spans[0]
    halo = jnp.concatenate([low_ref[...], up_ref[...]], axis=1)
    act_buf[pl.ds(width, 2 * half)] = act_only(halo, TN, w_in, b_in, w_both, b_msg)
    x_load[0].wait()
    for c in w_loads:
        c.wait()
    weights = (w_in, b_in, w_out, w_msg, b_msg)
    stores = []
    for p in range(0, width, tile):
        x = x_buf[:, p : min(p + tile, width)]
        stores += embed_tile(x, weights, lat_ref, act_buf, buf, sem, p, start + p)
    for c in loads:
        c.wait()
    sum_ref[...] += dot(s_buf[...], act_buf[...])
    for c in stores:
        c.wait()


def embed(x, counts, weights, later, pts, spans, tile, tail=None, src=None, before=None):
    rows = x.shape[0]
    nodes = counts.shape[0]
    w_in, b_in, w_both, b_msg = weights
    lat = w_in.shape[1]
    wide = sum(width for _, width in spans)
    held = at_vmem(w_in, b_in, b_msg)
    remote = [at_hbm(a) for a in (*later, counts)]
    if before is None:
        kernel = functools.partial(first_kernel, spans=spans)
        span = wide
        args = [*at_vmem(x, tail), src, *held, *remote]
        specs = [VM] * 6 + [ANY] * 3
        alias = {}
        inner = [pltpu.VMEM((pts, src.shape[1]), BF)]
        sems = []
        more = [pltpu.VMEM((rows, src.shape[1]), BF)]
    else:
        kernel = functools.partial(second_kernel, spans=spans, tile=tile)
        span = spans[0][1]
        latent, total, low, up = before
        args = [*at_vmem(low, up, w_both), *held, *remote, at_hbm(total), at_hbm(x), at_hbm(latent)]
        specs = [VM] * 6 + [ANY] * 6
        alias = {11: 0}
        inner = [pltpu.VMEM((rows, span), BF)]
        sems = [pltpu.SemaphoreType.DMA((1,))]
        more = []
    return pl.pallas_call(
        kernel,
        in_specs=specs,
        out_specs=[ANY, VM] + [VM] * len(more),
        out_shape=(pltpu.HBM((pts, lat), BF), pltpu.VMEM((nodes, lat), F32), *more),
        scratch_shapes=[
            pltpu.VMEM((nodes, wide), BF),
            pltpu.VMEM((wide, lat), BF),
            pltpu.VMEM((span, lat), BF),
            pltpu.VMEM((lat, lat), BF),
            pltpu.VMEM((lat, lat), BF),
            *inner,
            pltpu.SemaphoreType.DMA((span // PIECE,)),
            pltpu.SemaphoreType.DMA((len(spans),)),
            pltpu.SemaphoreType.DMA((3,)),
            *sems,
        ],
        input_output_aliases=alias,
        compiler_params=params(28),
        cost_estimate=cost(2 * span * lat * (rows + 2 * lat + nodes), span * (rows + lat) * 2),
        name="embed",
    )(*args)


def node_kernel(r_ref, w_in, b_in, w_both, b_msg, sum_ref, *rest, pad):
    sources, o_ref, buffers, sem = rest[:5], rest[5], rest[6:11], rest[11]
    loads = [pltpu.make_async_copy(f, t, sem.at[k]) for k, (f, t) in enumerate(zip(sources, buffers))]
    for c in loads:
        c.start()
    w_mo, w_nb, pre_ref, w_no, mesh_ref = buffers
    nodes = sum_ref.shape[0]
    rows = r_ref[...]
    act = act_only(rows, (((1,), (0,)), ((), ())), w_in, b_in, w_both, b_msg)
    lane = lax.broadcasted_iota(jnp.int32, (8, rows.shape[1]), 1)
    pick = jnp.where(lane == pad, 16.0, jnp.where(lane == 2 * pad + 1, 1.0, 0.0)).astype(BF)
    dst = dot(pick, rows, NT)[:1].astype(jnp.int32) - 1
    ids = lax.broadcasted_iota(jnp.int32, (nodes, rows.shape[0]), 0)
    total = sum_ref[...] + dot(hot(ids, dst), act)
    high = total.astype(BF)
    low = (total - high.astype(F32)).astype(BF)
    loads[0].wait()
    summed = (dot(high, w_mo[...]) + dot(low, w_mo[...])).astype(BF)
    loads[1].wait()
    loads[2].wait()
    node = silu2(pre_ref[...] + dot(summed, w_nb[...]))
    loads[3].wait()
    loads[4].wait()
    o_ref[...] = (mesh_ref[...].astype(F32) + dot(node, w_no[...])).astype(BF)


def node_update(rows, weights, total, w_mo, mesh, pre, w_nb, w_no, pad):
    args = at_vmem(rows, *weights, total)
    later = [at_hbm(a) for a in (w_mo, w_nb, pre, w_no, mesh)]
    slots = rows.shape[0]
    lat = mesh.shape[1]
    return pl.pallas_call(
        functools.partial(node_kernel, pad=pad),
        in_specs=[VM] * len(args) + [ANY] * len(later),
        out_specs=VM,
        out_shape=jax.ShapeDtypeStruct(mesh.shape, BF),
        scratch_shapes=[pltpu.VMEM(a.shape, a.dtype) for a in later]
        + [pltpu.SemaphoreType.DMA((len(later),))],
        compiler_params=params(20),
        cost_estimate=cost(6 * slots * lat * lat, 6 * lat * lat * 2),
        name="node",
    )(*args, *later)


def shards(
    fields,
    chan_mean,
    chan_scale,
    w_embed_in,
    b_embed,
    w_embed_out,
    halo_index,
    local_src,
    local_dst,
    remote_src,
    remote_dst,
    w_msg_in,
    b_msg,
    w_msg_out,
    mesh_nodes,
    w_node_in,
    b_node,
    w_node_out,
):
    levels = lax.axis_size("lev")
    tiles = lax.axis_size("tile")
    chans, points = fields.shape
    pts = points // levels
    slot_count = remote_src.shape[2]
    halo = halo_index.shape[2]
    table = pts + 2 * halo
    wide = (chans + 1) * levels

    me = lax.axis_index("lev").astype(jnp.int32).reshape(1)
    sent = pack(me, chan_mean, chan_scale, fields, levels)
    got = lax.all_to_all(sent, "lev", split_axis=0, concat_axis=0, tiled=True)
    main = pts // (chans + 1) * chans
    x = got.reshape(wide, main)

    src = remote_src.reshape(1, -1)
    dst = remote_dst.reshape(1, -1)
    idx = halo_index.reshape(1, 2 * halo)
    first_src, src, dst, idx = lax.optimization_barrier((local_src, src, dst, idx))
    counts, w_in, pre, w_msg, w_both, b_in, b_out, w_nb = count_edges(
        first_src,
        local_dst,
        w_embed_in,
        b_embed[None, :],
        mesh_nodes,
        b_node[None, :],
        b_msg[None, :],
        w_node_in,
        w_embed_out,
        w_msg_in,
        table,
        wide,
        chans,
    )
    weights = [w_in, b_in, w_both, b_out]
    later = [w_embed_out, w_msg]

    low, high, tail = select(x, idx, chans)
    ahead = [(i, (i + 1) % tiles) for i in range(tiles)]
    back = [(t, s) for s, t in ahead]
    from_low = lax.ppermute(high, "tile", ahead)
    from_up = lax.ppermute(low, "tile", back)

    tile = 2 * PIECE
    latent, total, own = embed(
        x, counts, weights, later, pts, ((main, pts - main),), tile, tail, src
    )

    rows = slots_rows(own, from_low, from_up, src, dst, pts, chans)
    rows = lax.all_to_all(
        rows.reshape(levels, slot_count, wide), "lev", split_axis=0, concat_axis=0, tiled=True
    ).reshape(levels * slot_count, wide)

    latent, total = embed(
        x,
        counts,
        weights,
        later,
        pts,
        ((0, main), (pts, 2 * halo)),
        tile,
        before=(latent, total, from_low, from_up),
    )
    mesh_out = node_update(
        rows, weights, total, w_msg_out, mesh_nodes, pre, w_nb, w_node_out, chans
    )
    return (latent, mesh_out)


def solution(mesh):
    return jax.shard_map(
        shards,
        mesh=mesh,
        in_specs=(
            P("lev", "tile"),
            P(),
            P(),
            P(),
            P(),
            P(),
            P(("tile", "lev"), None, None),
            P(("tile", "lev"), None),
            P(("tile", "lev"), None),
            P(("tile", "lev"), None, None),
            P(("tile", "lev"), None, None),
            P(),
            P(),
            P(),
            P(("tile", "lev"), None),
            P(),
            P(),
            P(),
        ),
        out_specs=(P(("tile", "lev"), None), P(("tile", "lev"), None)),
        check_vma=False,
    )
```

```python
import functools

import jax
import jax.numpy as jnp
from jax import lax
from jax.experimental import pallas as pl
from jax.experimental.pallas import tpu as pltpu
from jax.sharding import PartitionSpec as P


BF = jnp.bfloat16
F32 = jnp.float32
NT = (((1,), (1,)), ((), ()))
TN = (((0,), (0,)), ((), ()))
PIECE = 512
MIB = 1024 * 1024


def params(mib, **kw):
    return pltpu.CompilerParams(vmem_limit_bytes=mib * MIB, **kw)


def cost(flops, nbytes):
    return pl.CostEstimate(flops=int(flops), bytes_accessed=int(nbytes), transcendentals=0)


def dot(a, b, dims=(((1,), (0,)), ((), ()))):
    return lax.dot_general(a, b, dims, preferred_element_type=F32)


def silu2(h):
    return (h + h * jnp.tanh(h)).astype(BF)


def hot(ids, index, value=1.0):
    return jnp.where(ids == index, jnp.asarray(value, BF), jnp.asarray(0.0, BF))


def at_vmem(*arrays):
    return [pltpu.with_memory_space_constraint(a, pltpu.VMEM) for a in arrays]


def at_hbm(array):
    return pltpu.with_memory_space_constraint(array, pltpu.HBM)


VM = pl.BlockSpec(memory_space=pltpu.VMEM)
ANY = pl.BlockSpec(memory_space=pl.ANY)


def pack_kernel(me_ref, mean_ref, scale_ref, x_ref, o_ref, in_buf, out_buf, in_sem, out_sem, *, parts):
    chans, points = in_buf.shape
    levels, _, main = out_buf.shape
    pts = points // levels
    per = levels // parts
    width = per * pts

    def load(k):
        at = pl.ds(k * width, width)
        return pltpu.make_async_copy(x_ref.at[:, at], in_buf.at[:, at], in_sem.at[k])

    def store(k):
        at = pl.ds(k * per, per)
        return pltpu.make_async_copy(out_buf.at[at], o_ref.at[at], out_sem.at[k])

    for k in range(parts):
        load(k).start()
    base = me_ref[0] * chans
    row = lax.broadcasted_iota(jnp.int32, (chans, 1), 0)
    mean = jnp.zeros((chans, 1), F32)
    scale = jnp.zeros((chans, 1), F32)
    for c in range(chans):
        mean = jnp.where(row == c, mean_ref[base + c], mean)
        scale = jnp.where(row == c, scale_ref[base + c], scale)
    for k in range(parts):
        load(k).wait()
        for j in range(k * per, (k + 1) * per):
            val = (in_buf[:, j * pts : (j + 1) * pts] - mean) * scale
            last = jnp.concatenate([val[c : c + 1, main:] for c in range(chans)], axis=1)
            out_buf[j] = jnp.concatenate([val[:, :main], last], axis=0).astype(BF)
        store(k).start()
    for k in range(parts):
        store(k).wait()


def pack(me, mean, scale, fields, levels):
    chans, points = fields.shape
    pts = points // levels
    parts = 8
    smem = pl.BlockSpec(memory_space=pltpu.SMEM)
    shape = (levels, chans + 1, pts * chans // (chans + 1))
    return pl.pallas_call(
        functools.partial(pack_kernel, parts=parts),
        in_specs=[smem, smem, smem, pl.BlockSpec(memory_space=pl.ANY)],
        out_specs=pl.BlockSpec(memory_space=pl.ANY),
        out_shape=jax.ShapeDtypeStruct(shape, BF),
        scratch_shapes=[
            pltpu.VMEM(fields.shape, F32),
            pltpu.VMEM(shape, BF),
            pltpu.SemaphoreType.DMA((parts,)),
            pltpu.SemaphoreType.DMA((parts,)),
        ],
        compiler_params=params(60),
        cost_estimate=cost(points * 16, points * 48),
        name="pack",
    )(me, mean, scale, fields)


def count_kernel(
    src_ref, dst_ref, w_ref, b_ref, mesh_ref, b_n, b_m, w_node, w_out, w_msg,
    o_ref, w_in_ref, pre_ref, msg_ref, both_ref, bi_ref, bm_ref, nb_ref, hot_ref, na_ref, out_ref, sem, *, chans,
):
    nodes, edges = hot_ref.shape
    lat = w_out.shape[0]
    tile = 512
    chunk = 1024
    pairs = (
        (w_node.at[pl.ds(0, lat)], na_ref),
        (w_node.at[pl.ds(lat, lat)], nb_ref),
        (w_out, out_ref),
        (w_msg, msg_ref),
    )
    copies = [pltpu.make_async_copy(f, t, sem.at[k]) for k, (f, t) in enumerate(pairs)]
    for c in copies:
        c.start()
    ids = lax.broadcasted_iota(jnp.int32, (nodes, edges), 0).astype(jnp.int16)
    hot_ref[...] = hot(ids, dst_ref[...].astype(jnp.int16))
    shape = (w_in_ref.shape[0], w_ref.shape[0])
    row = lax.broadcasted_iota(jnp.int32, shape, 0)
    col = lax.broadcasted_iota(jnp.int32, shape, 1)
    lane = row % (chans + 1)
    place = jnp.where(lane < chans, row // (chans + 1) * chans + lane, -1)
    w_in_ref[...] = dot(hot(col, place, 0.5), w_ref[...]).astype(BF)
    bi_ref[...] = 0.5 * b_ref[...]
    bm_ref[...] = 0.5 * b_m[...]

    @pl.loop(0, o_ref.shape[1] // tile)
    def _(i):
        start = pl.multiple_of(i * tile, tile)
        rows = lax.broadcasted_iota(jnp.int32, (tile, chunk), 0).astype(jnp.int16)
        acc = jnp.zeros((nodes, tile), F32)
        for c in range(edges // chunk):
            at = slice(c * chunk, (c + 1) * chunk)
            acc = acc + dot(hot_ref[:, at], hot(rows, (src_ref[:, at] - start).astype(jnp.int16)), NT)
        o_ref[:, pl.ds(start, tile)] = acc.astype(BF)

    for c in copies:
        c.wait()
    msg_ref[...] = msg_ref[...] * 0.5
    both_ref[...] = dot(out_ref[...], msg_ref[...]).astype(BF)
    nb_ref[...] = nb_ref[...] * 0.5
    pre_ref[...] = 0.5 * (dot(mesh_ref[...], na_ref[...]) + b_n[...])


def count_edges(src, dst, w_in, b_in, mesh, b_node, b_msg, w_node, w_out, w_msg, table, wide, chans):
    edges = src.shape[1]
    nodes, lat = mesh.shape
    square = pltpu.VMEM((lat, lat), BF)
    return pl.pallas_call(
        functools.partial(count_kernel, chans=chans),
        in_specs=[VM] * 7 + [ANY] * 3,
        out_specs=[VM] * 8,
        out_shape=(
            pltpu.HBM((nodes, table), BF),
            pltpu.VMEM((wide, lat), BF),
            pltpu.HBM((nodes, lat), F32),
            pltpu.HBM((lat, lat), BF),
            square,
            pltpu.VMEM((1, lat), F32),
            pltpu.VMEM((1, lat), F32),
            pltpu.HBM((lat, lat), BF),
        ),
        scratch_shapes=[
            pltpu.VMEM((nodes, edges), BF),
            pltpu.VMEM((lat, lat), BF),
            pltpu.VMEM((lat, lat), BF),
            pltpu.SemaphoreType.DMA((4,)),
        ],
        compiler_params=params(24),
        cost_estimate=cost(2 * nodes * edges * table, nodes * table * 2),
        name="count",
    )(src, dst, w_in, b_in, mesh, b_node, b_msg, *map(at_hbm, (w_node, w_out, w_msg)))


def hots(index, ref):
    step = 1024
    ids = lax.broadcasted_iota(jnp.int32, (step, ref.shape[1]), 0).astype(jnp.int16)
    for start in range(0, ref.shape[0], step):
        ref[pl.ds(start, step)] = hot(ids, (index - start).astype(jnp.int16))


def select_kernel(x_ref, idx_ref, low_ref, high_ref, tail_ref, near_hot, *, chans):
    rows, main = x_ref.shape
    half = low_ref.shape[1]
    last = main // chans
    group = chans + 1
    hots(idx_ref[...], near_hot)
    near = dot(x_ref[...], near_hot[:main])
    row = lax.broadcasted_iota(jnp.int32, (1, group, 1), 1)
    tail = jnp.zeros((rows // group, group, last), F32)
    for c in range(chans):
        part = x_ref[:, c * last : (c + 1) * last].astype(F32).reshape(rows // group, group, last)
        tail = jnp.where(row == c, part[:, chans:], tail)
    tail = tail.reshape(rows, last).astype(BF)
    tail_ref[...] = tail
    near = near + dot(tail, near_hot[main:])
    low_ref[...] = near[:, :half].astype(BF)
    high_ref[...] = near[:, half:].astype(BF)


def select(x, idx, chans):
    rows, main = x.shape
    last = main // chans
    pts = main + last
    half = idx.shape[1] // 2
    out = jax.ShapeDtypeStruct((rows, half), BF)
    return pl.pallas_call(
        functools.partial(select_kernel, chans=chans),
        in_specs=[VM, VM],
        out_specs=[VM] * 3,
        out_shape=(out, out, pltpu.VMEM((rows, last), BF)),
        scratch_shapes=[pltpu.VMEM((pts, 2 * half), BF)],
        compiler_params=params(24),
        cost_estimate=cost(4 * rows * pts * half, rows * pts * 2),
        name="select",
    )(*at_vmem(x), idx)


def slots_kernel(own_ref, low_ref, up_ref, src_ref, dst_ref, o_ref, *, start, pad):
    half = low_ref.shape[1]
    shape = (half, own_ref.shape[1])
    ids = lax.broadcasted_iota(jnp.int32, shape, 0) + start
    acc = own_ref[...].astype(F32)
    acc = acc + dot(low_ref[...], hot(ids, src_ref[...]))
    acc = acc + dot(up_ref[...], hot(ids + half, src_ref[...]))
    code = dst_ref[...] + 1
    row = lax.broadcasted_iota(jnp.int32, acc.shape, 0)
    acc = jnp.where(row == pad, (code // 16).astype(F32), acc)
    acc = jnp.where(row == 2 * pad + 1, (code % 16).astype(F32), acc)
    o_ref[...] = acc.T.astype(BF)


def slots_rows(own, low, up, src, dst, start, pad):
    rows, slots = own.shape
    return pl.pallas_call(
        functools.partial(slots_kernel, start=start, pad=pad),
        in_specs=[VM] * 5,
        out_shape=jax.ShapeDtypeStruct((slots, rows), BF),
        compiler_params=params(16),
        cost_estimate=cost(4 * rows * low.shape[1] * slots, slots * rows * 4),
        name="slots",
    )(*at_vmem(own, low, up), src, dst)


def act_of(x, dims, w_in, b_in, w_out, w_msg, b_msg):
    hidden = silu2(dot(x, w_in[...], dims) + b_in[...])
    latent = dot(hidden, w_out[...]).astype(BF)
    return latent, silu2(dot(latent, w_msg[...]) + b_msg[...])


def act_only(x, dims, w_in, b_in, w_both, b_msg):
    hidden = silu2(dot(x, w_in[...], dims) + b_in[...])
    return silu2(dot(hidden, w_both[...]) + b_msg[...])


def embed_tile(x, weights, lat_hbm, act_ref, buf, sem, row, point):
    latent, act = act_of(x, TN, *weights)
    rows = pl.ds(row, x.shape[1])
    buf[rows] = latent
    act_ref[rows] = act
    store = pltpu.make_async_copy(
        buf.at[rows], lat_hbm.at[pl.ds(point, x.shape[1])], sem.at[row // PIECE]
    )
    store.start()
    return [store]


def whole_copies(pairs, sem):
    copies = [pltpu.make_async_copy(f, t, sem.at[k]) for k, (f, t) in enumerate(pairs)]
    for c in copies:
        c.start()
    return copies


def first_kernel(
    x_ref, tail_ref, src_ref, w_in, b_in, b_msg, w_out_hbm, w_msg_hbm, lat_ref, act_hbm, own_ref,
    act_buf, buf, w_out, w_msg, far_hot, sem, w_sem, act_sem, *, point,
):
    w_loads = whole_copies(((w_out_hbm, w_out), (w_msg_hbm, w_msg)), w_sem)
    hots(src_ref[...], far_hot)
    main = x_ref.shape[1]
    far = dot(x_ref[...], far_hot[:main]) + dot(tail_ref[...], far_hot[main:])
    own_ref[...] = far.astype(BF)
    for c in w_loads:
        c.wait()
    weights = (w_in, b_in, w_out, w_msg, b_msg)
    stores = embed_tile(tail_ref[...], weights, lat_ref, act_buf, buf, sem, 0, point)
    stores.append(pltpu.make_async_copy(act_buf, act_hbm, act_sem))
    stores[-1].start()
    for c in stores:
        c.wait()


def second_kernel(
    low_ref, up_ref, w_both, w_in, b_in, b_msg, w_out_hbm, w_msg_hbm, s_hbm, act_hbm, x_hbm, _, lat_ref, sum_ref,
    act_buf, buf, w_out, w_msg, s_buf, x_buf, sem, w_sem, in_sem, *, tile,
):
    half = low_ref.shape[1]
    width = x_hbm.shape[1]
    pts = width + act_hbm.shape[0]
    x_load = whole_copies(((x_hbm, x_buf),), in_sem)[0]
    w_loads = whole_copies(((w_out_hbm, w_out), (w_msg_hbm, w_msg)), w_sem)
    s_load = pltpu.make_async_copy(s_hbm, s_buf, in_sem.at[1])
    act_load = pltpu.make_async_copy(act_hbm, act_buf.at[pl.ds(width, pts - width)], in_sem.at[2])
    s_load.start()
    act_load.start()
    halo = jnp.concatenate([low_ref[...], up_ref[...]], axis=1)
    act_buf[pl.ds(pts, 2 * half)] = act_only(halo, TN, w_in, b_in, w_both, b_msg)
    x_load.wait()
    for c in w_loads:
        c.wait()
    weights = (w_in, b_in, w_out, w_msg, b_msg)
    stores = []
    for p in range(0, width, tile):
        x = x_buf[:, p : min(p + tile, width)]
        stores += embed_tile(x, weights, lat_ref, act_buf, buf, sem, p, p)
    s_load.wait()
    act_load.wait()
    sum_ref[...] = dot(s_buf[...], act_buf[...])
    for c in stores:
        c.wait()


def embed_call(kernel, args, specs, out_shape, out_specs, span, acts, lat, inner, sems, alias, flops):
    return pl.pallas_call(
        kernel,
        in_specs=specs,
        out_specs=[ANY, *out_specs],
        out_shape=out_shape,
        scratch_shapes=[
            pltpu.VMEM((acts, lat), BF),
            pltpu.VMEM((span, lat), BF),
            pltpu.VMEM((lat, lat), BF),
            pltpu.VMEM((lat, lat), BF),
            *inner,
            pltpu.SemaphoreType.DMA((-(-span // PIECE),)),
            pltpu.SemaphoreType.DMA((2,)),
            *sems,
        ],
        input_output_aliases=alias,
        compiler_params=params(28),
        cost_estimate=cost(flops, span * lat * 4),
        name="embed",
    )(*args)


def embed_first(x, tail, src, weights, later):
    w_in, b_in, _, b_msg = weights
    rows, main = x.shape
    span = tail.shape[1]
    pts = main + span
    lat = w_in.shape[1]
    slots = src.shape[1]
    return embed_call(
        functools.partial(first_kernel, point=main),
        [*at_vmem(x, tail), src, *at_vmem(w_in, b_in, b_msg), *map(at_hbm, later)],
        [VM] * 6 + [ANY] * 2,
        (pltpu.HBM((pts, lat), BF), pltpu.HBM((span, lat), BF), pltpu.VMEM((rows, slots), BF)),
        [ANY, VM],
        span,
        span,
        lat,
        [pltpu.VMEM((pts, slots), BF)],
        [pltpu.SemaphoreType.DMA],
        {},
        2 * rows * pts * slots + 2 * span * lat * (rows + 2 * lat),
    )


def embed_second(x, counts, weights, later, latent, acts, low, up, tile):
    w_in, b_in, w_both, b_msg = weights
    rows, main = x.shape
    nodes, table = counts.shape
    lat = w_in.shape[1]
    return embed_call(
        functools.partial(second_kernel, tile=tile),
        [*at_vmem(low, up, w_both, w_in, b_in, b_msg), *map(at_hbm, (*later, counts, acts, x, latent))],
        [VM] * 6 + [ANY] * 6,
        (pltpu.HBM(latent.shape, BF), pltpu.VMEM((nodes, lat), F32)),
        [VM],
        main,
        table,
        lat,
        [pltpu.VMEM((nodes, table), BF), pltpu.VMEM((rows, main), BF)],
        [pltpu.SemaphoreType.DMA((3,))],
        {11: 0},
        2 * main * lat * (rows + 2 * lat) + 2 * nodes * table * lat,
    )


def node_kernel(r_ref, w_in, b_in, w_both, b_msg, sum_ref, *rest, pad):
    sources, o_ref, buffers, sem = rest[:5], rest[5], rest[6:11], rest[11]
    loads = [pltpu.make_async_copy(f, t, sem.at[k]) for k, (f, t) in enumerate(zip(sources, buffers))]
    for c in loads:
        c.start()
    w_mo, w_nb, pre_ref, w_no, mesh_ref = buffers
    nodes = sum_ref.shape[0]
    rows = r_ref[...]
    act = act_only(rows, (((1,), (0,)), ((), ())), w_in, b_in, w_both, b_msg)
    lane = lax.broadcasted_iota(jnp.int32, (8, rows.shape[1]), 1)
    pick = jnp.where(lane == pad, 16.0, jnp.where(lane == 2 * pad + 1, 1.0, 0.0)).astype(BF)
    dst = dot(pick, rows, NT)[:1].astype(jnp.int32) - 1
    ids = lax.broadcasted_iota(jnp.int32, (nodes, rows.shape[0]), 0)
    total = sum_ref[...] + dot(hot(ids, dst), act)
    high = total.astype(BF)
    low = (total - high.astype(F32)).astype(BF)
    loads[0].wait()
    summed = (dot(high, w_mo[...]) + dot(low, w_mo[...])).astype(BF)
    loads[1].wait()
    loads[2].wait()
    node = silu2(pre_ref[...] + dot(summed, w_nb[...]))
    loads[3].wait()
    loads[4].wait()
    o_ref[...] = (mesh_ref[...].astype(F32) + dot(node, w_no[...])).astype(BF)


def node_update(rows, weights, total, w_mo, mesh, pre, w_nb, w_no, pad):
    args = at_vmem(rows, *weights, total)
    later = [at_hbm(a) for a in (w_mo, w_nb, pre, w_no, mesh)]
    slots = rows.shape[0]
    lat = mesh.shape[1]
    return pl.pallas_call(
        functools.partial(node_kernel, pad=pad),
        in_specs=[VM] * len(args) + [ANY] * len(later),
        out_specs=VM,
        out_shape=jax.ShapeDtypeStruct(mesh.shape, BF),
        scratch_shapes=[pltpu.VMEM(a.shape, a.dtype) for a in later]
        + [pltpu.SemaphoreType.DMA((len(later),))],
        compiler_params=params(20),
        cost_estimate=cost(6 * slots * lat * lat, 6 * lat * lat * 2),
        name="node",
    )(*args, *later)


def shards(
    fields,
    chan_mean,
    chan_scale,
    w_embed_in,
    b_embed,
    w_embed_out,
    halo_index,
    local_src,
    local_dst,
    remote_src,
    remote_dst,
    w_msg_in,
    b_msg,
    w_msg_out,
    mesh_nodes,
    w_node_in,
    b_node,
    w_node_out,
):
    levels = lax.axis_size("lev")
    tiles = lax.axis_size("tile")
    chans, points = fields.shape
    pts = points // levels
    slot_count = remote_src.shape[2]
    halo = halo_index.shape[2]
    table = pts + 2 * halo
    wide = (chans + 1) * levels

    me = lax.axis_index("lev").astype(jnp.int32).reshape(1)
    sent = pack(me, chan_mean, chan_scale, fields, levels)
    got = lax.all_to_all(sent, "lev", split_axis=0, concat_axis=0, tiled=True)
    main = pts // (chans + 1) * chans
    x = got.reshape(wide, main)

    src = remote_src.reshape(1, -1)
    dst = remote_dst.reshape(1, -1)
    idx = halo_index.reshape(1, 2 * halo)
    first_src, src, dst, idx = lax.optimization_barrier((local_src, src, dst, idx))
    counts, w_in, pre, w_msg, w_both, b_in, b_out, w_nb = count_edges(
        first_src,
        local_dst,
        w_embed_in,
        b_embed[None, :],
        mesh_nodes,
        b_node[None, :],
        b_msg[None, :],
        w_node_in,
        w_embed_out,
        w_msg_in,
        table,
        wide,
        chans,
    )
    weights = [w_in, b_in, w_both, b_out]
    later = [w_embed_out, w_msg]

    low, high, tail = select(x, idx, chans)
    ahead = [(i, (i + 1) % tiles) for i in range(tiles)]
    back = [(t, s) for s, t in ahead]
    from_low = lax.ppermute(high, "tile", ahead)
    from_up = lax.ppermute(low, "tile", back)

    latent, acts, own = embed_first(x, tail, src, weights, later)

    rows = slots_rows(own, from_low, from_up, src, dst, pts, chans)
    rows = lax.all_to_all(
        rows.reshape(levels, slot_count, wide), "lev", split_axis=0, concat_axis=0, tiled=True
    ).reshape(levels * slot_count, wide)

    latent, total = embed_second(
        x, counts, weights, later, latent, acts, from_low, from_up, 2 * PIECE
    )
    mesh_out = node_update(
        rows, weights, total, w_msg_out, mesh_nodes, pre, w_nb, w_node_out, chans
    )
    return (latent, mesh_out)


def solution(mesh):
    return jax.shard_map(
        shards,
        mesh=mesh,
        in_specs=(
            P("lev", "tile"),
            P(),
            P(),
            P(),
            P(),
            P(),
            P(("tile", "lev"), None, None),
            P(("tile", "lev"), None),
            P(("tile", "lev"), None),
            P(("tile", "lev"), None, None),
            P(("tile", "lev"), None, None),
            P(),
            P(),
            P(),
            P(("tile", "lev"), None),
            P(),
            P(),
            P(),
        ),
        out_specs=(P(("tile", "lev"), None), P(("tile", "lev"), None)),
        check_vma=False,
    )
```
